256 devices in a mesh: samp: 8 (over z), row: 8 (over y, x_lo), col: 4 (over x_hi, core).
Axes of the slice: x: 4 (x_hi: 2, x_lo: 2; x = x_hi * 2 + x_lo), y: 4, z: 8, core: 2. Of those that a mesh axis runs over, the one named last changes fastest.
Arguments:
- tokens: bfloat16 [8, 1024, 768], P('samp', 'row'), may hold values from -6 to 6
- atom_type: int32 [1024], P('row'), may hold values from 0 to 31
- noise_step: int32 [8], P('samp'), may hold values from 0 to 199
- pair_rep: bfloat16 [1024, 1024, 128], P('row', 'col'), may hold values from -8 to 8
- bond_blocks: int32 [64, 2], replicated, may hold values from 0 to 31
- chiral_blocks: int32 [32, 2], replicated, may hold values from 0 to 31
- type_table: bfloat16 [32, 768], replicated, may hold values from -6 to 6
- noise_row: float32 [768], replicated, may hold values from -6 to 6
- norm_gain: float32 [768], replicated, may hold values from 0.5 to 1.5
- pair_gain: float32 [128], replicated, may hold values from 0.5 to 1.5
- in_weight: bfloat16 [4, 768, 768], P(None, 'col'), may hold values from -0.21875 to 0.21875
- out_weight: bfloat16 [768, 768], P('col'), may hold values from -0.21875 to 0.21875
- pair_weight: float32 [128, 16], replicated, may hold values from -16 to 16
- restraint_weight: float32 [2, 16], replicated, may hold values from -3 to 3
- cotangent: bfloat16 [8, 1024, 768], P('samp', 'row'), may hold values from -6 to 6
Outputs:
- updated: bfloat16 [8, 1024, 768], P('samp', 'row')
- token_grad: bfloat16 [8, 1024, 768], P('samp', 'row')
- pair_grad: bfloat16 [1024, 1024, 128], P('row', 'col', 'samp')
- in_grad: bfloat16 [4, 768, 768], P(None, 'col')
- out_grad: bfloat16 [768, 768], P('col')
- proj_grad: float32 [128, 16], replicated
The draws below stay inside these ranges and needn't reach their ends.
All inputs are finite; a program needn't handle non-finite values.
Results may differ from the reference program's by a relative error of at most 0.015.
Values may be sent and summed in bfloat16 or wider, within the bound.
A program may use at most 128 MiB of HBM per device.

```python
import math
import jax
import jax.numpy as jnp
import numpy as np
from jax import lax

D = 768
HEADS = 16
HEAD_DIM = 48
PAIR_CH = 128
TYPES = 32
BONDS = 64
CHIRAL = 32
BLOCK = 32
STEPS = 200
TOKENS = 1024
SAMPLES = 8


def draw_pair_rep(key, part):
    array_shape = (TOKENS, TOKENS, PAIR_CH)
    key_values = jax.random.fold_in(jax.random.fold_in(key, 11), 1)
    entries = jax.random.normal(key_values, array_shape, jnp.float32)
    return jnp.clip(entries, -8.0, 8.0).astype(jnp.bfloat16)


def draw_pair_weight(key, part):
    key_values = jax.random.fold_in(jax.random.fold_in(key, 23), 0)
    entries = jax.random.normal(key_values, (PAIR_CH, HEADS), jnp.float32) * PAIR_CH ** (-0.5)
    return jnp.clip(entries, -16.0, 16.0)


def set_ends(array, own_key, least, high):
    spot = [jax.random.randint(jax.random.fold_in(own_key, axis), (), 0, length) for axis, length in enumerate(array.shape)]
    main_axis = array.shape.index(max(array.shape))
    next_to = spot[:main_axis] + [(spot[main_axis] + 1) % array.shape[main_axis]] + spot[main_axis + 1:]
    return array.at[tuple(spot)].set(least).at[tuple(next_to)].set(high)


def block_scale(own_key, dims, shards, least, largest):
    def one(dim, shards_of):
        draws = jax.random.uniform(jax.random.fold_in(jax.random.fold_in(own_key, 6), dim), (shards_of,), jnp.float32, least / len(shards), largest / len(shards))
        return jnp.repeat(jnp.exp(draws), dims[dim] // shards_of).reshape((-1,) + (1,) * (len(dims) - dim - 1))

    factor_of = one(*shards[0])
    for cut in shards[1:]:
        factor_of = factor_of * one(*cut)
    return factor_of


def rank_table(count, skew):
    loads = [(1 << 20) // math.isqrt(rank ** skew) + 1 for rank in range(1, count + 1)]
    scale = 1 + sum(loads) // (1 << 30)
    return np.cumsum(np.array([max(1, weight // scale) for weight in loads]))


def ranked(key, shape, number_of, skew):
    listing = rank_table(number_of, skew)
    ticket = jax.random.randint(jax.random.fold_in(key, 1), shape, 0, int(listing[number_of - 1]))
    grade = jnp.searchsorted(jnp.asarray(listing, jnp.int32), ticket, side="right")
    return jax.random.permutation(jax.random.fold_in(key, 2), number_of)[grade].astype(jnp.int32)


def scatter_about(own_key, dims, scale, bound, shards=(), kind=jnp.bfloat16):
    values = jax.random.normal(own_key, dims, jnp.float32) * scale
    if len(shards) > 0:
        values = block_scale(own_key, dims, shards, -0.22, 0.18) * values
    return jnp.clip(values, min=-bound, max=bound).astype(kind)


def setup_inputs(seed: int = 0) -> dict:
    streams_of = jax.random.split(jax.random.key(seed), 16)
    return {
        "tokens": scatter_about(streams_of[0], (SAMPLES, TOKENS, D), 1.0, 6.0, ((0, 8), (1, 8))),
        "atom_type": set_ends(ranked(streams_of[1], (TOKENS,), TYPES, 2), jax.random.fold_in(streams_of[1], 3), 0, TYPES - 1).astype(jnp.int32),
        "noise_step": set_ends(jax.random.randint(streams_of[2], (SAMPLES,), 0, STEPS), jax.random.fold_in(streams_of[2], 1), 0, STEPS - 1).astype(jnp.int32),
        "pair_rep": draw_pair_rep(jax.random.fold_in(streams_of[15], 71), 0),
        "bond_blocks": set_ends(jax.random.randint(streams_of[4], (BONDS, 2), 0, TOKENS // BLOCK), jax.random.fold_in(streams_of[4], 1), 0, (TOKENS // BLOCK) - 1).astype(jnp.int32),
        "chiral_blocks": set_ends(jax.random.randint(streams_of[5], (CHIRAL, 2), 0, TOKENS // BLOCK), jax.random.fold_in(streams_of[5], 1), 0, (TOKENS // BLOCK) - 1).astype(jnp.int32),
        "type_table": scatter_about(streams_of[6], (TYPES, D), 1.0, 6.0),
        "noise_row": scatter_about(streams_of[7], (D,), 1.0, 6.0, (), jnp.float32),
        "norm_gain": jnp.clip(1.0 + 0.1 * jax.random.normal(streams_of[8], (D,), jnp.float32), 0.5, 1.5),
        "pair_gain": jnp.clip(1.0 + 0.1 * jax.random.normal(streams_of[9], (PAIR_CH,), jnp.float32), 0.5, 1.5),
        "in_weight": scatter_about(streams_of[10], (4, HEADS * HEAD_DIM, D), D ** -0.5, 0.21875, ((1, 4),)),
        "out_weight": scatter_about(streams_of[11], (HEADS * HEAD_DIM, D), (HEADS * HEAD_DIM) ** -0.5, 0.21875, ((0, 4),)),
        "pair_weight": draw_pair_weight(jax.random.fold_in(streams_of[15], 71), 0),
        "restraint_weight": jnp.clip(jax.random.uniform(streams_of[13], (2, HEADS), jnp.float32, -3.0, 3.0), -3.0, 3.0),
        "cotangent": scatter_about(streams_of[14], (SAMPLES, TOKENS, D), 1.0, 6.0, ((0, 8), (1, 8))),
    }


eps = 1e-05

def rounded(values):
    return lax.optimization_barrier(values.astype(jnp.bfloat16)).astype(jnp.float32)

def noise_level(noise_step):
    top_root = 160.0 ** (1.0 / 7.0)
    low_root = 0.0004 ** (1.0 / 7.0)
    root_base = top_root + noise_step.astype(jnp.float32) / (STEPS - 1) * (low_root - top_root)
    return 7.0 / 4.0 * jnp.log(root_base)

def normalize(values, scales):
    center = lax.optimization_barrier(jnp.mean(values, axis=-1, keepdims=True))
    centered = values - center
    inv_std = lax.rsqrt(lax.optimization_barrier(jnp.mean(centered * centered, axis=-1, keepdims=True)) + eps)
    unit_rows = centered * inv_std
    return (unit_rows, inv_std, unit_rows * scales)

def norm_back(upstream, unit_rows, inv_std, scales):
    scaled = upstream * scales
    return inv_std * (scaled - lax.optimization_barrier(jnp.mean(scaled, axis=-1, keepdims=True)) - unit_rows * lax.optimization_barrier(jnp.mean(scaled * unit_rows, axis=-1, keepdims=True)))

def restraint_map(blocks, row_first, row_total, col_first, col_total, block_total):
    first_hot = jax.nn.one_hot(blocks[:, 0], block_total, dtype=jnp.float32)
    second_hot = jax.nn.one_hot(blocks[:, 1], block_total, dtype=jnp.float32)
    counts = jnp.dot(first_hot.T, second_hot)
    row_hot = jax.nn.one_hot((row_first + jnp.arange(row_total)) // BLOCK, block_total, dtype=jnp.float32)
    col_hot = jax.nn.one_hot((col_first + jnp.arange(col_total)) // BLOCK, block_total, dtype=jnp.float32)
    return jnp.dot(jnp.dot(row_hot, counts), col_hot.T)

def sample_pass(base_one, cot_one, bias_full, norm_gain, in_weight, out_weight):
    highest = lax.Precision.HIGHEST
    unit_rows, inv_std, token_scaled = normalize(base_one, norm_gain)
    normed = token_scaled.astype(jnp.bfloat16)
    projected = jnp.einsum('nd,mkd->nmk', normed.astype(jnp.float32), in_weight.astype(jnp.float32), precision=highest)
    query_heads = rounded(projected[:, 0]).reshape(TOKENS, HEADS, HEAD_DIM)
    key_heads = rounded(projected[:, 1]).reshape(TOKENS, HEADS, HEAD_DIM)
    value_heads = rounded(projected[:, 2]).reshape(TOKENS, HEADS, HEAD_DIM)
    gate_value = jax.nn.sigmoid(projected[:, 3])
    score_scale = 1.0 / math.sqrt(HEAD_DIM)
    scores = jnp.einsum('qhd,khd->hqk', query_heads, key_heads) * score_scale + bias_full
    attn_probs = jax.nn.softmax(scores, axis=-1)
    attn_low = rounded(attn_probs)
    attended = jnp.einsum('hqk,khd->qhd', attn_low, value_heads).reshape(TOKENS, -1)
    mixed = (gate_value * attended).astype(jnp.bfloat16)
    updated_one = (base_one + jnp.dot(mixed, out_weight, preferred_element_type=jnp.float32)).astype(jnp.bfloat16)
    out_one = jnp.dot(mixed.T, cot_one, preferred_element_type=jnp.float32)
    grad_mixed = jnp.dot(cot_one, out_weight.T, preferred_element_type=jnp.float32)
    attend_heads = rounded(grad_mixed * gate_value).reshape(TOKENS, HEADS, HEAD_DIM)
    grad_gate = grad_mixed * attended * gate_value * (1.0 - gate_value)
    grad_probs = jnp.einsum('qhd,khd->hqk', attend_heads, value_heads)
    row_delta = lax.optimization_barrier(jnp.sum(attn_probs * grad_probs, axis=-1, keepdims=True))
    grad_scores = attn_probs * (grad_probs - row_delta)
    grad_low = rounded(grad_scores)
    grad_query = jnp.einsum('hqk,khd->qhd', grad_low, key_heads).reshape(TOKENS, -1) * score_scale
    grad_keys = jnp.einsum('hqk,qhd->khd', grad_low, query_heads).reshape(TOKENS, -1) * score_scale
    grad_values = jnp.einsum('hqk,qhd->khd', attn_low, attend_heads).reshape(TOKENS, -1)
    grads = jnp.stack([grad_query, grad_keys, grad_values, grad_gate], axis=1)
    in_one = jnp.einsum('nd,nmk->mkd', normed.astype(jnp.float32), grads, precision=highest)
    grad_normed = jnp.einsum('nmk,mkd->nd', grads, in_weight.astype(jnp.float32), precision=highest)
    token_one = (cot_one.astype(jnp.float32) + norm_back(grad_normed, unit_rows, inv_std, norm_gain)).astype(jnp.bfloat16)
    return (updated_one, token_one, grad_scores, in_one, out_one)

def reference(tokens, atom_type, noise_step, pair_rep, bond_blocks, chiral_blocks, type_table, noise_row, norm_gain, pair_gain, in_weight, out_weight, pair_weight, restraint_weight, cotangent):
    highest = lax.Precision.HIGHEST
    block_total = TOKENS // BLOCK
    unit_pair, pair_inv, pair_scaled = normalize(pair_rep.astype(jnp.float32), pair_gain)
    bond_map = restraint_map(bond_blocks, 0, TOKENS, 0, TOKENS, block_total)
    chiral_map = restraint_map(chiral_blocks, 0, TOKENS, 0, TOKENS, block_total)
    bias_full = jnp.einsum('ijc,ch->hij', pair_scaled, pair_weight, precision=highest)
    bias_full = bias_full + restraint_weight[0][:, None, None] * bond_map + restraint_weight[1][:, None, None] * chiral_map
    type_rows = jnp.dot(jax.nn.one_hot(atom_type, TYPES, dtype=jnp.bfloat16), type_table, preferred_element_type=jnp.float32)
    noise_levels = noise_level(noise_step)
    base_rows = tokens.astype(jnp.float32) + type_rows[None] + noise_levels[:, None, None] * noise_row

    def one_sample(carry, inputs):
        base_one, cot_one = inputs
        updated_one, token_one, bias_one, in_one, out_one = sample_pass(base_one, cot_one, bias_full, norm_gain, in_weight, out_weight)
        bias_acc, in_acc, out_acc = carry
        return ((bias_acc + bias_one, in_acc + in_one, out_acc + out_one), (updated_one, token_one))
    start_carry = (jnp.zeros((HEADS, TOKENS, TOKENS), jnp.float32), jnp.zeros(in_weight.shape, jnp.float32), jnp.zeros(out_weight.shape, jnp.float32))
    (bias_grad, in_grad, out_grad), (updated, token_grad) = lax.scan(one_sample, start_carry, (base_rows, cotangent))
    spread = jnp.einsum('hij,ch->ijc', bias_grad, pair_weight, precision=highest)
    pair_grad = norm_back(spread, unit_pair, pair_inv, pair_gain).astype(jnp.bfloat16)
    proj_grad = jnp.einsum('ijc,hij->ch', pair_scaled, bias_grad, precision=highest)
    return (updated, token_grad, pair_grad, in_grad.astype(jnp.bfloat16), out_grad.astype(jnp.bfloat16), proj_grad)
```

```python
import math

import jax
import jax.numpy as jnp
from jax import lax
from jax.experimental import pallas as pl
from jax.experimental.pallas import tpu as pltpu
from jax.sharding import Mesh
from jax.sharding import PartitionSpec as P

HEAD_DIM = 48
BLOCK = 32
STEPS = 200
COL = ("col_0", "col_1")
ROW = ("row_0", "row_1")
MESH = pl.DeviceIdType.MESH
F32, BF16 = jnp.float32, jnp.bfloat16
SCALE = 1.0 / math.sqrt(HEAD_DIM)
eps = 1e-05


def nn(a, b):
    return lax.dot_general(a, b, (((1,), (0,)), ((), ())), preferred_element_type=F32)


def nt(a, b):
    return lax.dot_general(a, b, (((1,), (1,)), ((), ())), preferred_element_type=F32)


def tn(a, b):
    return lax.dot_general(a, b, (((0,), (0,)), ((), ())), preferred_element_type=F32)


SCRATCH = dict(
    xbuf=((128, 256, 128), BF16),
    tokens=((128, 768), BF16),
    win=((768, 768), BF16),
    wout=((192, 768), BF16),
    base=((128, 768), F32),
    unit=((128, 768), F32),
    inv=((128, 1), F32),
    gate=((192, 128), F32),
    gmix=((192, 128), F32),
    waug=((80, 128), BF16),
    gh=((16, 1), F32),
    rst=((4, 16, 256), F32),
    amat=((2, 256, 256), BF16),
    emat=((256, 256), BF16),
    planes=((2, 2048, 128), F32),
    hat=((2048, 256), F32),
    invb=((2048, 256), F32),
    st=((128, 8, 256), F32),
    qg=((4, 2, 4, 48, 128), BF16),
    kvown=((2, 4, 48, 128), BF16),
    kv=((2, 4, 2, 4, 48, 128), BF16),
    nc=((8, 2, 128, 768), BF16),
    pr=((16, 128, 256), F32),
    dp=((16, 128, 256), F32),
    ot=((4, 4, 48, 128), BF16),
    oin=((4, 4, 48, 128), BF16),
    stats=((4, 48, 128), F32),
    acol=((128, 128), F32),
    arow=((4, 16, 128), F32),
    arow_own=((16, 128), F32),
    bgf=((2, 2048, 128), F32),
    bsp=((7, 2, 128, 128), BF16),
    bsm=((7, 2, 128, 128), BF16),
    brp=((7, 2, 128, 128), BF16),
    brm=((7, 2, 128, 128), BF16),
    bgt=((2, 256, 128), F32),
    bga=((8, 2, 256, 128), BF16),
    dqt=((4, 4, 48, 128), BF16),
    dqin=((4, 4, 48, 128), BF16),
    dkv=((2, 4, 2, 4, 48, 128), BF16),
    xin=((4, 2, 4, 48, 128), BF16),
    sx=((4, 2, 4, 48, 128), BF16),
    y1in=((4, 2, 4, 48, 128), BF16),
    y3in=((4, 2, 4, 48, 128), BF16),
    y2in=((4, 2, 4, 48, 128), BF16),
    fin=((4, 2, 4, 48, 128), BF16),
    dkvown=((2, 4, 48, 128), BF16),
    att=((192, 128), F32),
    gin=((768, 128), BF16),
    gout=((256, 128), BF16),
    zin=((8, 96, 128), BF16),
    zout=((8, 32, 128), BF16),
    po=((4, 32, 768), BF16),
    por=((4, 32, 768), BF16),
    upd=((4, 32, 768), BF16),
    gn=((4, 32, 768), BF16),
    gnr=((4, 32, 768), BF16),
    tok=((4, 32, 768), BF16),
    dws=((8, 16, 768), BF16),
    dwr=((8, 16, 768), BF16),
    dwall=((4, 2, 8, 16, 768), BF16),
    pjz=((8, 16, 128), F32),
    pjr=((8, 16, 128), F32),
    pjc=((4, 16, 128), F32),
    pj1=((16, 128), F32),
    pj2=((16, 128), F32),
)
SEMS = dict(
    s_pair=8,
    s_in=4,
    s_send=220,
    s_qgx=1,
    s_qgc=2,
    s_kvg=4,
    s_yb=4,
    s_xb=4,
    s_ncp=5,
    s_ncm=4,
    s_ncc=8,
    s_st=4,
    s_o=4,
    s_dq=4,
    s_xin=4,
    s_y2=4,
    s_y1=4,
    s_y3=4,
    s_fin=4,
    s_brp=7,
    s_brm=7,
    s_bgp=5,
    s_bgm=5,
    s_po=4,
    s_upd=4,
    s_gn=4,
    s_tok=4,
    s_zi=8,
    s_zo=8,
    s_dw=8,
    s_dz=8,
    s_ax=1,
    s_ay=4,
    s_by=4,
    s_bx=4,
    s_pz=8,
    s_pr=8,
    s_pc=4,
)
INPUTS = (
    "h_tokens", "h_cot", "h_win", "h_wout", "pair",
    "atom", "step", "bonds", "chirs", "table", "nrow", "gain", "pgain", "pw", "rw",
)
OUTPUTS = ("o_upd", "o_tok", "o_pg", "o_in", "o_out", "o_proj")


def kernel(*refs):
    names = INPUTS + OUTPUTS + tuple(SCRATCH) + tuple(SEMS)
    r = dict(zip(names, refs, strict=True))

    class R:
        pass

    k = R()
    k.__dict__.update(r)
    z = lax.axis_index("samp")
    y = lax.axis_index("row_0")
    xl = lax.axis_index("row_1")
    xh = lax.axis_index("col_0")
    co = lax.axis_index("col_1")
    c = 2 * xh + co
    row = 2 * y + xl
    zof = [lax.rem(z + n, 8) for n in range(8)]
    zback = [lax.rem(z + 8 - n, 8) for n in range(8)]
    yof = [lax.rem(y + n, 4) for n in range(4)]
    dy = lax.rem(y + 4 - c, 4)
    x_other = {"row_1": 1 - xl}
    y_up = {"row_0": yof[1]}
    y_down = {"row_0": yof[3]}
    z_up = {"samp": zof[1]}
    z_down = {"samp": zof[7]}
    core_other = {"col_1": 1 - co}
    xh_other = {"col_0": 1 - xh}
    c_core = 2 * xh + (1 - co)
    c_xh = 2 * (1 - xh) + co
    cpeers = []
    for n in range(1, 4):
        ph, pc = lax.rem(xh + n // 2, 2), lax.rem(co + n % 2, 2)
        cpeers.append((n, {"col_0": ph, "col_1": pc}, 2 * ph + pc))
    rpeers = []
    for n in range(1, 8):
        py, px = lax.rem(y + n // 2, 4), lax.rem(xl + n % 2, 2)
        fy, fx = lax.rem(y + 4 - n // 2, 4), lax.rem(xl + n % 2, 2)
        rpeers.append((n, {"row_0": py, "row_1": px}, 2 * py + px, 2 * fy + fx))

    loads = [
        pltpu.make_async_copy(k.h_tokens, k.tokens, k.s_in.at[0]),
        pltpu.make_async_copy(k.h_win, k.win, k.s_in.at[1]),
        pltpu.make_async_copy(k.h_cot, k.nc.at[z, 1], k.s_in.at[2]),
        pltpu.make_async_copy(k.h_wout, k.wout, k.s_in.at[3]),
    ]
    for copy in loads:
        copy.start()
    pair_copies = []
    for n in range(8):
        part = pl.ds(16 * n, 16)
        copy = pltpu.make_async_copy(k.pair.at[part], k.xbuf.at[part], k.s_pair.at[n])
        copy.start()
        pair_copies.append(copy)

    barrier = pltpu.get_barrier_semaphore()
    for n in range(1, 8):
        pl.semaphore_signal(barrier, inc=1, device_id={"samp": zof[n]}, device_id_type=MESH)
    for _, dev, _, _ in rpeers:
        pl.semaphore_signal(barrier, inc=1, device_id=dev, device_id_type=MESH)
    for _, dev, _ in cpeers:
        pl.semaphore_signal(barrier, inc=1, device_id=dev, device_id_type=MESH)

    types = lax.broadcasted_iota(jnp.int32, (32, 128), 0) == k.atom[...]
    top_root = 160.0 ** (1.0 / 7.0)
    low_root = 0.0004 ** (1.0 / 7.0)
    root = top_root + k.step[...].astype(F32) / (STEPS - 1) * (low_root - top_root)
    level = 7.0 / 4.0 * jnp.log(root)
    add = tn(types.astype(F32).astype(BF16), k.table[...]) + level * k.nrow[...]
    loads[0].wait()
    base = k.tokens[...].astype(F32) + add
    k.base[...] = base
    centered = base - jnp.mean(base, axis=1, keepdims=True)
    inv = lax.rsqrt(jnp.mean(centered * centered, axis=1, keepdims=True) + eps)
    unit = centered * inv
    k.inv[...] = inv
    k.unit[...] = unit
    normed = (unit * k.gain[...]).astype(BF16)
    k.nc[z, 0] = normed
    loads[1].wait()
    proj_kv = nt(k.win[192:576], normed)
    for m in range(2):
        for hh in range(4):
            at = 192 * m + 48 * hh
            k.kvown[m, hh] = proj_kv[at : at + 48].astype(BF16)
    pl.semaphore_wait(barrier, 17)

    started = []
    count = [0]

    def make(src, dst, sem, dev):
        d = pltpu.make_async_remote_copy(
            src_ref=src,
            dst_ref=dst,
            send_sem=k.s_send.at[count[0]],
            recv_sem=sem,
            device_id=dev,
            device_id_type=MESH,
        )
        count[0] += 1
        return d

    def send(src, dst, sem, dev):
        d = make(src, dst, sem, dev)
        d.start()
        started.append((None, d))

    def arrived(dst, sem):
        pltpu.make_async_remote_copy(
            src_ref=dst,
            dst_ref=dst,
            send_sem=k.s_send.at[0],
            recv_sem=sem,
            device_id=z_up,
            device_id_type=MESH,
        ).wait_recv()

    def when(cond, body):
        pl.when(cond)(body)

    gather_kv = make(
        k.kvown,
        k.kv.at[xl, c],
        k.s_kvg.at[2 * lax.rem(xh + y // 2, 2) + lax.rem(co + y % 2, 2)],
        {"col_0": y // 2, "col_1": y % 2},
    )
    started.append((dy != 0, gather_kv))
    when(dy != 0, lambda: gather_kv.start())
    groups = (c, c_core, c_xh, 2 * (1 - xh) + 1 - co)
    to_x = [make(k.kv.at[xl, g], k.kv.at[xl, g], k.s_xb.at[n], x_other) for n, g in enumerate(groups)]
    to_up = [make(k.kv.at[xl, g], k.kv.at[xl, g], k.s_yb.at[n], y_up) for n, g in enumerate(groups)]
    to_down = [make(k.kv.at[xl, g], k.kv.at[xl, g], k.s_yb.at[n], y_down) for n, g in enumerate(groups)]
    started += [(None, d) for d in to_x]
    started += [(dy == 0, d) for d in to_up + to_down]
    started += [(dy == 1, to_up[0]), (dy == 1, to_up[2]), (dy == 3, to_down[1]), (dy == 3, to_down[3])]

    def kv_step(n):
        def source():
            if n == 0:
                k.kv[xl, c] = k.kvown[...]
            else:
                arrived(k.kv.at[xl, groups[n]], k.s_kvg.at[n])
            to_up[n].start()
            to_down[n].start()
            to_x[n].start()

        def relay(near):
            arrived(k.kv.at[xl, groups[n]], k.s_yb.at[n])
            if near is not None:
                near[n].start()
            to_x[n].start()

        when(dy == 0, source)
        when(dy == 1, lambda: relay(to_up if n % 2 == 0 else None))
        when(dy == 3, lambda: relay(to_down if n % 2 == 1 else None))
        when(dy == 2, lambda: relay(None))

    def kv_first():
        k.kv[xl, c] = k.kvown[...]
        to_up[0].start()
        to_down[0].start()
        to_x[0].start()

    when(dy == 0, kv_first)
    loads[3].wait()
    loads[2].wait()
    proj_q = nt(k.win[0:192], normed)
    gate = jax.nn.sigmoid(nt(k.win[576:768], normed))
    gmix = nt(k.wout[...], k.nc[z, 1])
    k.gate[...] = gate
    k.gmix[...] = gmix
    grad_attend = gmix * gate
    for hh in range(4):
        k.qg[c, 0, hh] = proj_q[48 * hh : 48 * hh + 48].astype(BF16)
        k.qg[c, 1, hh] = grad_attend[48 * hh : 48 * hh + 48].astype(BF16)
    send(k.qg.at[c], k.qg.at[c], k.s_qgx.at[0], xh_other)
    send(k.qg.at[c], k.qg.at[c], k.s_qgc.at[0], core_other)
    half = pl.ds(64 * co, 64)
    send(k.nc.at[z, :, half], k.nc.at[z, :, half], k.s_ncp.at[1], z_up)
    send(k.nc.at[z, :, half], k.nc.at[z, :, half], k.s_ncm.at[1], z_down)

    weights = k.pw[...] * k.pgain[...]
    w_hi = weights.astype(BF16)
    rest = weights - w_hi.astype(F32)
    w_mid = rest.astype(BF16)
    w_lo = (rest - w_mid.astype(F32)).astype(BF16)
    sub16 = lax.broadcasted_iota(jnp.int32, (16, 128), 0)
    lane16 = lax.broadcasted_iota(jnp.int32, (16, 128), 1)
    pick = (lane16 == 16 * z + sub16).astype(F32).astype(BF16)
    k.waug[0:16] = w_hi
    k.waug[16:32] = w_mid
    k.waug[32:48] = w_lo
    k.waug[48:64] = pick
    k.waug[64:80] = jnp.ones((16, 128), BF16)
    k.gh[...] = jnp.sum(weights, axis=1, keepdims=True)
    spread = weights - jnp.mean(weights, axis=1, keepdims=True)
    s_hi = spread.astype(BF16)
    s_lo = (spread - s_hi.astype(F32)).astype(BF16)
    sub256 = lax.broadcasted_iota(jnp.int32, (256, 256), 0)
    lane256 = lax.broadcasted_iota(jnp.int32, (256, 256), 1)
    same = (sub256 // 16) == (lane256 // 16)
    tall = (
        lax.broadcasted_iota(jnp.int32, (256, 16), 0) % 16 == lax.broadcasted_iota(jnp.int32, (256, 16), 1)
    ).astype(F32).astype(BF16)
    for n, part in enumerate((s_hi, s_lo)):
        small = nt(pick, part).astype(BF16)
        wide = nt(nn(tall, small).astype(BF16), tall)
        k.amat[n] = jnp.where(same, wide, 0.0).astype(BF16)
    k.emat[...] = jnp.where(same, 1.0 / 128.0, 0.0).astype(BF16)
    eye = lax.broadcasted_iota(jnp.int32, (16, 16), 0) == lax.broadcasted_iota(jnp.int32, (16, 16), 1)

    def block_counts(ref, total):
        first = (lax.broadcasted_iota(jnp.int32, (16, total), 0) + 4 * row) == ref[0:1]
        second = lax.broadcasted_iota(jnp.int32, (256, total), 0) // BLOCK + 8 * c == ref[1:2]
        return nt(first.astype(F32).astype(BF16), second.astype(F32).astype(BF16))

    bond = block_counts(k.bonds, 64)
    chir = block_counts(k.chirs, 32)
    w_bond = jnp.sum(jnp.where(eye, k.rw[0:1], 0.0), axis=1, keepdims=True)
    w_chir = jnp.sum(jnp.where(eye, k.rw[1:2], 0.0), axis=1, keepdims=True)
    for n in range(4):
        k.rst[n] = w_bond * bond[n : n + 1] + w_chir * chir[n : n + 1]

    ones = jnp.ones((8, 128), BF16)

    def pair_rows(n):
        pair_copies[n].wait()

        def body(i, carry):
            x = k.xbuf[i]
            res = nt(k.waug[...], x)
            xf = x.astype(F32)
            sq = xf * xf
            hi = sq.astype(BF16)
            lo = (sq - hi.astype(F32)).astype(BF16)
            ss = nt(ones, hi) + nt(ones, lo)
            mean = res[64:65] * (1.0 / 128.0)
            var = ss[0:1] * (1.0 / 128.0) - mean * mean
            inv = lax.rsqrt(jnp.maximum(var, 0.0) + eps)
            bias = res[0:16] + res[16:32] + res[32:48]
            bias = inv * (bias - mean * k.gh[...])
            rows = pl.ds(pl.multiple_of(i * 16, 16), 16)
            k.planes[0, rows, :] = bias[:, :128]
            k.planes[1, rows, :] = bias[:, 128:]
            k.hat[rows, :] = (res[48:64] - mean) * (inv * inv)
            k.invb[rows, :] = jnp.broadcast_to(inv, (16, 256))
            k.st[i, 0:1] = inv
            k.st[i, 1:2] = mean * inv
            return carry

        lax.fori_loop(16 * n, 16 * n + 16, body, 0, unroll=4)

    def nc_relay(n):
        src = k.nc.at[zback[n], :, half]
        arrived(src, k.s_ncp.at[n])
        if n < 4:
            send(src, src, k.s_ncp.at[n + 1], z_up)
        send(src, src, k.s_ncc.at[n], core_other)
        if n < 4:
            src = k.nc.at[zof[n], :, half]
            arrived(src, k.s_ncm.at[n])
            if n < 3:
                send(src, src, k.s_ncm.at[n + 1], z_down)
            send(src, src, k.s_ncc.at[8 - n], core_other)

    pair_rows(0)
    when(dy != 0, lambda: kv_step(0))
    pair_rows(1)
    kv_step(1)
    pair_rows(2)
    arrived(k.qg.at[c_xh], k.s_qgx.at[0])
    send(k.qg.at[c_xh], k.qg.at[c_xh], k.s_qgc.at[1], core_other)
    kv_step(2)
    pair_rows(3)
    kv_step(3)
    pair_rows(4)
    nc_relay(1)
    pair_rows(5)
    pair_rows(6)
    pair_rows(7)
    nc_relay(2)
    for n, g in enumerate(groups):
        arrived(k.kv.at[1 - xl, g], k.s_xb.at[n])
    arrived(k.qg.at[c_core], k.s_qgc.at[0])
    arrived(k.qg.at[2 * (1 - xh) + 1 - co], k.s_qgc.at[1])

    lane = lax.broadcasted_iota(jnp.int32, (128, 128), 1)

    def head_kv(g, m, hh):
        return jnp.concatenate([k.kv[0, g, m, hh], k.kv[1, g, m, hh]], axis=1)

    def forward(h, packed):
        g, hh = h // 4, h % 4
        keys = head_kv(g, 0, hh)
        vals = head_kv(g, 1, hh)
        by_head = pl.ds(h, 128, stride=16)
        bias = jnp.concatenate([k.planes[0, by_head, :], k.planes[1, by_head, :]], axis=1)
        extra = [jnp.broadcast_to(k.rst[n, pl.ds(h, 1), :], (32, 256)) for n in range(4)]
        s = tn(k.qg[g, 0, hh], keys) * SCALE + (bias + jnp.concatenate(extra, axis=0))
        top = jnp.max(s, axis=1, keepdims=True)
        p = jnp.exp(s - top)
        dp = tn(k.qg[g, 1, hh], vals)
        k.pr[h] = p
        k.dp[h] = dp
        k.ot[g, hh] = nt(vals, p.astype(BF16)).astype(BF16)
        total = jnp.sum(p, axis=1, keepdims=True)
        dots = jnp.sum(p * dp, axis=1, keepdims=True)
        packed = jnp.where(lane == h, top, packed)
        packed = jnp.where(lane == 16 + h, total, packed)
        return jnp.where(lane == 32 + h, dots, packed)

    packed = lax.fori_loop(0, 16, forward, jnp.zeros((128, 128), F32), unroll=2)
    k.stats[c] = packed.T[0:48]
    for n, dev, _ in cpeers:
        send(k.stats.at[c], k.stats.at[c], k.s_st.at[n], dev)
    for n, dev, who in cpeers:
        send(k.ot.at[who], k.oin.at[c], k.s_o.at[n], dev)
    k.oin[c] = k.ot[c]
    nc_relay(3)
    for n, _, who in cpeers:
        arrived(k.stats.at[who], k.s_st.at[n])
    top = k.stats[0, 0:16]
    for n in range(1, 4):
        top = jnp.maximum(top, k.stats[n, 0:16])
    total = jnp.zeros((16, 128), F32)
    dots = jnp.zeros((16, 128), F32)
    for n in range(4):
        w = jnp.exp(k.stats[n, 0:16] - top)
        k.arow[n] = w
        total += w * k.stats[n, 16:32]
        dots += w * k.stats[n, 32:48]
    inv_total = 1.0 / total
    for n in range(4):
        k.arow[n] = k.arow[n] * inv_total
    own = k.arow[c]
    k.arow_own[...] = own
    k.acol[...] = jnp.concatenate([own, dots * inv_total, jnp.zeros((96, 128), F32)], axis=0).T

    def backward(h, carry):
        g, hh = h // 4, h % 4
        columns = k.acol[...]
        alpha = jnp.sum(jnp.where(lane == h, columns, 0.0), axis=1, keepdims=True)
        delta = jnp.sum(jnp.where(lane == 16 + h, columns, 0.0), axis=1, keepdims=True)
        p = k.pr[h]
        ds = p * alpha * (k.dp[h] - delta)
        by_head = pl.ds(h, 128, stride=16)
        k.bgf[0, by_head, :] = ds[:, :128]
        k.bgf[1, by_head, :] = ds[:, 128:]
        low = ds.astype(BF16)
        k.dqt[g, hh] = (nt(head_kv(g, 0, hh), low) * SCALE).astype(BF16)
        dk = (nn(k.qg[g, 0, hh], low) * SCALE).astype(BF16)
        k.dkv[0, g, 0, hh] = dk[:, :128]
        k.dkv[1, g, 0, hh] = dk[:, 128:]
        ga = (k.qg[g, 1, hh].astype(F32) * k.arow_own[pl.ds(h, 1), :]).astype(BF16)
        dv = nn(ga, p.astype(BF16)).astype(BF16)
        k.dkv[0, g, 1, hh] = dv[:, :128]
        k.dkv[1, g, 1, hh] = dv[:, 128:]
        return carry

    for n in range(4):
        lax.fori_loop(4 * n, 4 * n + 4, backward, 0, unroll=2)
        send(k.dkv.at[1 - xl, n], k.xin.at[n], k.s_xin.at[n], x_other)

    def ring_step(n):
        for back, stage, come, sem, dev, first in (
            (zback, k.bsp, k.brp, k.s_brp, z_up, 0),
            (zof, k.bsm, k.brm, k.s_brm, z_down, 128),
        ):
            owner = back[1 + n]
            part = pl.ds(pl.multiple_of(owner * 256 + first, 128), 128)
            value = k.bgf[:, part, :]
            if n > 0:
                arrived(come.at[n - 1], sem.at[n - 1])
                value = value + come[n - 1].astype(F32)
            stage[n] = value.astype(BF16)
            send(stage.at[n], come.at[n], sem.at[n], dev)

    ring_step(0)
    for n, dev, who in cpeers:
        send(k.dqt.at[who], k.dqin.at[c], k.s_dq.at[n], dev)
    k.dqin[c] = k.dqt[c]

    for n, _, who in cpeers:
        arrived(k.oin.at[who], k.s_o.at[n])
    for hh in range(4):
        att = jnp.zeros((48, 128), F32)
        for n in range(4):
            w = k.arow[n, pl.ds(4 * c + hh, 1), :]
            att += k.oin[n, hh].astype(F32) * w
        k.att[48 * hh : 48 * hh + 48] = att
    gate = k.gate[...]
    att = k.att[...]
    mixed = (gate * att).astype(BF16)
    k.gout[0:192] = mixed
    k.gout[192:256] = jnp.zeros((64, 128), BF16)
    k.gin[576:768] = (k.gmix[...] * att * gate * (1.0 - gate)).astype(BF16)
    part_out = tn(mixed, k.wout[...]).astype(BF16)
    for n in range(4):
        k.po[n] = part_out[32 * n : 32 * n + 32]
    for n, dev, who in cpeers:
        send(k.po.at[who], k.por.at[c], k.s_po.at[n], dev)
    k.por[c] = k.po[c]
    for n in range(1, 8):
        send(
            k.gout.at[pl.ds(pl.multiple_of(zof[n] * 32, 32), 32)],
            k.zout.at[z],
            k.s_zo.at[n],
            {"samp": zof[n]},
        )
    k.zout[z] = k.gout[pl.ds(pl.multiple_of(z * 32, 32), 32)]

    ring_step(1)

    def plus(dst, piece, a, b):
        dst[piece] = (a.astype(F32) + b.astype(F32)).astype(BF16)

    r2 = [
        make(k.sx.at[n], k.y2in.at[n], k.s_y2.at[n], y_down if n % 2 == 0 else y_up)
        for n in range(4)
    ]
    r1 = [make(k.sx.at[n], k.y1in.at[n], k.s_y1.at[n], y_down) for n in range(4)]
    r3 = [make(k.sx.at[n], k.y3in.at[n], k.s_y3.at[n], y_up) for n in range(4)]
    started += [(dy == 2, d) for d in r2] + [(dy == 1, d) for d in r1] + [(dy == 3, d) for d in r3]
    spread_kv = {}
    for n, dev, who in cpeers:
        spread_kv[n] = make(k.fin.at[who], k.dkvown, k.s_fin.at[n], dev)
        started.append((dy == 0, spread_kv[n]))

    def first_sum(n):
        arrived(k.xin.at[n], k.s_xin.at[n])
        plus(k.sx, n, k.dkv[xl, n], k.xin[n])
        when(dy == 2, lambda: r2[n].start())
        when(dy == 1 if n % 2 == 1 else dy == 3, lambda: (r1 if n % 2 == 1 else r3)[n].start())

    def second_sum(n):
        def body():
            arrived(k.y2in.at[n], k.s_y2.at[n])
            plus(k.sx, n, k.sx[n], k.y2in[n])
            (r1 if n % 2 == 0 else r3)[n].start()

        when(dy == 1 if n % 2 == 0 else dy == 3, body)

    def last_sum(n):
        def body():
            arrived(k.y1in.at[n], k.s_y1.at[n])
            arrived(k.y3in.at[n], k.s_y3.at[n])
            total = k.sx[n].astype(F32) + k.y1in[n].astype(F32) + k.y3in[n].astype(F32)
            k.fin[n] = total.astype(BF16)

        when(dy == 0, body)

    first_sum(0)
    first_sum(1)
    ring_step(2)
    first_sum(2)
    second_sum(0)
    second_sum(1)
    first_sum(3)
    ring_step(3)

    for n, _, who in cpeers:
        arrived(k.por.at[who], k.s_po.at[n])
    mine = pl.ds(pl.multiple_of(32 * c, 32), 32)
    total = k.base[mine]
    for n in range(4):
        total = total + k.por[n].astype(F32)
    k.upd[c] = total.astype(BF16)
    for n, dev, _ in cpeers:
        send(k.upd.at[c], k.upd.at[c], k.s_upd.at[n], dev)
    second_sum(2)
    second_sum(3)
    nc_relay(4)
    ring_step(4)
    for n in range(4):
        last_sum(n)

    def spread_out():
        for d in spread_kv.values():
            d.start()
        k.dkvown[...] = k.fin[c]

    when(dy == 0, spread_out)
    ring_step(5)
    when(
        dy != 0,
        lambda: arrived(k.dkvown, k.s_fin.at[2 * lax.rem(xh + y // 2, 2) + lax.rem(co + y % 2, 2)]),
    )

    for n, _, who in cpeers:
        arrived(k.dqin.at[who], k.s_dq.at[n])
    for hh in range(4):
        dq = k.dqin[0, hh].astype(F32)
        for n in range(1, 4):
            dq += k.dqin[n, hh].astype(F32)
        k.gin[48 * hh : 48 * hh + 48] = dq.astype(BF16)
        k.gin[192 + 48 * hh : 240 + 48 * hh] = k.dkvown[0, hh]
        k.gin[384 + 48 * hh : 432 + 48 * hh] = k.dkvown[1, hh]
    for n in range(1, 8):
        send(
            k.gin.at[pl.ds(pl.multiple_of(zof[n] * 96, 96), 96)],
            k.zin.at[z],
            k.s_zi.at[n],
            {"samp": zof[n]},
        )
    k.zin[z] = k.gin[pl.ds(pl.multiple_of(z * 96, 96), 96)]
    part_normed = tn(k.gin[...], k.win[...]).astype(BF16)
    for n in range(4):
        k.gn[n] = part_normed[32 * n : 32 * n + 32]
    for n, dev, who in cpeers:
        send(k.gn.at[who], k.gnr.at[c], k.s_gn.at[n], dev)
    k.gnr[c] = k.gn[c]

    ring_step(6)
    for first, come, sem in ((0, k.brp, k.s_brp), (128, k.brm, k.s_brm)):
        arrived(come.at[6], sem.at[6])
        part = pl.ds(pl.multiple_of(z * 256 + first, 128), 128)
        k.bgt[:, first : first + 128] = k.bgf[:, part, :] + come[6].astype(F32)
    k.bga[z] = k.bgt[...].astype(BF16)
    send(k.bga.at[z], k.bga.at[z], k.s_bgp.at[1], z_up)
    send(k.bga.at[z], k.bga.at[z], k.s_bgm.at[1], z_down)

    def bg_relay(n):
        if n < 4:
            below, above = k.bga.at[zback[n]], k.bga.at[zof[n]]
            arrived(below, k.s_bgp.at[n])
            if n == 3:
                below, above = below.at[:, 0:128], above.at[:, 128:256]
            send(below, below, k.s_bgp.at[n + 1], z_up)
            arrived(k.bga.at[zof[n]], k.s_bgm.at[n])
            send(above, above, k.s_bgm.at[n + 1], z_down)
        else:
            arrived(k.bga.at[zof[4], :, 0:128], k.s_bgp.at[4])
            arrived(k.bga.at[zof[4], :, 128:256], k.s_bgm.at[4])

    def pair_back(owner):
        bg = jnp.concatenate([k.bga[owner, 0], k.bga[owner, 1]], axis=1)
        rows = pl.ds(pl.multiple_of(owner * 256, 256), 256)
        plane = jnp.concatenate([k.planes[0, rows, :], k.planes[1, rows, :]], axis=1)
        product = bg.astype(F32) * plane
        hi = product.astype(BF16)
        lo = (product - hi.astype(F32)).astype(BF16)
        both = nn(k.emat[...], hi) + nn(k.emat[...], lo)
        out = nn(k.amat[0], bg) + nn(k.amat[1], bg)
        k.o_pg[rows, :] = (k.invb[rows, :] * out - k.hat[rows, :] * both).astype(BF16)

    def project_pairs(n, carry):
        acc, low = carry
        part = pl.ds(pl.multiple_of(n * 16, 16), 16)
        bg = jnp.concatenate([k.bgt[0, part, :], k.bgt[1, part, :]], axis=1)
        i = 16 * z + n
        scaled = bg * k.st[i, 0:1]
        hi = scaled.astype(BF16)
        rest = (scaled - hi.astype(F32)).astype(BF16)
        acc = acc + nn(jnp.concatenate([hi, rest], axis=0), k.xbuf[i])
        low = low + jnp.sum(bg * k.st[i, 1:2], axis=1, keepdims=True)
        return (acc, low)

    acc, low = lax.fori_loop(
        0, 16, project_pairs, (jnp.zeros((32, 128), F32), jnp.zeros((16, 1), F32)), unroll=2
    )
    k.pj1[...] = k.pgain[...] * (acc[0:16] + acc[16:32] - low)
    for n in range(1, 8):
        send(k.pj1, k.pjz.at[z], k.s_pz.at[n], {"samp": zof[n]})
    k.pjz[z] = k.pj1[...]

    for n, _, who in cpeers:
        arrived(k.gnr.at[who], k.s_gn.at[n])
    total = k.gnr[0].astype(F32)
    for n in range(1, 4):
        total += k.gnr[n].astype(F32)
    scaled = total * k.gain[...]
    hat = k.unit[mine]
    back = k.inv[mine] * (
        scaled
        - jnp.mean(scaled, axis=1, keepdims=True)
        - hat * jnp.mean(scaled * hat, axis=1, keepdims=True)
    )
    k.tok[c] = (k.nc[z, 1, mine].astype(F32) + back).astype(BF16)
    for n, dev, _ in cpeers:
        send(k.tok.at[c], k.tok.at[c], k.s_tok.at[n], dev)

    for n in range(1, 8):
        arrived(k.nc.at[zback[n], :, pl.ds(64 * (1 - co), 64)], k.s_ncc.at[n])
    for n in range(1, 8):
        arrived(k.zin.at[zback[n]], k.s_zi.at[n])
        arrived(k.zout.at[zback[n]], k.s_zo.at[n])
    acc = nn(k.zin[0], k.nc[0, 0])
    acc_out = nn(k.zout[0], k.nc[0, 1])
    for n in range(1, 8):
        acc += nn(k.zin[n], k.nc[n, 0])
        acc_out += nn(k.zout[n], k.nc[n, 1])
    for n in range(6):
        k.dws[n] = acc[16 * n : 16 * n + 16].astype(BF16)
    for n in range(2):
        k.dws[6 + n] = acc_out[16 * n : 16 * n + 16].astype(BF16)
    for n, dev, to, _ in rpeers:
        send(k.dws.at[to], k.dwr.at[row], k.s_dw.at[n], dev)
    k.dwr[row] = k.dws[row]
    bg_relay(1)
    for n in range(1, 8):
        arrived(k.pjz.at[zback[n]], k.s_pz.at[n])
    total = k.pjz[0]
    for n in range(1, 8):
        total += k.pjz[n]
    k.pj2[...] = total
    for n, dev, _, _ in rpeers:
        send(k.pj2, k.pjr.at[row], k.s_pr.at[n], dev)
    k.pjr[row] = total

    for n, _, _, came in rpeers:
        arrived(k.dwr.at[came], k.s_dw.at[n])
    total = k.dwr[0].astype(F32)
    for n in range(1, 8):
        total += k.dwr[n].astype(F32)
    k.dwall[y, xl, z] = total.astype(BF16)
    for n in range(1, 8):
        here = k.dwall.at[y, xl, z]
        send(here, here, k.s_dz.at[n], {"samp": zof[n]})
    pair_back(z)
    bg_relay(2)
    for n, _, _, came in rpeers:
        arrived(k.pjr.at[came], k.s_pr.at[n])
    total = k.pjr[0]
    for n in range(1, 8):
        total += k.pjr[n]
    k.pjc[c] = total
    for n, dev, _ in cpeers:
        send(k.pjc.at[c], k.pjc.at[c], k.s_pc.at[n], dev)
    pair_back(zof[1])
    pair_back(zback[1])

    def same_place(ref, sem, dev):
        send(ref, ref, sem, dev)

    low_z, high_z = pl.ds(0, 4), pl.ds(4, 4)
    for n in range(1, 8):
        arrived(k.dwall.at[y, xl, zback[n]], k.s_dz.at[n])
    same_place(k.dwall.at[y, xl, low_z], k.s_ax.at[0], x_other)
    same_place(k.dwall.at[y, xl, high_z], k.s_by.at[0], y_up)
    same_place(k.dwall.at[y, xl, high_z], k.s_by.at[1], y_down)
    same_place(k.dwall.at[y, xl, high_z], k.s_bx.at[0], x_other)
    bg_relay(3)
    arrived(k.dwall.at[y, 1 - xl, low_z], k.s_ax.at[0])
    same_place(k.dwall.at[y, :, low_z], k.s_ay.at[0], y_up)
    same_place(k.dwall.at[y, :, low_z], k.s_ay.at[1], y_down)
    pair_back(zof[2])
    y1, y2, y3 = yof[1], yof[2], yof[3]
    arrived(k.dwall.at[y3, xl, high_z], k.s_by.at[0])
    same_place(k.dwall.at[y3, xl, pl.ds(4, 2)], k.s_by.at[2], y_up)
    same_place(k.dwall.at[y3, xl, high_z], k.s_bx.at[1], x_other)
    arrived(k.dwall.at[y1, xl, high_z], k.s_by.at[1])
    same_place(k.dwall.at[y1, xl, pl.ds(6, 2)], k.s_by.at[3], y_down)
    same_place(k.dwall.at[y1, xl, high_z], k.s_bx.at[2], x_other)
    pair_back(zback[2])
    arrived(k.dwall.at[y2, xl, pl.ds(4, 2)], k.s_by.at[2])
    arrived(k.dwall.at[y2, xl, pl.ds(6, 2)], k.s_by.at[3])
    same_place(k.dwall.at[y2, xl, high_z], k.s_bx.at[3], x_other)
    bg_relay(4)
    pair_back(zof[3])
    arrived(k.dwall.at[y3, :, low_z], k.s_ay.at[0])
    same_place(k.dwall.at[y3, 0, low_z], k.s_ay.at[2], y_up)
    arrived(k.dwall.at[y1, :, low_z], k.s_ay.at[1])
    same_place(k.dwall.at[y1, 1, low_z], k.s_ay.at[3], y_down)
    pair_back(zback[3])
    pair_back(zof[4])
    arrived(k.dwall.at[y, 1 - xl, high_z], k.s_bx.at[0])
    arrived(k.dwall.at[y3, 1 - xl, high_z], k.s_bx.at[1])
    arrived(k.dwall.at[y1, 1 - xl, high_z], k.s_bx.at[2])
    arrived(k.dwall.at[y2, 1 - xl, high_z], k.s_bx.at[3])
    arrived(k.dwall.at[y2, 0, low_z], k.s_ay.at[2])
    arrived(k.dwall.at[y2, 1, low_z], k.s_ay.at[3])

    for n, _, who in cpeers:
        arrived(k.upd.at[who], k.s_upd.at[n])
        arrived(k.tok.at[who], k.s_tok.at[n])
        arrived(k.pjc.at[who], k.s_pc.at[n])
    k.o_upd[...] = k.upd[...]
    k.o_tok[...] = k.tok[...]
    k.o_proj[...] = k.pjc[0] + k.pjc[1] + k.pjc[2] + k.pjc[3]
    for n in range(8):
        for m in range(6):
            k.o_in[96 * n + 16 * m : 96 * n + 16 * m + 16] = k.dwall[m // 2, m % 2, n]
        if n < 6:
            for m in range(2):
                k.o_out[32 * n + 16 * m : 32 * n + 16 * m + 16] = k.dwall[3, m, n]
    for cond, d in started:
        if cond is None:
            d.wait_send()
        else:
            when(cond, lambda d=d: d.wait_send())


def copy_out(*refs):
    n = len(OUTPUTS)
    src, dst, buf, sems = refs[:n], refs[n : 2 * n], refs[2 * n : 3 * n], refs[3 * n]
    come = [pltpu.make_async_copy(src[m], buf[m], sems.at[m]) for m in range(n)]
    go = [pltpu.make_async_copy(buf[m], dst[m], sems.at[n + m]) for m in range(n)]
    for d in come:
        d.start()
    for d, e in zip(come, go):
        d.wait()
        e.start()
    for e in go:
        e.wait()


def on_device(
    tokens,
    atom_type,
    noise_step,
    pair_rep,
    bond_blocks,
    chiral_blocks,
    type_table,
    noise_row,
    norm_gain,
    pair_gain,
    in_weight,
    out_weight,
    pair_weight,
    restraint_weight,
    cotangent,
):
    args = dict(
        h_tokens=tokens[0],
        h_cot=cotangent[0],
        h_win=in_weight.reshape(768, 768),
        h_wout=out_weight,
        pair=pair_rep,
        atom=atom_type[None, :],
        step=noise_step[None, :],
        bonds=bond_blocks.T,
        chirs=chiral_blocks.T,
        table=type_table,
        nrow=noise_row[None, :],
        gain=norm_gain[None, :],
        pgain=pair_gain[None, :],
        pw=pair_weight.T,
        rw=restraint_weight,
    )
    vmem = pl.BlockSpec(memory_space=pltpu.VMEM)
    hbm = pl.BlockSpec(memory_space=pl.ANY)
    shapes = (
        jax.ShapeDtypeStruct((4, 32, 768), BF16),
        jax.ShapeDtypeStruct((4, 32, 768), BF16),
        jax.ShapeDtypeStruct((2048, 256), BF16),
        jax.ShapeDtypeStruct((768, 768), BF16),
        jax.ShapeDtypeStruct((192, 768), BF16),
        jax.ShapeDtypeStruct((16, 128), F32),
    )
    results = pl.pallas_call(
        kernel,
        out_shape=shapes,
        in_specs=[hbm if name.startswith("h_") or name == "pair" else vmem for name in INPUTS],
        out_specs=(vmem,) * 6,
        scratch_shapes=[pltpu.VMEM(*s) for s in SCRATCH.values()]
        + [pltpu.SemaphoreType.DMA((n,)) for n in SEMS.values()],
        compiler_params=pltpu.CompilerParams(
            collective_id=0, has_side_effects=True, vmem_limit_bytes=60 * 1024 * 1024
        ),
    )(*(args[name] for name in INPUTS))
    upd, tok, pg, ing, outg, proj = pl.pallas_call(
        copy_out,
        out_shape=shapes,
        in_specs=[hbm] * 6,
        out_specs=(hbm,) * 6,
        scratch_shapes=[pltpu.VMEM(s.shape, s.dtype) for s in shapes]
        + [pltpu.SemaphoreType.DMA((12,))],
    )(*results)
    return (
        upd.reshape(1, 128, 768),
        tok.reshape(1, 128, 768),
        jnp.swapaxes(pg.reshape(128, 16, 256), 1, 2),
        ing.reshape(4, 192, 768),
        outg,
        proj.T,
    )


def solution(mesh):
    torus = Mesh(
        mesh.devices.reshape(mesh.shape["samp"], 4, 2, 2, 2),
        ("samp", "row_0", "row_1", "col_0", "col_1"),
    )
    placed = (
        P("samp", ROW, None),
        P(ROW),
        P("samp"),
        P(ROW, COL, None),
        P(),
        P(),
        P(),
        P(),
        P(),
        P(),
        P(None, COL, None),
        P(COL, None),
        P(),
        P(),
        P("samp", ROW, None),
    )
    return jax.shard_map(
        on_device,
        mesh=torus,
        in_specs=placed,
        out_specs=(
            P("samp", ROW, None),
            P("samp", ROW, None),
            P(ROW, COL, "samp"),
            P(None, COL, None),
            P(COL, None),
            P(),
        ),
        check_vma=False,
    )
```

```python
import math

import jax
import jax.numpy as jnp
from jax import lax
from jax.experimental import pallas as pl
from jax.experimental.pallas import tpu as pltpu
from jax.sharding import Mesh
from jax.sharding import PartitionSpec as P

HEAD_DIM = 48
BLOCK = 32
STEPS = 200
COL = ("col_0", "col_1")
ROW = ("row_0", "row_1")
MESH = pl.DeviceIdType.MESH
F32, BF16 = jnp.float32, jnp.bfloat16
SCALE = 1.0 / math.sqrt(HEAD_DIM)
eps = 1e-05


def nn(a, b):
    return lax.dot_general(a, b, (((1,), (0,)), ((), ())), preferred_element_type=F32)


def nt(a, b):
    return lax.dot_general(a, b, (((1,), (1,)), ((), ())), preferred_element_type=F32)


def tn(a, b):
    return lax.dot_general(a, b, (((0,), (0,)), ((), ())), preferred_element_type=F32)


SCRATCH = dict(
    xbuf=((128, 256, 128), BF16),
    tokens=((128, 768), BF16),
    win=((768, 768), BF16),
    wout=((192, 768), BF16),
    base=((128, 768), F32),
    unit=((128, 768), F32),
    inv=((128, 1), F32),
    gate=((192, 128), F32),
    gmix=((192, 128), F32),
    waug=((80, 128), BF16),
    gh=((16, 1), F32),
    rst=((4, 16, 256), F32),
    amat=((2, 256, 256), BF16),
    emat=((256, 256), BF16),
    planes=((2, 2048, 128), F32),
    hat=((2048, 256), F32),
    invb=((2048, 256), F32),
    st=((128, 8, 256), F32),
    qg=((4, 2, 4, 48, 128), BF16),
    kvown=((2, 4, 48, 128), BF16),
    kv=((2, 4, 2, 4, 48, 128), BF16),
    nc=((8, 2, 128, 768), BF16),
    pr=((16, 128, 256), F32),
    dp=((16, 128, 256), F32),
    ot=((4, 4, 48, 128), BF16),
    oin=((4, 4, 48, 128), BF16),
    stats=((4, 48, 128), F32),
    acol=((128, 128), F32),
    arow=((4, 16, 128), F32),
    arow_own=((16, 128), F32),
    bgf=((2, 2048, 128), F32),
    bsp=((7, 2, 128, 128), BF16),
    bsm=((7, 2, 128, 128), BF16),
    brp=((7, 2, 128, 128), BF16),
    brm=((7, 2, 128, 128), BF16),
    bgt=((2, 256, 128), F32),
    bga=((8, 2, 256, 128), BF16),
    dqt=((4, 4, 48, 128), BF16),
    dqin=((4, 4, 48, 128), BF16),
    dkv=((2, 4, 2, 4, 48, 128), BF16),
    xin=((4, 2, 4, 48, 128), BF16),
    sx=((4, 2, 4, 48, 128), BF16),
    y1in=((4, 2, 4, 48, 128), BF16),
    y3in=((4, 2, 4, 48, 128), BF16),
    y2in=((4, 2, 4, 48, 128), BF16),
    fin=((4, 2, 4, 48, 128), BF16),
    dkvown=((2, 4, 48, 128), BF16),
    att=((192, 128), F32),
    gin=((768, 128), BF16),
    gsh=((2, 8, 64, 128), BF16),
    zsh=((2, 8, 64, 128), BF16),
    po=((4, 32, 768), BF16),
    por=((4, 32, 768), BF16),
    upd=((4, 32, 768), BF16),
    gn=((4, 32, 768), BF16),
    gnr=((4, 32, 768), BF16),
    tok=((4, 32, 768), BF16),
    dws=((2, 8, 16, 384), BF16),
    dwr=((2, 8, 16, 384), BF16),
    dwall=((2, 4, 2, 8, 16, 384), BF16),
    pjz=((8, 16, 128), F32),
    pjr=((8, 16, 128), F32),
    pjc=((4, 16, 128), F32),
    pj1=((16, 128), F32),
    pj2=((16, 128), F32),
)
SEMS = dict(
    s_pair=8,
    s_in=4,
    s_send=260,
    s_qgx=1,
    s_qgc=2,
    s_kvg=4,
    s_yb=4,
    s_xb=4,
    s_ncp=5,
    s_ncm=4,
    s_ncc=8,
    s_st=4,
    s_o=4,
    s_dq=4,
    s_xin=4,
    s_y2=4,
    s_y1=4,
    s_y3=4,
    s_fin=4,
    s_brp=7,
    s_brm=7,
    s_bgp=5,
    s_bgm=5,
    s_po=4,
    s_upd=4,
    s_gn=4,
    s_tok=4,
    s_zi=16,
    s_dw=16,
    s_dz=16,
    s_ax=2,
    s_ay=8,
    s_by=8,
    s_bx=8,
    s_pz=8,
    s_pr=8,
    s_pc=4,
)
INPUTS = (
    "h_tokens", "h_cot", "h_win", "h_wout", "pair",
    "atom", "step", "bonds", "chirs", "table", "nrow", "gain", "pgain", "pw", "rw",
)
OUTPUTS = ("o_upd", "o_tok", "o_pg", "o_in", "o_out", "o_proj")


def wide_row(ref):
    return jnp.concatenate([ref[n : n + 1] for n in range(6)], axis=1)


def kernel(*refs):
    names = INPUTS + OUTPUTS + tuple(SCRATCH) + tuple(SEMS)
    r = dict(zip(names, refs, strict=True))

    class R:
        pass

    k = R()
    k.__dict__.update(r)
    z = lax.axis_index("samp")
    y = lax.axis_index("row_0")
    xl = lax.axis_index("row_1")
    xh = lax.axis_index("col_0")
    co = lax.axis_index("col_1")
    c = 2 * xh + co
    row = 2 * y + xl
    zof = [lax.rem(z + n, 8) for n in range(8)]
    zback = [lax.rem(z + 8 - n, 8) for n in range(8)]
    yof = [lax.rem(y + n, 4) for n in range(4)]
    dy = lax.rem(y + 4 - c, 4)
    x_other = {"row_1": 1 - xl}
    y_up = {"row_0": yof[1]}
    y_down = {"row_0": yof[3]}
    z_up = {"samp": zof[1]}
    z_down = {"samp": zof[7]}
    core_other = {"col_1": 1 - co}
    xh_other = {"col_0": 1 - xh}
    c_core = 2 * xh + (1 - co)
    c_xh = 2 * (1 - xh) + co
    cpeers = []
    for n in range(1, 4):
        ph, pc = lax.rem(xh + n // 2, 2), lax.rem(co + n % 2, 2)
        cpeers.append((n, {"col_0": ph, "col_1": pc}, 2 * ph + pc))
    rpeers = []
    for n in range(1, 8):
        py, px = lax.rem(y + n // 2, 4), lax.rem(xl + n % 2, 2)
        fy, fx = lax.rem(y + 4 - n // 2, 4), lax.rem(xl + n % 2, 2)
        rpeers.append((n, {"row_0": py, "row_1": px}, 2 * py + px, 2 * fy + fx))

    loads = [
        pltpu.make_async_copy(k.h_tokens, k.tokens, k.s_in.at[0]),
        pltpu.make_async_copy(k.h_win, k.win, k.s_in.at[1]),
        pltpu.make_async_copy(k.h_cot, k.nc.at[z, 1], k.s_in.at[2]),
        pltpu.make_async_copy(k.h_wout, k.wout, k.s_in.at[3]),
    ]
    for copy in loads:
        copy.start()
    pair_copies = []
    for n in range(8):
        part = pl.ds(16 * n, 16)
        copy = pltpu.make_async_copy(k.pair.at[part], k.xbuf.at[part], k.s_pair.at[n])
        copy.start()
        pair_copies.append(copy)

    barrier = pltpu.get_barrier_semaphore()
    for n in range(1, 8):
        pl.semaphore_signal(barrier, inc=1, device_id={"samp": zof[n]}, device_id_type=MESH)
    for _, dev, _, _ in rpeers:
        pl.semaphore_signal(barrier, inc=1, device_id=dev, device_id_type=MESH)
    for _, dev, _ in cpeers:
        pl.semaphore_signal(barrier, inc=1, device_id=dev, device_id_type=MESH)

    types = lax.broadcasted_iota(jnp.int32, (32, 128), 0) == k.atom[...]
    top_root = 160.0 ** (1.0 / 7.0)
    low_root = 0.0004 ** (1.0 / 7.0)
    root = top_root + k.step[...].astype(F32) / (STEPS - 1) * (low_root - top_root)
    level = 7.0 / 4.0 * jnp.log(root)
    add = tn(types.astype(F32).astype(BF16), k.table[...]) + level * wide_row(k.nrow)
    loads[0].wait()
    base = k.tokens[...].astype(F32) + add
    k.base[...] = base
    centered = base - jnp.mean(base, axis=1, keepdims=True)
    inv = lax.rsqrt(jnp.mean(centered * centered, axis=1, keepdims=True) + eps)
    unit = centered * inv
    k.inv[...] = inv
    k.unit[...] = unit
    normed = (unit * wide_row(k.gain)).astype(BF16)
    k.nc[z, 0] = normed
    loads[1].wait()
    proj_kv = nt(k.win[192:576], normed)
    for m in range(2):
        for hh in range(4):
            at = 192 * m + 48 * hh
            k.kvown[m, hh] = proj_kv[at : at + 48].astype(BF16)
    pl.semaphore_wait(barrier, 17)

    started = []
    count = [0]

    def make(src, dst, sem, dev):
        d = pltpu.make_async_remote_copy(
            src_ref=src,
            dst_ref=dst,
            send_sem=k.s_send.at[count[0]],
            recv_sem=sem,
            device_id=dev,
            device_id_type=MESH,
        )
        count[0] += 1
        return d

    def send(src, dst, sem, dev):
        d = make(src, dst, sem, dev)
        d.start()
        started.append((None, d))

    def arrived(dst, sem):
        pltpu.make_async_remote_copy(
            src_ref=dst,
            dst_ref=dst,
            send_sem=k.s_send.at[0],
            recv_sem=sem,
            device_id=z_up,
            device_id_type=MESH,
        ).wait_recv()

    def when(cond, body):
        pl.when(cond)(body)

    gather_kv = make(
        k.kvown,
        k.kv.at[xl, c],
        k.s_kvg.at[2 * lax.rem(xh + y // 2, 2) + lax.rem(co + y % 2, 2)],
        {"col_0": y // 2, "col_1": y % 2},
    )
    started.append((dy != 0, gather_kv))
    when(dy != 0, lambda: gather_kv.start())
    groups = (c, c_core, c_xh, 2 * (1 - xh) + 1 - co)
    to_x = [make(k.kv.at[xl, g], k.kv.at[xl, g], k.s_xb.at[n], x_other) for n, g in enumerate(groups)]
    to_up = [make(k.kv.at[xl, g], k.kv.at[xl, g], k.s_yb.at[n], y_up) for n, g in enumerate(groups)]
    to_down = [make(k.kv.at[xl, g], k.kv.at[xl, g], k.s_yb.at[n], y_down) for n, g in enumerate(groups)]
    started += [(None, d) for d in to_x]
    started += [(dy == 0, d) for d in to_up + to_down]
    started += [(dy == 1, to_up[0]), (dy == 1, to_up[2]), (dy == 3, to_down[1]), (dy == 3, to_down[3])]

    def kv_step(n):
        def source():
            if n == 0:
                k.kv[xl, c] = k.kvown[...]
            else:
                arrived(k.kv.at[xl, groups[n]], k.s_kvg.at[n])
            to_up[n].start()
            to_down[n].start()
            to_x[n].start()

        def relay(near):
            arrived(k.kv.at[xl, groups[n]], k.s_yb.at[n])
            if near is not None:
                near[n].start()
            to_x[n].start()

        when(dy == 0, source)
        when(dy == 1, lambda: relay(to_up if n % 2 == 0 else None))
        when(dy == 3, lambda: relay(to_down if n % 2 == 1 else None))
        when(dy == 2, lambda: relay(None))

    def kv_first():
        k.kv[xl, c] = k.kvown[...]
        to_up[0].start()
        to_down[0].start()
        to_x[0].start()

    when(dy == 0, kv_first)
    loads[3].wait()
    loads[2].wait()
    proj_q = nt(k.win[0:192], normed)
    gate = jax.nn.sigmoid(nt(k.win[576:768], normed))
    gmix = nt(k.wout[...], k.nc[z, 1])
    k.gate[...] = gate
    k.gmix[...] = gmix
    grad_attend = gmix * gate
    for hh in range(4):
        k.qg[c, 0, hh] = proj_q[48 * hh : 48 * hh + 48].astype(BF16)
        k.qg[c, 1, hh] = grad_attend[48 * hh : 48 * hh + 48].astype(BF16)
    send(k.qg.at[c], k.qg.at[c], k.s_qgx.at[0], xh_other)
    send(k.qg.at[c], k.qg.at[c], k.s_qgc.at[0], core_other)
    half = pl.ds(64 * co, 64)
    send(k.nc.at[z, :, half], k.nc.at[z, :, half], k.s_ncp.at[1], z_up)
    send(k.nc.at[z, :, half], k.nc.at[z, :, half], k.s_ncm.at[1], z_down)

    weights = k.pw[...] * k.pgain[...]
    w_hi = weights.astype(BF16)
    rest = weights - w_hi.astype(F32)
    w_mid = rest.astype(BF16)
    w_lo = (rest - w_mid.astype(F32)).astype(BF16)
    sub16 = lax.broadcasted_iota(jnp.int32, (16, 128), 0)
    lane16 = lax.broadcasted_iota(jnp.int32, (16, 128), 1)
    pick = (lane16 == 16 * z + sub16).astype(F32).astype(BF16)
    k.waug[0:16] = w_hi
    k.waug[16:32] = w_mid
    k.waug[32:48] = w_lo
    k.waug[48:64] = pick
    k.waug[64:80] = jnp.ones((16, 128), BF16)
    k.gh[...] = jnp.sum(weights, axis=1, keepdims=True)
    spread = weights - jnp.mean(weights, axis=1, keepdims=True)
    s_hi = spread.astype(BF16)
    s_lo = (spread - s_hi.astype(F32)).astype(BF16)
    sub256 = lax.broadcasted_iota(jnp.int32, (256, 256), 0)
    lane256 = lax.broadcasted_iota(jnp.int32, (256, 256), 1)
    same = (sub256 // 16) == (lane256 // 16)
    tall = (
        lax.broadcasted_iota(jnp.int32, (256, 16), 0) % 16 == lax.broadcasted_iota(jnp.int32, (256, 16), 1)
    ).astype(F32).astype(BF16)
    for n, part in enumerate((s_hi, s_lo)):
        small = nt(pick, part).astype(BF16)
        wide = nt(nn(tall, small).astype(BF16), tall)
        k.amat[n] = jnp.where(same, wide, 0.0).astype(BF16)
    k.emat[...] = jnp.where(same, 1.0 / 128.0, 0.0).astype(BF16)
    eye = lax.broadcasted_iota(jnp.int32, (16, 16), 0) == lax.broadcasted_iota(jnp.int32, (16, 16), 1)

    def block_counts(ref, total):
        first = (lax.broadcasted_iota(jnp.int32, (16, total), 0) + 4 * row) == ref[0:1]
        second = lax.broadcasted_iota(jnp.int32, (256, total), 0) // BLOCK + 8 * c == ref[1:2]
        return nt(first.astype(F32).astype(BF16), second.astype(F32).astype(BF16))

    bond = block_counts(k.bonds, 64)
    chir = block_counts(k.chirs, 32)
    w_bond = jnp.sum(jnp.where(eye, k.rw[0:1], 0.0), axis=1, keepdims=True)
    w_chir = jnp.sum(jnp.where(eye, k.rw[1:2], 0.0), axis=1, keepdims=True)
    for n in range(4):
        k.rst[n] = w_bond * bond[n : n + 1] + w_chir * chir[n : n + 1]

    ones = jnp.ones((8, 128), BF16)

    def pair_rows(n):
        pair_copies[n].wait()

        def body(i, carry):
            x = k.xbuf[i]
            res = nt(k.waug[...], x)
            xf = x.astype(F32)
            sq = xf * xf
            hi = sq.astype(BF16)
            lo = (sq - hi.astype(F32)).astype(BF16)
            ss = nt(ones, hi) + nt(ones, lo)
            mean = res[64:65] * (1.0 / 128.0)
            var = ss[0:1] * (1.0 / 128.0) - mean * mean
            inv = lax.rsqrt(jnp.maximum(var, 0.0) + eps)
            bias = res[0:16] + res[16:32] + res[32:48]
            bias = inv * (bias - mean * k.gh[...])
            rows = pl.ds(pl.multiple_of(i * 16, 16), 16)
            k.planes[0, rows, :] = bias[:, :128]
            k.planes[1, rows, :] = bias[:, 128:]
            k.hat[rows, :] = (res[48:64] - mean) * (inv * inv)
            k.invb[rows, :] = jnp.broadcast_to(inv, (16, 256))
            k.st[i, 0:1] = inv
            k.st[i, 1:2] = mean * inv
            return carry

        lax.fori_loop(16 * n, 16 * n + 16, body, 0, unroll=4)

    def nc_relay(n):
        src = k.nc.at[zback[n], :, half]
        arrived(src, k.s_ncp.at[n])
        if n < 4:
            send(src, src, k.s_ncp.at[n + 1], z_up)
        send(src, src, k.s_ncc.at[n], core_other)
        if n < 4:
            src = k.nc.at[zof[n], :, half]
            arrived(src, k.s_ncm.at[n])
            if n < 3:
                send(src, src, k.s_ncm.at[n + 1], z_down)
            send(src, src, k.s_ncc.at[8 - n], core_other)

    pair_rows(0)
    when(dy != 0, lambda: kv_step(0))
    pair_rows(1)
    kv_step(1)
    pair_rows(2)
    arrived(k.qg.at[c_xh], k.s_qgx.at[0])
    send(k.qg.at[c_xh], k.qg.at[c_xh], k.s_qgc.at[1], core_other)
    kv_step(2)
    pair_rows(3)
    kv_step(3)
    pair_rows(4)
    nc_relay(1)
    pair_rows(5)
    pair_rows(6)
    pair_rows(7)
    nc_relay(2)
    for n, g in enumerate(groups):
        arrived(k.kv.at[1 - xl, g], k.s_xb.at[n])
    arrived(k.qg.at[c_core], k.s_qgc.at[0])
    arrived(k.qg.at[2 * (1 - xh) + 1 - co], k.s_qgc.at[1])

    lane = lax.broadcasted_iota(jnp.int32, (128, 128), 1)

    def head_kv(g, m, hh):
        return jnp.concatenate([k.kv[0, g, m, hh], k.kv[1, g, m, hh]], axis=1)

    def forward(h, packed):
        g, hh = h // 4, h % 4
        keys = head_kv(g, 0, hh)
        vals = head_kv(g, 1, hh)
        by_head = pl.ds(h, 128, stride=16)
        bias = jnp.concatenate([k.planes[0, by_head, :], k.planes[1, by_head, :]], axis=1)
        extra = [jnp.broadcast_to(k.rst[n, pl.ds(h, 1), :], (32, 256)) for n in range(4)]
        s = tn(k.qg[g, 0, hh], keys) * SCALE + (bias + jnp.concatenate(extra, axis=0))
        top = jnp.max(s, axis=1, keepdims=True)
        p = jnp.exp(s - top)
        dp = tn(k.qg[g, 1, hh], vals)
        k.pr[h] = p
        k.dp[h] = dp
        k.ot[g, hh] = nt(vals, p.astype(BF16)).astype(BF16)
        total = jnp.sum(p, axis=1, keepdims=True)
        dots = jnp.sum(p * dp, axis=1, keepdims=True)
        packed = jnp.where(lane == h, top, packed)
        packed = jnp.where(lane == 16 + h, total, packed)
        return jnp.where(lane == 32 + h, dots, packed)

    packed = lax.fori_loop(0, 16, forward, jnp.zeros((128, 128), F32), unroll=2)
    k.stats[c] = packed.T[0:48]
    for n, dev, _ in cpeers:
        send(k.stats.at[c], k.stats.at[c], k.s_st.at[n], dev)
    for n, dev, who in cpeers:
        send(k.ot.at[who], k.oin.at[c], k.s_o.at[n], dev)
    k.oin[c] = k.ot[c]
    nc_relay(3)
    for n, _, who in cpeers:
        arrived(k.stats.at[who], k.s_st.at[n])
    top = k.stats[0, 0:16]
    for n in range(1, 4):
        top = jnp.maximum(top, k.stats[n, 0:16])
    total = jnp.zeros((16, 128), F32)
    dots = jnp.zeros((16, 128), F32)
    for n in range(4):
        w = jnp.exp(k.stats[n, 0:16] - top)
        k.arow[n] = w
        total += w * k.stats[n, 16:32]
        dots += w * k.stats[n, 32:48]
    inv_total = 1.0 / total
    for n in range(4):
        k.arow[n] = k.arow[n] * inv_total
    own = k.arow[c]
    k.arow_own[...] = own
    k.acol[...] = jnp.concatenate([own, dots * inv_total, jnp.zeros((96, 128), F32)], axis=0).T

    def backward(h, carry):
        g, hh = h // 4, h % 4
        columns = k.acol[...]
        alpha = jnp.sum(jnp.where(lane == h, columns, 0.0), axis=1, keepdims=True)
        delta = jnp.sum(jnp.where(lane == 16 + h, columns, 0.0), axis=1, keepdims=True)
        p = k.pr[h]
        ds = p * alpha * (k.dp[h] - delta)
        by_head = pl.ds(h, 128, stride=16)
        k.bgf[0, by_head, :] = ds[:, :128]
        k.bgf[1, by_head, :] = ds[:, 128:]
        low = ds.astype(BF16)
        k.dqt[g, hh] = (nt(head_kv(g, 0, hh), low) * SCALE).astype(BF16)
        dk = (nn(k.qg[g, 0, hh], low) * SCALE).astype(BF16)
        k.dkv[0, g, 0, hh] = dk[:, :128]
        k.dkv[1, g, 0, hh] = dk[:, 128:]
        ga = (k.qg[g, 1, hh].astype(F32) * k.arow_own[pl.ds(h, 1), :]).astype(BF16)
        dv = nn(ga, p.astype(BF16)).astype(BF16)
        k.dkv[0, g, 1, hh] = dv[:, :128]
        k.dkv[1, g, 1, hh] = dv[:, 128:]
        return carry

    def key_value_out(n):
        lax.fori_loop(4 * n, 4 * n + 4, backward, 0, unroll=2)
        send(k.dkv.at[1 - xl, n], k.xin.at[n], k.s_xin.at[n], x_other)
        d = make(
            k.dqt.at[n],
            k.dqin.at[c],
            k.s_dq.at[2 * lax.rem(xh + n // 2, 2) + lax.rem(co + n % 2, 2)],
            {"col_0": n // 2, "col_1": n % 2},
        )
        started.append((c != n, d))
        when(c != n, lambda: d.start())

    key_value_out(0)
    key_value_out(1)

    for n, _, who in cpeers:
        arrived(k.oin.at[who], k.s_o.at[n])
    for hh in range(4):
        att = jnp.zeros((48, 128), F32)
        for n in range(4):
            w = k.arow[n, pl.ds(4 * c + hh, 1), :]
            att += k.oin[n, hh].astype(F32) * w
        k.att[48 * hh : 48 * hh + 48] = att
    gate = k.gate[...]
    att = k.att[...]
    mixed = (gate * att).astype(BF16)
    grad_gate = (k.gmix[...] * att * gate * (1.0 - gate)).astype(BF16)
    k.gin[576:768] = grad_gate
    for n in range(4):
        k.gsh[0, 4 + n, 0:48] = grad_gate[48 * n : 48 * n + 48]
    for n in range(8):
        for m in range(2):
            at = 32 * n + 16 * m
            k.gsh[m, n, 48:64] = mixed[at : at + 16] if n < 6 else jnp.zeros((16, 128), BF16)
    part_out = tn(mixed, k.wout[...]).astype(BF16)
    for n in range(4):
        k.po[n] = part_out[32 * n : 32 * n + 32]
    for n, dev, who in cpeers:
        send(k.po.at[who], k.por.at[c], k.s_po.at[n], dev)
    k.por[c] = k.po[c]

    key_value_out(2)
    key_value_out(3)
    k.dqin[c] = k.dqt[c]

    def ring_step(n):
        for back, stage, come, sem, dev, first in (
            (zback, k.bsp, k.brp, k.s_brp, z_up, 0),
            (zof, k.bsm, k.brm, k.s_brm, z_down, 128),
        ):
            owner = back[1 + n]
            part = pl.ds(pl.multiple_of(owner * 256 + first, 128), 128)
            value = k.bgf[:, part, :]
            if n > 0:
                arrived(come.at[n - 1], sem.at[n - 1])
                value = value + come[n - 1].astype(F32)
            stage[n] = value.astype(BF16)
            send(stage.at[n], come.at[n], sem.at[n], dev)

    ring_step(0)
    def share(b):
        for n in range(1, 8):
            send(k.gsh.at[b, zof[n]], k.zsh.at[b, z], k.s_zi.at[8 * b + n], {"samp": zof[n]})
        k.zsh[b, z] = k.gsh[b, z]

    def weight_rows(b):
        for n in range(1, 8):
            arrived(k.zsh.at[b, zback[n]], k.s_zi.at[8 * b + n])
        acc = nn(k.zsh[b, 0, 0:48], k.nc[0, 0])
        acc_out = nn(k.zsh[b, 0, 48:64], k.nc[0, 1])
        for n in range(1, 8):
            acc += nn(k.zsh[b, n, 0:48], k.nc[n, 0])
            acc_out += nn(k.zsh[b, n, 48:64], k.nc[n, 1])
        for n in range(4):
            tall = (acc[16 * n : 16 * n + 16] if n < 3 else acc_out).astype(BF16)
            k.dws[b, 2 * n] = tall[:, :384]
            k.dws[b, 2 * n + 1] = tall[:, 384:]
        for n, dev, to, _ in rpeers:
            send(k.dws.at[b, to], k.dwr.at[b, row], k.s_dw.at[8 * b + n], dev)
        k.dwr[b, row] = k.dws[b, row]

    def weight_sum(b):
        for n, _, _, came in rpeers:
            arrived(k.dwr.at[b, came], k.s_dw.at[8 * b + n])
        total = k.dwr[b, 0].astype(F32)
        for n in range(1, 8):
            total += k.dwr[b, n].astype(F32)
        k.dwall[b, y, xl, z] = total.astype(BF16)
        for n in range(1, 8):
            here = k.dwall.at[b, y, xl, z]
            send(here, here, k.s_dz.at[8 * b + n], {"samp": zof[n]})

    low_z, high_z = pl.ds(0, 4), pl.ds(4, 4)
    y1, y2, y3 = yof[1], yof[2], yof[3]

    def same_place(ref, sem, dev):
        send(ref, ref, sem, dev)

    def spread_1(b):
        w, ay, by, bx = k.dwall.at[b], 4 * b, 4 * b, 4 * b
        for n in range(1, 8):
            arrived(w.at[y, xl, zback[n]], k.s_dz.at[8 * b + n])
        same_place(w.at[y, xl, low_z], k.s_ax.at[b], x_other)
        same_place(w.at[y, xl, high_z], k.s_by.at[by], y_up)
        same_place(w.at[y, xl, high_z], k.s_by.at[by + 1], y_down)
        same_place(w.at[y, xl, high_z], k.s_bx.at[bx], x_other)

    def spread_2(b):
        w, ay, by, bx = k.dwall.at[b], 4 * b, 4 * b, 4 * b
        arrived(w.at[y, 1 - xl, low_z], k.s_ax.at[b])
        same_place(w.at[y, :, low_z], k.s_ay.at[ay], y_up)
        same_place(w.at[y, :, low_z], k.s_ay.at[ay + 1], y_down)
        arrived(w.at[y3, xl, high_z], k.s_by.at[by])
        same_place(w.at[y3, xl, pl.ds(4, 2)], k.s_by.at[by + 2], y_up)
        same_place(w.at[y3, xl, high_z], k.s_bx.at[bx + 1], x_other)
        arrived(w.at[y1, xl, high_z], k.s_by.at[by + 1])
        same_place(w.at[y1, xl, pl.ds(6, 2)], k.s_by.at[by + 3], y_down)
        same_place(w.at[y1, xl, high_z], k.s_bx.at[bx + 2], x_other)

    def spread_3(b):
        w, ay, by, bx = k.dwall.at[b], 4 * b, 4 * b, 4 * b
        arrived(w.at[y3, :, low_z], k.s_ay.at[ay])
        same_place(w.at[y3, 0, low_z], k.s_ay.at[ay + 2], y_up)
        arrived(w.at[y1, :, low_z], k.s_ay.at[ay + 1])
        same_place(w.at[y1, 1, low_z], k.s_ay.at[ay + 3], y_down)
        arrived(w.at[y2, xl, pl.ds(4, 2)], k.s_by.at[by + 2])
        arrived(w.at[y2, xl, pl.ds(6, 2)], k.s_by.at[by + 3])
        same_place(w.at[y2, xl, high_z], k.s_bx.at[bx + 3], x_other)

    def spread_4(b):
        w, ay, by, bx = k.dwall.at[b], 4 * b, 4 * b, 4 * b
        arrived(w.at[y, 1 - xl, high_z], k.s_bx.at[bx])
        arrived(w.at[y3, 1 - xl, high_z], k.s_bx.at[bx + 1])
        arrived(w.at[y1, 1 - xl, high_z], k.s_bx.at[bx + 2])
        arrived(w.at[y2, 1 - xl, high_z], k.s_bx.at[bx + 3])
        arrived(w.at[y2, 0, low_z], k.s_ay.at[ay + 2])
        arrived(w.at[y2, 1, low_z], k.s_ay.at[ay + 3])

    def plus(dst, piece, a, b):
        dst[piece] = (a.astype(F32) + b.astype(F32)).astype(BF16)

    r2 = [
        make(k.sx.at[n], k.y2in.at[n], k.s_y2.at[n], y_down if n % 2 == 0 else y_up)
        for n in range(4)
    ]
    r1 = [make(k.sx.at[n], k.y1in.at[n], k.s_y1.at[n], y_down) for n in range(4)]
    r3 = [make(k.sx.at[n], k.y3in.at[n], k.s_y3.at[n], y_up) for n in range(4)]
    started += [(dy == 2, d) for d in r2] + [(dy == 1, d) for d in r1] + [(dy == 3, d) for d in r3]
    spread_kv = {}
    for n in range(4):
        spread_kv[n] = make(
            k.fin.at[n],
            k.dkvown,
            k.s_fin.at[2 * lax.rem(xh + n // 2, 2) + lax.rem(co + n % 2, 2)],
            {"col_0": n // 2, "col_1": n % 2},
        )
        started.append((jnp.logical_and(dy == 0, c != n), spread_kv[n]))

    def first_sum(n):
        arrived(k.xin.at[n], k.s_xin.at[n])
        plus(k.sx, n, k.dkv[xl, n], k.xin[n])
        when(dy == 2, lambda: r2[n].start())
        when(dy == 1 if n % 2 == 1 else dy == 3, lambda: (r1 if n % 2 == 1 else r3)[n].start())

    def second_sum(n):
        def body():
            arrived(k.y2in.at[n], k.s_y2.at[n])
            plus(k.sx, n, k.sx[n], k.y2in[n])
            (r1 if n % 2 == 0 else r3)[n].start()

        when(dy == 1 if n % 2 == 0 else dy == 3, body)

    def keep(n):
        k.dkvown[...] = k.fin[n]

    def last_sum(n):
        def body():
            arrived(k.y1in.at[n], k.s_y1.at[n])
            arrived(k.y3in.at[n], k.s_y3.at[n])
            total = k.sx[n].astype(F32) + k.y1in[n].astype(F32) + k.y3in[n].astype(F32)
            k.fin[n] = total.astype(BF16)

            when(c == n, lambda: keep(n))
            when(c != n, lambda: spread_kv[n].start())

        when(dy == 0, body)

    first_sum(0)
    first_sum(1)
    for n, _, who in cpeers:
        arrived(k.dqin.at[who], k.s_dq.at[n])
    for hh in range(4):
        dq = k.dqin[0, hh].astype(F32)
        for n in range(1, 4):
            dq += k.dqin[n, hh].astype(F32)
        k.gin[48 * hh : 48 * hh + 48] = dq.astype(BF16)
        k.gsh[0, hh, 0:48] = dq.astype(BF16)
    share(0)
    ring_step(1)
    first_sum(2)
    second_sum(0)
    second_sum(1)
    first_sum(3)
    ring_step(2)
    second_sum(2)
    second_sum(3)
    nc_relay(4)
    for n in range(1, 8):
        arrived(k.nc.at[zback[n], :, pl.ds(64 * (1 - co), 64)], k.s_ncc.at[n])
    last_sum(0)
    last_sum(1)
    weight_rows(0)
    ring_step(3)
    last_sum(2)
    last_sum(3)
    weight_sum(0)
    when(
        dy != 0,
        lambda: arrived(k.dkvown, k.s_fin.at[2 * lax.rem(xh + y // 2, 2) + lax.rem(co + y % 2, 2)]),
    )
    for hh in range(4):
        k.gin[192 + 48 * hh : 240 + 48 * hh] = k.dkvown[0, hh]
        k.gin[384 + 48 * hh : 432 + 48 * hh] = k.dkvown[1, hh]
        k.gsh[1, hh, 0:48] = k.dkvown[0, hh]
        k.gsh[1, 4 + hh, 0:48] = k.dkvown[1, hh]
    share(1)
    ring_step(4)
    part_normed = tn(k.gin[...], k.win[...]).astype(BF16)
    for n in range(4):
        k.gn[n] = part_normed[32 * n : 32 * n + 32]
    for n, dev, who in cpeers:
        send(k.gn.at[who], k.gnr.at[c], k.s_gn.at[n], dev)
    k.gnr[c] = k.gn[c]

    for n, _, who in cpeers:
        arrived(k.por.at[who], k.s_po.at[n])
    mine = pl.ds(pl.multiple_of(32 * c, 32), 32)
    total = k.base[mine]
    for n in range(4):
        total = total + k.por[n].astype(F32)
    k.upd[c] = total.astype(BF16)
    for n, dev, _ in cpeers:
        send(k.upd.at[c], k.upd.at[c], k.s_upd.at[n], dev)
    spread_1(0)
    ring_step(5)
    weight_rows(1)
    spread_2(0)

    ring_step(6)
    for first, come, sem in ((0, k.brp, k.s_brp), (128, k.brm, k.s_brm)):
        arrived(come.at[6], sem.at[6])
        part = pl.ds(pl.multiple_of(z * 256 + first, 128), 128)
        k.bgt[:, first : first + 128] = k.bgf[:, part, :] + come[6].astype(F32)
    k.bga[z] = k.bgt[...].astype(BF16)
    send(k.bga.at[z], k.bga.at[z], k.s_bgp.at[1], z_up)
    send(k.bga.at[z], k.bga.at[z], k.s_bgm.at[1], z_down)

    def bg_relay(n):
        if n < 4:
            below, above = k.bga.at[zback[n]], k.bga.at[zof[n]]
            arrived(below, k.s_bgp.at[n])
            if n == 3:
                below, above = below.at[:, 0:128], above.at[:, 128:256]
            send(below, below, k.s_bgp.at[n + 1], z_up)
            arrived(k.bga.at[zof[n]], k.s_bgm.at[n])
            send(above, above, k.s_bgm.at[n + 1], z_down)
        else:
            arrived(k.bga.at[zof[4], :, 0:128], k.s_bgp.at[4])
            arrived(k.bga.at[zof[4], :, 128:256], k.s_bgm.at[4])

    def pair_back(owner):
        bg = jnp.concatenate([k.bga[owner, 0], k.bga[owner, 1]], axis=1)
        rows = pl.ds(pl.multiple_of(owner * 256, 256), 256)
        plane = jnp.concatenate([k.planes[0, rows, :], k.planes[1, rows, :]], axis=1)
        product = bg.astype(F32) * plane
        hi = product.astype(BF16)
        lo = (product - hi.astype(F32)).astype(BF16)
        both = nn(k.emat[...], hi) + nn(k.emat[...], lo)
        out = nn(k.amat[0], bg) + nn(k.amat[1], bg)
        k.o_pg[rows, :] = (k.invb[rows, :] * out - k.hat[rows, :] * both).astype(BF16)

    def project_pairs(n, carry):
        acc, low = carry
        part = pl.ds(pl.multiple_of(n * 16, 16), 16)
        bg = jnp.concatenate([k.bgt[0, part, :], k.bgt[1, part, :]], axis=1)
        i = 16 * z + n
        scaled = bg * k.st[i, 0:1]
        hi = scaled.astype(BF16)
        rest = (scaled - hi.astype(F32)).astype(BF16)
        acc = acc + nn(jnp.concatenate([hi, rest], axis=0), k.xbuf[i])
        low = low + jnp.sum(bg * k.st[i, 1:2], axis=1, keepdims=True)
        return (acc, low)

    acc, low = lax.fori_loop(
        0, 16, project_pairs, (jnp.zeros((32, 128), F32), jnp.zeros((16, 1), F32)), unroll=2
    )
    k.pj1[...] = k.pgain[...] * (acc[0:16] + acc[16:32] - low)
    for n in range(1, 8):
        send(k.pj1, k.pjz.at[z], k.s_pz.at[n], {"samp": zof[n]})
    k.pjz[z] = k.pj1[...]

    for n, _, who in cpeers:
        arrived(k.gnr.at[who], k.s_gn.at[n])
    total = k.gnr[0].astype(F32)
    for n in range(1, 4):
        total += k.gnr[n].astype(F32)
    scaled = total * wide_row(k.gain)
    hat = k.unit[mine]
    back = k.inv[mine] * (
        scaled
        - jnp.mean(scaled, axis=1, keepdims=True)
        - hat * jnp.mean(scaled * hat, axis=1, keepdims=True)
    )
    k.tok[c] = (k.nc[z, 1, mine].astype(F32) + back).astype(BF16)
    for n, dev, _ in cpeers:
        send(k.tok.at[c], k.tok.at[c], k.s_tok.at[n], dev)

    weight_sum(1)
    bg_relay(1)
    for n in range(1, 8):
        arrived(k.pjz.at[zback[n]], k.s_pz.at[n])
    total = k.pjz[0]
    for n in range(1, 8):
        total += k.pjz[n]
    k.pj2[...] = total
    for n, dev, _, _ in rpeers:
        send(k.pj2, k.pjr.at[row], k.s_pr.at[n], dev)
    k.pjr[row] = total

    spread_3(0)
    spread_1(1)
    pair_back(z)
    bg_relay(2)
    for n, _, _, came in rpeers:
        arrived(k.pjr.at[came], k.s_pr.at[n])
    total = k.pjr[0]
    for n in range(1, 8):
        total += k.pjr[n]
    k.pjc[c] = total
    for n, dev, _ in cpeers:
        send(k.pjc.at[c], k.pjc.at[c], k.s_pc.at[n], dev)
    pair_back(zof[1])
    pair_back(zback[1])

    spread_2(1)
    bg_relay(3)
    pair_back(zof[2])
    pair_back(zback[2])
    spread_4(0)
    spread_3(1)
    pair_back(zof[3])
    bg_relay(4)
    pair_back(zback[3])
    pair_back(zof[4])
    spread_4(1)

    for n, _, who in cpeers:
        arrived(k.upd.at[who], k.s_upd.at[n])
        arrived(k.tok.at[who], k.s_tok.at[n])
        arrived(k.pjc.at[who], k.s_pc.at[n])
    k.o_upd[...] = k.upd[...]
    k.o_tok[...] = k.tok[...]
    k.o_proj[...] = k.pjc[0] + k.pjc[1] + k.pjc[2] + k.pjc[3]
    for b in range(2):
        for half_of in range(2):
            lanes = slice(384 * half_of, 384 * half_of + 384)
            for n in range(8):
                member = ((0, 3), (1, 2))[b][n // 4]
                for m in range(3):
                    at = 192 * member + 48 * (n % 4) + 16 * m
                    k.o_in[at : at + 16, lanes] = k.dwall[b, m, half_of, n]
                if n < 6:
                    at = 32 * n + 16 * b
                    k.o_out[at : at + 16, lanes] = k.dwall[b, 3, half_of, n]
    for cond, d in started:
        if cond is None:
            d.wait_send()
        else:
            when(cond, lambda d=d: d.wait_send())


def copy_out(*refs):
    n = len(OUTPUTS)
    src, dst, buf, sems = refs[:n], refs[n : 2 * n], refs[2 * n : 3 * n], refs[3 * n]
    come = [pltpu.make_async_copy(src[m], buf[m], sems.at[m]) for m in range(n)]
    go = [pltpu.make_async_copy(buf[m], dst[m], sems.at[n + m]) for m in range(n)]
    for d in come:
        d.start()
    for d, e in zip(come, go):
        d.wait()
        e.start()
    for e in go:
        e.wait()


def on_device(
    tokens,
    atom_type,
    noise_step,
    pair_rep,
    bond_blocks,
    chiral_blocks,
    type_table,
    noise_row,
    norm_gain,
    pair_gain,
    in_weight,
    out_weight,
    pair_weight,
    restraint_weight,
    cotangent,
):
    args = dict(
        h_tokens=tokens[0],
        h_cot=cotangent[0],
        h_win=in_weight.reshape(768, 768),
        h_wout=out_weight,
        pair=pair_rep,
        atom=atom_type[None, :],
        step=noise_step[None, :],
        bonds=bond_blocks.T,
        chirs=chiral_blocks.T,
        table=type_table,
        nrow=noise_row.reshape(6, 128),
        gain=norm_gain.reshape(6, 128),
        pgain=pair_gain[None, :],
        pw=pair_weight.T,
        rw=restraint_weight,
    )
    vmem = pl.BlockSpec(memory_space=pltpu.VMEM)
    hbm = pl.BlockSpec(memory_space=pl.ANY)
    shapes = (
        jax.ShapeDtypeStruct((4, 32, 768), BF16),
        jax.ShapeDtypeStruct((4, 32, 768), BF16),
        jax.ShapeDtypeStruct((2048, 256), BF16),
        jax.ShapeDtypeStruct((768, 768), BF16),
        jax.ShapeDtypeStruct((192, 768), BF16),
        jax.ShapeDtypeStruct((16, 128), F32),
    )
    results = pl.pallas_call(
        kernel,
        out_shape=shapes,
        in_specs=[hbm if name.startswith("h_") or name == "pair" else vmem for name in INPUTS],
        out_specs=(vmem,) * 6,
        scratch_shapes=[pltpu.VMEM(*s) for s in SCRATCH.values()]
        + [pltpu.SemaphoreType.DMA((n,)) for n in SEMS.values()],
        compiler_params=pltpu.CompilerParams(
            collective_id=0, has_side_effects=True, vmem_limit_bytes=60 * 1024 * 1024
        ),
    )(*(args[name] for name in INPUTS))
    upd, tok, pg, ing, outg, proj = pl.pallas_call(
        copy_out,
        out_shape=shapes,
        in_specs=[hbm] * 6,
        out_specs=(hbm,) * 6,
        scratch_shapes=[pltpu.VMEM(s.shape, s.dtype) for s in shapes]
        + [pltpu.SemaphoreType.DMA((12,))],
    )(*results)
    return (
        upd.reshape(1, 128, 768),
        tok.reshape(1, 128, 768),
        jnp.swapaxes(pg.reshape(128, 16, 256), 1, 2),
        ing.reshape(4, 192, 768),
        outg,
        proj.T,
    )


def solution(mesh):
    torus = Mesh(
        mesh.devices.reshape(mesh.shape["samp"], 4, 2, 2, 2),
        ("samp", "row_0", "row_1", "col_0", "col_1"),
    )
    placed = (
        P("samp", ROW, None),
        P(ROW),
        P("samp"),
        P(ROW, COL, None),
        P(),
        P(),
        P(),
        P(),
        P(),
        P(),
        P(None, COL, None),
        P(COL, None),
        P(),
        P(),
        P("samp", ROW, None),
    )
    return jax.shard_map(
        on_device,
        mesh=torus,
        in_specs=placed,
        out_specs=(
            P("samp", ROW, None),
            P("samp", ROW, None),
            P(ROW, COL, "samp"),
            P(None, COL, None),
            P(COL, None),
            P(),
        ),
        check_vma=False,
    )
```

```python
import math

import jax
import jax.numpy as jnp
from jax import lax
from jax.experimental import pallas as pl
from jax.experimental.pallas import tpu as pltpu
from jax.sharding import Mesh
from jax.sharding import PartitionSpec as P

HEAD_DIM = 48
BLOCK = 32
STEPS = 200
COL = ("col_0", "col_1")
ROW = ("row_0", "row_1")
MESH = pl.DeviceIdType.MESH
F32, BF16 = jnp.float32, jnp.bfloat16
SCALE = 1.0 / math.sqrt(HEAD_DIM)
eps = 1e-05


def nn(a, b):
    return lax.dot_general(a, b, (((1,), (0,)), ((), ())), preferred_element_type=F32)


def nt(a, b):
    return lax.dot_general(a, b, (((1,), (1,)), ((), ())), preferred_element_type=F32)


def tn(a, b):
    return lax.dot_general(a, b, (((0,), (0,)), ((), ())), preferred_element_type=F32)


SCRATCH = dict(
    xbuf=((128, 256, 128), BF16),
    tokens=((128, 768), BF16),
    win=((768, 768), BF16),
    wout=((192, 768), BF16),
    base=((128, 768), F32),
    unit=((128, 768), F32),
    inv=((128, 1), F32),
    gate=((192, 128), F32),
    gmix=((192, 128), F32),
    waug=((80, 128), BF16),
    gh=((16, 1), F32),
    rst=((4, 16, 256), F32),
    amat=((2, 256, 256), BF16),
    emat=((256, 256), BF16),
    planes=((2, 2048, 128), F32),
    hat=((2048, 256), F32),
    invb=((2048, 256), F32),
    st=((128, 8, 256), F32),
    qg=((4, 2, 4, 48, 128), BF16),
    kvown=((2, 4, 48, 128), BF16),
    kv=((2, 4, 2, 4, 48, 128), BF16),
    nc=((8, 2, 128, 768), BF16),
    pr=((16, 128, 256), F32),
    dp=((16, 128, 256), F32),
    ot=((4, 4, 48, 128), BF16),
    oin=((4, 4, 48, 128), BF16),
    stats=((4, 48, 128), F32),
    acol=((128, 128), F32),
    arow=((4, 16, 128), F32),
    arow_own=((16, 128), F32),
    bgf=((2, 2048, 128), F32),
    bst=((2, 4, 2, 2, 128, 128), BF16),
    brv=((2, 4, 2, 2, 128, 128), BF16),
    pg=((2048, 256), BF16),
    win_out=((768, 768), BF16),
    wout_out=((192, 768), BF16),
    bgt=((2, 256, 128), F32),
    bga=((8, 2, 256, 128), BF16),
    dqt=((4, 4, 48, 128), BF16),
    dqin=((4, 4, 48, 128), BF16),
    dkv=((2, 4, 2, 4, 48, 128), BF16),
    xin=((4, 2, 4, 48, 128), BF16),
    sx=((4, 2, 4, 48, 128), BF16),
    yin=((4, 2, 4, 48, 128), BF16),
    fin=((2, 4, 48, 128), BF16),
    dkvown=((2, 4, 48, 128), BF16),
    att=((192, 128), F32),
    gin=((768, 128), BF16),
    gsh=((2, 8, 64, 128), BF16),
    zsh=((2, 8, 64, 128), BF16),
    po=((4, 32, 768), BF16),
    por=((4, 32, 768), BF16),
    upd=((4, 32, 768), BF16),
    gn=((4, 32, 768), BF16),
    gnr=((4, 32, 768), BF16),
    tok=((4, 32, 768), BF16),
    dws=((2, 8, 16, 384), BF16),
    dwr=((2, 8, 16, 384), BF16),
    dwall=((2, 4, 2, 8, 16, 384), BF16),
    pjz=((8, 16, 128), F32),
    pjr=((8, 16, 128), F32),
    pjc=((4, 16, 128), F32),
    pj1=((16, 128), F32),
    pj2=((16, 128), F32),
)
SEMS = dict(
    s_pair=8,
    s_in=4,
    s_send=260,
    s_qgx=1,
    s_qgc=2,
    s_kvp=1,
    s_xb=1,
    s_yo=4,
    s_yp=4,
    s_ncp=5,
    s_ncm=4,
    s_ncc=8,
    s_st=4,
    s_o=4,
    s_dq=4,
    s_xin=4,
    s_yin=4,
    s_fin=1,
    s_br=16,
    s_bg=16,
    s_out=12,
    s_po=4,
    s_upd=4,
    s_gn=4,
    s_tok=4,
    s_zi=16,
    s_dw=16,
    s_dz=16,
    s_ax=2,
    s_ay=8,
    s_by=8,
    s_bx=8,
    s_pz=8,
    s_pr=8,
    s_pc=4,
)
INPUTS = (
    "h_tokens", "h_cot", "h_win", "h_wout", "pair",
    "atom", "step", "bonds", "chirs", "table", "nrow", "gain", "pgain", "pw", "rw",
)
OUTPUTS = ("o_upd", "o_tok", "o_pg", "o_in", "o_out", "o_proj")


def wide_row(ref):
    return jnp.concatenate([ref[n : n + 1] for n in range(6)], axis=1)


def kernel(*refs):
    names = INPUTS + OUTPUTS + tuple(SCRATCH) + tuple(SEMS)
    r = dict(zip(names, refs, strict=True))

    class R:
        pass

    k = R()
    k.__dict__.update(r)
    z = lax.axis_index("samp")
    y = lax.axis_index("row_0")
    xl = lax.axis_index("row_1")
    xh = lax.axis_index("col_0")
    co = lax.axis_index("col_1")
    c = 2 * xh + co
    row = 2 * y + xl
    zof = [lax.rem(z + n, 8) for n in range(8)]
    zback = [lax.rem(z + 8 - n, 8) for n in range(8)]
    yof = [lax.rem(y + n, 4) for n in range(4)]
    x_other = {"row_1": 1 - xl}
    y_up = {"row_0": yof[1]}
    y_down = {"row_0": yof[3]}
    z_up = {"samp": zof[1]}
    z_down = {"samp": zof[7]}
    core_other = {"col_1": 1 - co}
    xh_other = {"col_0": 1 - xh}
    c_core = 2 * xh + (1 - co)
    c_xh = 2 * (1 - xh) + co
    cpeers = []
    for n in range(1, 4):
        ph, pc = lax.rem(xh + n // 2, 2), lax.rem(co + n % 2, 2)
        cpeers.append((n, {"col_0": ph, "col_1": pc}, 2 * ph + pc))
    rpeers = []
    for n in range(1, 8):
        py, px = lax.rem(y + n // 2, 4), lax.rem(xl + n % 2, 2)
        fy, fx = lax.rem(y + 4 - n // 2, 4), lax.rem(xl + n % 2, 2)
        rpeers.append((n, {"row_0": py, "row_1": px}, 2 * py + px, 2 * fy + fx))

    def when(cond, body):
        pl.when(cond)(body)

    loads = [
        pltpu.make_async_copy(k.h_tokens, k.tokens, k.s_in.at[0]),
        pltpu.make_async_copy(k.h_win, k.win, k.s_in.at[1]),
        pltpu.make_async_copy(k.h_cot, k.nc.at[z, 1], k.s_in.at[2]),
        pltpu.make_async_copy(k.h_wout, k.wout, k.s_in.at[3]),
    ]
    for copy in loads:
        copy.start()
    barrier = pltpu.get_barrier_semaphore()
    for n in range(1, 8):
        pl.semaphore_signal(barrier, inc=1, device_id={"samp": zof[n]}, device_id_type=MESH)
    for _, dev, _, _ in rpeers:
        pl.semaphore_signal(barrier, inc=1, device_id=dev, device_id_type=MESH)
    for _, dev, _ in cpeers:
        pl.semaphore_signal(barrier, inc=1, device_id=dev, device_id_type=MESH)
    swapped = {"row_0": c, "col_0": y // 2, "col_1": y % 2}

    @pl.when(c != y)
    def _():
        pl.semaphore_signal(barrier, inc=1, device_id=swapped, device_id_type=MESH)


    types = lax.broadcasted_iota(jnp.int32, (32, 128), 0) == k.atom[...]
    top_root = 160.0 ** (1.0 / 7.0)
    low_root = 0.0004 ** (1.0 / 7.0)
    root = top_root + k.step[...].astype(F32) / (STEPS - 1) * (low_root - top_root)
    level = 7.0 / 4.0 * jnp.log(root)
    add = tn(types.astype(F32).astype(BF16), k.table[...]) + level * wide_row(k.nrow)
    loads[0].wait()
    base = k.tokens[...].astype(F32) + add
    k.base[...] = base
    centered = base - jnp.mean(base, axis=1, keepdims=True)
    inv = lax.rsqrt(jnp.mean(centered * centered, axis=1, keepdims=True) + eps)
    unit = centered * inv
    k.inv[...] = inv
    k.unit[...] = unit
    normed = (unit * wide_row(k.gain)).astype(BF16)
    k.nc[z, 0] = normed
    loads[1].wait()
    loads[3].wait()
    loads[2].wait()
    pair_copies = []
    for n in range(8):
        part = pl.ds(16 * n, 16)
        copy = pltpu.make_async_copy(k.pair.at[part], k.xbuf.at[part], k.s_pair.at[n])
        copy.start()
        pair_copies.append(copy)
    proj_kv = nt(k.win[192:576], normed)
    for m in range(2):
        for hh in range(4):
            at = 192 * m + 48 * hh
            k.kvown[m, hh] = proj_kv[at : at + 48].astype(BF16)
    when(c == y, lambda: pl.semaphore_wait(barrier, 17))
    when(c != y, lambda: pl.semaphore_wait(barrier, 18))

    started = []
    count = [0]

    def make(src, dst, sem, dev):
        d = pltpu.make_async_remote_copy(
            src_ref=src,
            dst_ref=dst,
            send_sem=k.s_send.at[count[0]],
            recv_sem=sem,
            device_id=dev,
            device_id_type=MESH,
        )
        count[0] += 1
        return d

    def send(src, dst, sem, dev):
        d = make(src, dst, sem, dev)
        d.start()
        started.append((None, d))

    def arrived(dst, sem):
        pltpu.make_async_remote_copy(
            src_ref=dst,
            dst_ref=dst,
            send_sem=k.s_send.at[0],
            recv_sem=sem,
            device_id=z_up,
            device_id_type=MESH,
        ).wait_recv()

    give_kv = make(k.kvown, k.kv.at[xl, c], k.s_kvp.at[0], swapped)
    started.append((c != y, give_kv))

    def keep_kv():
        k.kv[xl, y] = k.kvown[...]

    when(c != y, lambda: give_kv.start())
    when(c == y, keep_kv)
    y1, y2, y3 = yof[1], yof[2], yof[3]

    def kv_row(side, sem):
        block = k.kv.at[side, y]
        send(block, block, sem.at[0], y_up)
        send(block, block, sem.at[1], y_down)

    def kv_row_relay(side, sem):
        arrived(k.kv.at[side, y3], sem.at[0])
        send(k.kv.at[side, y3, 0], k.kv.at[side, y3, 0], sem.at[2], y_up)
        arrived(k.kv.at[side, y1], sem.at[1])
        send(k.kv.at[side, y1, 1], k.kv.at[side, y1, 1], sem.at[3], y_down)

    proj_q = nt(k.win[0:192], normed)
    gate = jax.nn.sigmoid(nt(k.win[576:768], normed))
    gmix = nt(k.wout[...], k.nc[z, 1])
    k.gate[...] = gate
    k.gmix[...] = gmix
    grad_attend = gmix * gate
    for hh in range(4):
        k.qg[c, 0, hh] = proj_q[48 * hh : 48 * hh + 48].astype(BF16)
        k.qg[c, 1, hh] = grad_attend[48 * hh : 48 * hh + 48].astype(BF16)
    send(k.qg.at[c], k.qg.at[c], k.s_qgx.at[0], xh_other)
    send(k.qg.at[c], k.qg.at[c], k.s_qgc.at[0], core_other)
    half = pl.ds(64 * co, 64)
    send(k.nc.at[z, :, half], k.nc.at[z, :, half], k.s_ncp.at[1], z_up)
    send(k.nc.at[z, :, half], k.nc.at[z, :, half], k.s_ncm.at[1], z_down)

    weights = k.pw[...] * k.pgain[...]
    w_hi = weights.astype(BF16)
    rest = weights - w_hi.astype(F32)
    w_mid = rest.astype(BF16)
    w_lo = (rest - w_mid.astype(F32)).astype(BF16)
    sub16 = lax.broadcasted_iota(jnp.int32, (16, 128), 0)
    lane16 = lax.broadcasted_iota(jnp.int32, (16, 128), 1)
    pick = (lane16 == 16 * z + sub16).astype(F32).astype(BF16)
    k.waug[0:16] = w_hi
    k.waug[16:32] = w_mid
    k.waug[32:48] = w_lo
    k.waug[48:64] = pick
    k.waug[64:80] = jnp.ones((16, 128), BF16)
    k.gh[...] = jnp.sum(weights, axis=1, keepdims=True)
    spread = weights - jnp.mean(weights, axis=1, keepdims=True)
    s_hi = spread.astype(BF16)
    s_lo = (spread - s_hi.astype(F32)).astype(BF16)
    sub256 = lax.broadcasted_iota(jnp.int32, (256, 256), 0)
    lane256 = lax.broadcasted_iota(jnp.int32, (256, 256), 1)
    same = (sub256 // 16) == (lane256 // 16)
    tall = (
        lax.broadcasted_iota(jnp.int32, (256, 16), 0) % 16 == lax.broadcasted_iota(jnp.int32, (256, 16), 1)
    ).astype(F32).astype(BF16)
    for n, part in enumerate((s_hi, s_lo)):
        small = nt(pick, part).astype(BF16)
        wide = nt(nn(tall, small).astype(BF16), tall)
        k.amat[n] = jnp.where(same, wide, 0.0).astype(BF16)
    k.emat[...] = jnp.where(same, 1.0 / 128.0, 0.0).astype(BF16)
    eye = lax.broadcasted_iota(jnp.int32, (16, 16), 0) == lax.broadcasted_iota(jnp.int32, (16, 16), 1)

    def block_counts(ref, total):
        first = (lax.broadcasted_iota(jnp.int32, (16, total), 0) + 4 * row) == ref[0:1]
        second = lax.broadcasted_iota(jnp.int32, (256, total), 0) // BLOCK + 8 * c == ref[1:2]
        return nt(first.astype(F32).astype(BF16), second.astype(F32).astype(BF16))

    bond = block_counts(k.bonds, 64)
    chir = block_counts(k.chirs, 32)
    w_bond = jnp.sum(jnp.where(eye, k.rw[0:1], 0.0), axis=1, keepdims=True)
    w_chir = jnp.sum(jnp.where(eye, k.rw[1:2], 0.0), axis=1, keepdims=True)
    for n in range(4):
        k.rst[n] = w_bond * bond[n : n + 1] + w_chir * chir[n : n + 1]

    ones = jnp.ones((8, 128), BF16)

    def pair_rows(n):
        pair_copies[n].wait()

        def body(i, carry):
            x = k.xbuf[i]
            res = nt(k.waug[...], x)
            xf = x.astype(F32)
            sq = xf * xf
            hi = sq.astype(BF16)
            lo = (sq - hi.astype(F32)).astype(BF16)
            ss = nt(ones, hi) + nt(ones, lo)
            mean = res[64:65] * (1.0 / 128.0)
            var = ss[0:1] * (1.0 / 128.0) - mean * mean
            inv = lax.rsqrt(jnp.maximum(var, 0.0) + eps)
            bias = res[0:16] + res[16:32] + res[32:48]
            bias = inv * (bias - mean * k.gh[...])
            rows = pl.ds(pl.multiple_of(i * 16, 16), 16)
            k.planes[0, rows, :] = bias[:, :128]
            k.planes[1, rows, :] = bias[:, 128:]
            k.hat[rows, :] = (res[48:64] - mean) * (inv * inv)
            k.invb[rows, :] = jnp.broadcast_to(inv, (16, 256))
            k.st[i, 0:1] = inv
            k.st[i, 1:2] = mean * inv
            return carry

        lax.fori_loop(16 * n, 16 * n + 16, body, 0, unroll=4)

    def nc_relay(n):
        src = k.nc.at[zback[n], :, half]
        arrived(src, k.s_ncp.at[n])
        if n < 4:
            send(src, src, k.s_ncp.at[n + 1], z_up)
        send(src, src, k.s_ncc.at[n], core_other)
        if n < 4:
            src = k.nc.at[zof[n], :, half]
            arrived(src, k.s_ncm.at[n])
            if n < 3:
                send(src, src, k.s_ncm.at[n + 1], z_down)
            send(src, src, k.s_ncc.at[8 - n], core_other)

    pair_rows(0)
    pair_rows(1)
    when(c != y, lambda: arrived(k.kv.at[xl, y], k.s_kvp.at[0]))
    send(k.kv.at[xl, y], k.kv.at[xl, y], k.s_xb.at[0], x_other)
    kv_row(xl, k.s_yo)
    pair_rows(2)
    arrived(k.qg.at[c_xh], k.s_qgx.at[0])
    send(k.qg.at[c_xh], k.qg.at[c_xh], k.s_qgc.at[1], core_other)
    pair_rows(3)
    arrived(k.kv.at[1 - xl, y], k.s_xb.at[0])
    kv_row(1 - xl, k.s_yp)
    kv_row_relay(xl, k.s_yo)
    pair_rows(4)
    pair_rows(5)
    nc_relay(1)
    kv_row_relay(1 - xl, k.s_yp)
    pair_rows(6)
    pair_rows(7)
    for side, sem in ((xl, k.s_yo), (1 - xl, k.s_yp)):
        arrived(k.kv.at[side, y2, 0], sem.at[2])
        arrived(k.kv.at[side, y2, 1], sem.at[3])
    arrived(k.qg.at[c_core], k.s_qgc.at[0])
    arrived(k.qg.at[2 * (1 - xh) + 1 - co], k.s_qgc.at[1])

    lane = lax.broadcasted_iota(jnp.int32, (128, 128), 1)

    def head_kv(g, m, hh):
        return jnp.concatenate([k.kv[0, g, m, hh], k.kv[1, g, m, hh]], axis=1)

    def forward(h, packed):
        g, hh = h // 4, h % 4
        keys = head_kv(g, 0, hh)
        vals = head_kv(g, 1, hh)
        by_head = pl.ds(h, 128, stride=16)
        bias = jnp.concatenate([k.planes[0, by_head, :], k.planes[1, by_head, :]], axis=1)
        extra = [jnp.broadcast_to(k.rst[n, pl.ds(h, 1), :], (32, 256)) for n in range(4)]
        s = tn(k.qg[g, 0, hh], keys) * SCALE + (bias + jnp.concatenate(extra, axis=0))
        top = jnp.max(s, axis=1, keepdims=True)
        p = jnp.exp(s - top)
        dp = tn(k.qg[g, 1, hh], vals)
        k.pr[h] = p
        k.dp[h] = dp
        k.ot[g, hh] = nt(vals, p.astype(BF16)).astype(BF16)
        total = jnp.sum(p, axis=1, keepdims=True)
        dots = jnp.sum(p * dp, axis=1, keepdims=True)
        packed = jnp.where(lane == h, top, packed)
        packed = jnp.where(lane == 16 + h, total, packed)
        return jnp.where(lane == 32 + h, dots, packed)

    packed = lax.fori_loop(0, 16, forward, jnp.zeros((128, 128), F32), unroll=2)
    k.stats[c] = packed.T[0:48]
    for n, dev, _ in cpeers:
        send(k.stats.at[c], k.stats.at[c], k.s_st.at[n], dev)
    for n, dev, who in cpeers:
        send(k.ot.at[who], k.oin.at[c], k.s_o.at[n], dev)
    k.oin[c] = k.ot[c]
    nc_relay(2)
    for n, _, who in cpeers:
        arrived(k.stats.at[who], k.s_st.at[n])
    top = k.stats[0, 0:16]
    for n in range(1, 4):
        top = jnp.maximum(top, k.stats[n, 0:16])
    total = jnp.zeros((16, 128), F32)
    dots = jnp.zeros((16, 128), F32)
    for n in range(4):
        w = jnp.exp(k.stats[n, 0:16] - top)
        k.arow[n] = w
        total += w * k.stats[n, 16:32]
        dots += w * k.stats[n, 32:48]
    inv_total = 1.0 / total
    for n in range(4):
        k.arow[n] = k.arow[n] * inv_total
    own = k.arow[c]
    k.arow_own[...] = own
    k.acol[...] = jnp.concatenate([own, dots * inv_total, jnp.zeros((96, 128), F32)], axis=0).T

    def backward(h, carry):
        g, hh = h // 4, h % 4
        columns = k.acol[...]
        alpha = jnp.sum(jnp.where(lane == h, columns, 0.0), axis=1, keepdims=True)
        delta = jnp.sum(jnp.where(lane == 16 + h, columns, 0.0), axis=1, keepdims=True)
        p = k.pr[h]
        ds = p * alpha * (k.dp[h] - delta)
        by_head = pl.ds(h, 128, stride=16)
        k.bgf[0, by_head, :] = ds[:, :128]
        k.bgf[1, by_head, :] = ds[:, 128:]
        low = ds.astype(BF16)
        k.dqt[g, hh] = (nt(head_kv(g, 0, hh), low) * SCALE).astype(BF16)
        dk = (nn(k.qg[g, 0, hh], low) * SCALE).astype(BF16)
        k.dkv[0, g, 0, hh] = dk[:, :128]
        k.dkv[1, g, 0, hh] = dk[:, 128:]
        ga = (k.qg[g, 1, hh].astype(F32) * k.arow_own[pl.ds(h, 1), :]).astype(BF16)
        dv = nn(ga, p.astype(BF16)).astype(BF16)
        k.dkv[0, g, 1, hh] = dv[:, :128]
        k.dkv[1, g, 1, hh] = dv[:, 128:]
        return carry

    def key_value_out(n):
        lax.fori_loop(4 * n, 4 * n + 4, backward, 0, unroll=2)
        send(k.dkv.at[1 - xl, n], k.xin.at[n], k.s_xin.at[n], x_other)
        d = make(
            k.dqt.at[n],
            k.dqin.at[c],
            k.s_dq.at[2 * lax.rem(xh + n // 2, 2) + lax.rem(co + n % 2, 2)],
            {"col_0": n // 2, "col_1": n % 2},
        )
        started.append((c != n, d))
        when(c != n, lambda: d.start())

    key_value_out(0)
    key_value_out(1)
    nc_relay(3)

    for n, _, who in cpeers:
        arrived(k.oin.at[who], k.s_o.at[n])
    for hh in range(4):
        att = jnp.zeros((48, 128), F32)
        for n in range(4):
            w = k.arow[n, pl.ds(4 * c + hh, 1), :]
            att += k.oin[n, hh].astype(F32) * w
        k.att[48 * hh : 48 * hh + 48] = att
    gate = k.gate[...]
    att = k.att[...]
    mixed = (gate * att).astype(BF16)
    grad_gate = (k.gmix[...] * att * gate * (1.0 - gate)).astype(BF16)
    k.gin[576:768] = grad_gate
    for n in range(4):
        k.gsh[0, 4 + n, 0:48] = grad_gate[48 * n : 48 * n + 48]
    for n in range(8):
        for m in range(2):
            at = 32 * n + 16 * m
            k.gsh[m, n, 48:64] = mixed[at : at + 16] if n < 6 else jnp.zeros((16, 128), BF16)
    part_out = tn(mixed, k.wout[...]).astype(BF16)
    for n in range(4):
        k.po[n] = part_out[32 * n : 32 * n + 32]
    for n, dev, who in cpeers:
        send(k.po.at[who], k.por.at[c], k.s_po.at[n], dev)
    k.por[c] = k.po[c]

    key_value_out(2)
    key_value_out(3)
    k.dqin[c] = k.dqt[c]

    def ring_step(n):
        for way, owner, dev in ((0, zof[4 - n], z_up), (1, zback[4 - n], z_down)):
            for part in range(2):
                if n == 0 and part != way:
                    continue
                rows = pl.ds(pl.multiple_of(owner * 256 + 128 * part, 128), 128)
                value = k.bgf[:, rows, :]
                if n > 1 or (n == 1 and part == way):
                    arrived(k.brv.at[way, n - 1, part], k.s_br.at[8 * way + 2 * (n - 1) + part])
                    value = value + k.brv[way, n - 1, part].astype(F32)
                k.bst[way, n, part] = value.astype(BF16)
                send(k.bst.at[way, n, part], k.brv.at[way, n, part], k.s_br.at[8 * way + 2 * n + part], dev)

    def bg_finish():
        for part in range(2):
            rows = pl.ds(pl.multiple_of(z * 256 + 128 * part, 128), 128)
            value = k.bgf[:, rows, :]
            for way in range(2):
                arrived(k.brv.at[way, 3, part], k.s_br.at[8 * way + 6 + part])
                value = value + k.brv[way, 3, part].astype(F32)
            k.bgt[:, 128 * part : 128 * part + 128] = value
            k.bga[z, :, 128 * part : 128 * part + 128] = value.astype(BF16)
        for part in range(2):
            mine_bg = k.bga.at[z, :, pl.ds(128 * part, 128)]
            send(mine_bg, mine_bg, k.s_bg.at[part], z_up)
            send(mine_bg, mine_bg, k.s_bg.at[8 + part], z_down)

    def bg_relay(n):
        for part in range(2):
            half_rows = pl.ds(128 * part, 128)
            for way, owner, dev in ((0, zback[n], z_up), (1, zof[n], z_down)):
                if n == 4 and part != way:
                    continue
                block = k.bga.at[owner, :, half_rows]
                arrived(block, k.s_bg.at[8 * way + 2 * (n - 1) + part])
                if n < 3 or (n == 3 and part == way):
                    send(block, block, k.s_bg.at[8 * way + 2 * n + part], dev)

    ring_step(0)

    def share(b):
        for n in range(1, 8):
            send(k.gsh.at[b, zof[n]], k.zsh.at[b, z], k.s_zi.at[8 * b + n], {"samp": zof[n]})
        k.zsh[b, z] = k.gsh[b, z]

    def weight_rows(b):
        for n in range(1, 8):
            arrived(k.zsh.at[b, zback[n]], k.s_zi.at[8 * b + n])
        acc = nn(k.zsh[b, 0, 0:48], k.nc[0, 0])
        acc_out = nn(k.zsh[b, 0, 48:64], k.nc[0, 1])
        for n in range(1, 8):
            acc += nn(k.zsh[b, n, 0:48], k.nc[n, 0])
            acc_out += nn(k.zsh[b, n, 48:64], k.nc[n, 1])
        for n in range(4):
            tall = (acc[16 * n : 16 * n + 16] if n < 3 else acc_out).astype(BF16)
            k.dws[b, 2 * n] = tall[:, :384]
            k.dws[b, 2 * n + 1] = tall[:, 384:]
        for n, dev, to, _ in rpeers:
            send(k.dws.at[b, to], k.dwr.at[b, row], k.s_dw.at[8 * b + n], dev)
        k.dwr[b, row] = k.dws[b, row]

    def weight_sum(b):
        for n, _, _, came in rpeers:
            arrived(k.dwr.at[b, came], k.s_dw.at[8 * b + n])
        total = k.dwr[b, 0].astype(F32)
        for n in range(1, 8):
            total += k.dwr[b, n].astype(F32)
        k.dwall[b, y, xl, z] = total.astype(BF16)
        for n in range(1, 8):
            here = k.dwall.at[b, y, xl, z]
            send(here, here, k.s_dz.at[8 * b + n], {"samp": zof[n]})

    low_z, high_z = pl.ds(0, 4), pl.ds(4, 4)

    def same_place(ref, sem, dev):
        send(ref, ref, sem, dev)

    def spread_1(b):
        w, ay, by, bx = k.dwall.at[b], 4 * b, 4 * b, 4 * b
        for n in range(1, 8):
            arrived(w.at[y, xl, zback[n]], k.s_dz.at[8 * b + n])
        same_place(w.at[y, xl, low_z], k.s_ax.at[b], x_other)
        same_place(w.at[y, xl, high_z], k.s_by.at[by], y_up)
        same_place(w.at[y, xl, high_z], k.s_by.at[by + 1], y_down)
        same_place(w.at[y, xl, high_z], k.s_bx.at[bx], x_other)

    def spread_2(b):
        w, ay, by, bx = k.dwall.at[b], 4 * b, 4 * b, 4 * b
        arrived(w.at[y, 1 - xl, low_z], k.s_ax.at[b])
        same_place(w.at[y, :, low_z], k.s_ay.at[ay], y_up)
        same_place(w.at[y, :, low_z], k.s_ay.at[ay + 1], y_down)
        arrived(w.at[y3, xl, high_z], k.s_by.at[by])
        same_place(w.at[y3, xl, pl.ds(4, 2)], k.s_by.at[by + 2], y_up)
        same_place(w.at[y3, xl, high_z], k.s_bx.at[bx + 1], x_other)
        arrived(w.at[y1, xl, high_z], k.s_by.at[by + 1])
        same_place(w.at[y1, xl, pl.ds(6, 2)], k.s_by.at[by + 3], y_down)
        same_place(w.at[y1, xl, high_z], k.s_bx.at[bx + 2], x_other)

    def spread_3(b):
        w, ay, by, bx = k.dwall.at[b], 4 * b, 4 * b, 4 * b
        arrived(w.at[y3, :, low_z], k.s_ay.at[ay])
        same_place(w.at[y3, 0, low_z], k.s_ay.at[ay + 2], y_up)
        arrived(w.at[y1, :, low_z], k.s_ay.at[ay + 1])
        same_place(w.at[y1, 1, low_z], k.s_ay.at[ay + 3], y_down)
        arrived(w.at[y2, xl, pl.ds(4, 2)], k.s_by.at[by + 2])
        arrived(w.at[y2, xl, pl.ds(6, 2)], k.s_by.at[by + 3])
        same_place(w.at[y2, xl, high_z], k.s_bx.at[bx + 3], x_other)

    def spread_4(b):
        w, ay, by, bx = k.dwall.at[b], 4 * b, 4 * b, 4 * b
        arrived(w.at[y, 1 - xl, high_z], k.s_bx.at[bx])
        arrived(w.at[y3, 1 - xl, high_z], k.s_bx.at[bx + 1])
        arrived(w.at[y1, 1 - xl, high_z], k.s_bx.at[bx + 2])
        arrived(w.at[y2, 1 - xl, high_z], k.s_bx.at[bx + 3])
        arrived(w.at[y2, 0, low_z], k.s_ay.at[ay + 2])
        arrived(w.at[y2, 1, low_z], k.s_ay.at[ay + 3])

    def plus(dst, piece, a, b):
        dst[piece] = (a.astype(F32) + b.astype(F32)).astype(BF16)

    def first_sum(n):
        arrived(k.xin.at[n], k.s_xin.at[n])
        plus(k.sx, n, k.dkv[xl, n], k.xin[n])
        d = make(k.sx.at[n], k.yin.at[y], k.s_yin.at[lax.rem(n + 4 - y, 4)], {"row_0": n})
        started.append((y != n, d))
        when(y != n, lambda: d.start())

    give_back = make(k.fin, k.dkvown, k.s_fin.at[0], swapped)
    started.append((c != y, give_back))

    def last_sum():
        total = k.sx[y].astype(F32)
        for n in range(1, 4):
            arrived(k.yin.at[yof[4 - n]], k.s_yin.at[n])
            total += k.yin[yof[4 - n]].astype(F32)
        total = total.astype(BF16)
        k.fin[...] = total

        def keep():
            k.dkvown[...] = k.fin[...]

        when(c == y, keep)
        when(c != y, lambda: give_back.start())

    outs = []

    def give_out(src, dst):
        copy = pltpu.make_async_copy(src, dst, k.s_out.at[len(outs)])
        copy.start()
        outs.append(copy)

    def pair_back(owner):
        bg = jnp.concatenate([k.bga[owner, 0], k.bga[owner, 1]], axis=1)
        rows = pl.ds(pl.multiple_of(owner * 256, 256), 256)
        plane = jnp.concatenate([k.planes[0, rows, :], k.planes[1, rows, :]], axis=1)
        product = bg.astype(F32) * plane
        hi = product.astype(BF16)
        lo = (product - hi.astype(F32)).astype(BF16)
        both = nn(k.emat[...], hi) + nn(k.emat[...], lo)
        out = nn(k.amat[0], bg) + nn(k.amat[1], bg)
        k.pg[rows, :] = (k.invb[rows, :] * out - k.hat[rows, :] * both).astype(BF16)
        give_out(k.pg.at[rows], k.o_pg.at[rows])

    def project_pairs(n, carry):
        acc, low = carry
        part = pl.ds(pl.multiple_of(n * 16, 16), 16)
        bg = jnp.concatenate([k.bgt[0, part, :], k.bgt[1, part, :]], axis=1)
        i = 16 * z + n
        scaled = bg * k.st[i, 0:1]
        hi = scaled.astype(BF16)
        rest = (scaled - hi.astype(F32)).astype(BF16)
        acc = acc + nn(jnp.concatenate([hi, rest], axis=0), k.xbuf[i])
        low = low + jnp.sum(bg * k.st[i, 1:2], axis=1, keepdims=True)
        return (acc, low)

    first_sum(0)
    first_sum(1)
    for n, _, who in cpeers:
        arrived(k.dqin.at[who], k.s_dq.at[n])
    for hh in range(4):
        dq = k.dqin[0, hh].astype(F32)
        for n in range(1, 4):
            dq += k.dqin[n, hh].astype(F32)
        k.gin[48 * hh : 48 * hh + 48] = dq.astype(BF16)
        k.gsh[0, hh, 0:48] = dq.astype(BF16)
    share(0)
    ring_step(1)
    first_sum(2)
    first_sum(3)
    nc_relay(4)
    ring_step(2)
    last_sum()
    for n in range(1, 8):
        arrived(k.nc.at[zback[n], :, pl.ds(64 * (1 - co), 64)], k.s_ncc.at[n])
    weight_rows(0)
    when(c != y, lambda: arrived(k.dkvown, k.s_fin.at[0]))
    for hh in range(4):
        k.gin[192 + 48 * hh : 240 + 48 * hh] = k.dkvown[0, hh]
        k.gin[384 + 48 * hh : 432 + 48 * hh] = k.dkvown[1, hh]
        k.gsh[1, hh, 0:48] = k.dkvown[0, hh]
        k.gsh[1, 4 + hh, 0:48] = k.dkvown[1, hh]
    share(1)
    ring_step(3)
    weight_sum(0)
    part_normed = tn(k.gin[...], k.win[...]).astype(BF16)
    for n in range(4):
        k.gn[n] = part_normed[32 * n : 32 * n + 32]
    for n, dev, who in cpeers:
        send(k.gn.at[who], k.gnr.at[c], k.s_gn.at[n], dev)
    k.gnr[c] = k.gn[c]
    bg_finish()
    weight_rows(1)
    spread_1(0)
    acc, low = lax.fori_loop(
        0, 16, project_pairs, (jnp.zeros((32, 128), F32), jnp.zeros((16, 1), F32)), unroll=2
    )
    k.pj1[...] = k.pgain[...] * (acc[0:16] + acc[16:32] - low)
    for n in range(1, 8):
        send(k.pj1, k.pjz.at[z], k.s_pz.at[n], {"samp": zof[n]})
    k.pjz[z] = k.pj1[...]

    for n, _, who in cpeers:
        arrived(k.por.at[who], k.s_po.at[n])
    mine = pl.ds(pl.multiple_of(32 * c, 32), 32)
    total = k.base[mine]
    for n in range(4):
        total = total + k.por[n].astype(F32)
    k.upd[c] = total.astype(BF16)
    for n, dev, _ in cpeers:
        send(k.upd.at[c], k.upd.at[c], k.s_upd.at[n], dev)
    weight_sum(1)
    bg_relay(1)
    spread_2(0)
    for n, _, who in cpeers:
        arrived(k.gnr.at[who], k.s_gn.at[n])
    total = k.gnr[0].astype(F32)
    for n in range(1, 4):
        total += k.gnr[n].astype(F32)
    scaled = total * wide_row(k.gain)
    hat = k.unit[mine]
    back = k.inv[mine] * (
        scaled
        - jnp.mean(scaled, axis=1, keepdims=True)
        - hat * jnp.mean(scaled * hat, axis=1, keepdims=True)
    )
    k.tok[c] = (k.nc[z, 1, mine].astype(F32) + back).astype(BF16)
    for n, dev, _ in cpeers:
        send(k.tok.at[c], k.tok.at[c], k.s_tok.at[n], dev)

    pair_back(z)
    bg_relay(2)
    spread_1(1)
    for n in range(1, 8):
        arrived(k.pjz.at[zback[n]], k.s_pz.at[n])
    total = k.pjz[0]
    for n in range(1, 8):
        total += k.pjz[n]
    k.pj2[...] = total
    for n, dev, _, _ in rpeers:
        send(k.pj2, k.pjr.at[row], k.s_pr.at[n], dev)
    k.pjr[row] = total
    spread_3(0)
    pair_back(zof[1])
    pair_back(zback[1])
    spread_2(1)
    bg_relay(3)
    for n, _, _, came in rpeers:
        arrived(k.pjr.at[came], k.s_pr.at[n])
    total = k.pjr[0]
    for n in range(1, 8):
        total += k.pjr[n]
    k.pjc[c] = total
    for n, dev, _ in cpeers:
        send(k.pjc.at[c], k.pjc.at[c], k.s_pc.at[n], dev)
    pair_back(zof[2])
    spread_3(1)
    pair_back(zback[2])
    bg_relay(4)
    pair_back(zof[3])
    pair_back(zback[3])
    pair_back(zof[4])
    spread_4(0)
    for n, _, who in cpeers:
        arrived(k.upd.at[who], k.s_upd.at[n])
        arrived(k.tok.at[who], k.s_tok.at[n])
        arrived(k.pjc.at[who], k.s_pc.at[n])
    give_out(k.upd, k.o_upd)
    give_out(k.tok, k.o_tok)
    k.o_proj[...] = k.pjc[0] + k.pjc[1] + k.pjc[2] + k.pjc[3]

    def weight_out(b):
        for half_of in range(2):
            lanes = slice(384 * half_of, 384 * half_of + 384)
            for n in range(8):
                member = ((0, 3), (1, 2))[b][n // 4]
                for m in range(3):
                    at = 192 * member + 48 * (n % 4) + 16 * m
                    k.win_out[at : at + 16, lanes] = k.dwall[b, m, half_of, n]
                if n < 6:
                    at = 32 * n + 16 * b
                    k.wout_out[at : at + 16, lanes] = k.dwall[b, 3, half_of, n]

    weight_out(0)
    spread_4(1)
    weight_out(1)
    give_out(k.win_out, k.o_in)
    give_out(k.wout_out, k.o_out)
    for copy in outs:
        copy.wait()
    for cond, d in started:
        if cond is None:
            d.wait_send()
        else:
            when(cond, lambda d=d: d.wait_send())


def copy_out(*refs):
    n = len(OUTPUTS)
    src, dst, buf, sems = refs[:n], refs[n : 2 * n], refs[2 * n : 3 * n], refs[3 * n]
    come = [pltpu.make_async_copy(src[m], buf[m], sems.at[m]) for m in range(n)]
    go = [pltpu.make_async_copy(buf[m], dst[m], sems.at[n + m]) for m in range(n)]
    for d in come:
        d.start()
    for d, e in zip(come, go):
        d.wait()
        e.start()
    for e in go:
        e.wait()


def on_device(
    tokens,
    atom_type,
    noise_step,
    pair_rep,
    bond_blocks,
    chiral_blocks,
    type_table,
    noise_row,
    norm_gain,
    pair_gain,
    in_weight,
    out_weight,
    pair_weight,
    restraint_weight,
    cotangent,
):
    args = dict(
        h_tokens=tokens[0],
        h_cot=cotangent[0],
        h_win=in_weight.reshape(768, 768),
        h_wout=out_weight,
        pair=pair_rep,
        atom=atom_type[None, :],
        step=noise_step[None, :],
        bonds=bond_blocks.T,
        chirs=chiral_blocks.T,
        table=type_table,
        nrow=noise_row.reshape(6, 128),
        gain=norm_gain.reshape(6, 128),
        pgain=pair_gain[None, :],
        pw=pair_weight.T,
        rw=restraint_weight,
    )
    vmem = pl.BlockSpec(memory_space=pltpu.VMEM)
    hbm = pl.BlockSpec(memory_space=pl.ANY)
    shapes = (
        jax.ShapeDtypeStruct((4, 32, 768), BF16),
        jax.ShapeDtypeStruct((4, 32, 768), BF16),
        jax.ShapeDtypeStruct((2048, 256), BF16),
        jax.ShapeDtypeStruct((768, 768), BF16),
        jax.ShapeDtypeStruct((192, 768), BF16),
        jax.ShapeDtypeStruct((16, 128), F32),
    )
    results = pl.pallas_call(
        kernel,
        out_shape=shapes,
        in_specs=[hbm if name.startswith("h_") or name == "pair" else vmem for name in INPUTS],
        out_specs=(hbm,) * 5 + (vmem,),
        scratch_shapes=[pltpu.VMEM(*s) for s in SCRATCH.values()]
        + [pltpu.SemaphoreType.DMA((n,)) for n in SEMS.values()],
        compiler_params=pltpu.CompilerParams(
            collective_id=0, has_side_effects=True, vmem_limit_bytes=60 * 1024 * 1024
        ),
    )(*(args[name] for name in INPUTS))
    upd, tok, pg, ing, outg, proj = pl.pallas_call(
        copy_out,
        out_shape=shapes,
        in_specs=[hbm] * 6,
        out_specs=(hbm,) * 6,
        scratch_shapes=[pltpu.VMEM(s.shape, s.dtype) for s in shapes]
        + [pltpu.SemaphoreType.DMA((12,))],
    )(*results)
    return (
        upd.reshape(1, 128, 768),
        tok.reshape(1, 128, 768),
        jnp.swapaxes(pg.reshape(128, 16, 256), 1, 2),
        ing.reshape(4, 192, 768),
        outg,
        proj.T,
    )


def solution(mesh):
    torus = Mesh(
        mesh.devices.reshape(mesh.shape["samp"], 4, 2, 2, 2),
        ("samp", "row_0", "row_1", "col_0", "col_1"),
    )
    placed = (
        P("samp", ROW, None),
        P(ROW),
        P("samp"),
        P(ROW, COL, None),
        P(),
        P(),
        P(),
        P(),
        P(),
        P(),
        P(None, COL, None),
        P(COL, None),
        P(),
        P(),
        P("samp", ROW, None),
    )
    return jax.shard_map(
        on_device,
        mesh=torus,
        in_specs=placed,
        out_specs=(
            P("samp", ROW, None),
            P("samp", ROW, None),
            P(ROW, COL, "samp"),
            P(None, COL, None),
            P(COL, None),
            P(),
        ),
        check_vma=False,
    )
```

```python
import math

import jax
import jax.numpy as jnp
from jax import lax
from jax.experimental import pallas as pl
from jax.experimental.pallas import tpu as pltpu
from jax.sharding import Mesh
from jax.sharding import PartitionSpec as P

HEAD_DIM = 48
BLOCK = 32
STEPS = 200
COL = ("col_0", "col_1")
ROW = ("row_0", "row_1")
MESH = pl.DeviceIdType.MESH
F32, BF16 = jnp.float32, jnp.bfloat16
SCALE = 1.0 / math.sqrt(HEAD_DIM)
eps = 1e-05


def nn(a, b):
    return lax.dot_general(a, b, (((1,), (0,)), ((), ())), preferred_element_type=F32)


def nt(a, b):
    return lax.dot_general(a, b, (((1,), (1,)), ((), ())), preferred_element_type=F32)


def tn(a, b):
    return lax.dot_general(a, b, (((0,), (0,)), ((), ())), preferred_element_type=F32)


SCRATCH = dict(
    xbuf=((128, 256, 128), BF16),
    tokens=((128, 768), BF16),
    win=((768, 768), BF16),
    wout=((192, 768), BF16),
    base=((128, 768), F32),
    unit=((128, 768), F32),
    inv=((128, 1), F32),
    gate=((192, 128), F32),
    gmix=((192, 128), F32),
    waug=((80, 128), BF16),
    gh=((16, 1), F32),
    rst=((4, 16, 256), F32),
    amat=((2, 256, 256), BF16),
    emat=((256, 256), BF16),
    planes=((2, 2048, 128), F32),
    hat=((2048, 256), F32),
    invb=((2048, 256), F32),
    st=((128, 8, 256), F32),
    qg=((4, 2, 4, 48, 128), BF16),
    kvown=((2, 4, 48, 128), BF16),
    kv=((2, 4, 2, 4, 48, 128), BF16),
    nc=((8, 2, 128, 768), BF16),
    pr=((16, 128, 256), F32),
    dp=((16, 128, 256), F32),
    ot=((4, 4, 48, 128), BF16),
    oin=((4, 4, 48, 128), BF16),
    stats=((2, 4, 24, 128), F32),
    acol=((2, 128, 128), F32),
    arow=((4, 16, 128), F32),
    arow_own=((16, 128), F32),
    bgf=((2, 2048, 128), F32),
    bst=((2, 4, 2, 2, 128, 128), BF16),
    brv=((2, 4, 2, 2, 128, 128), BF16),
    pg=((2048, 256), BF16),
    win_out=((768, 768), BF16),
    wout_out=((192, 768), BF16),
    bgt=((2, 256, 128), F32),
    bga=((8, 2, 256, 128), BF16),
    dqt=((4, 4, 48, 128), BF16),
    dqin=((4, 4, 48, 128), BF16),
    dkv=((2, 4, 2, 4, 48, 128), BF16),
    xin=((4, 2, 4, 48, 128), BF16),
    sx=((4, 2, 4, 48, 128), BF16),
    yin=((4, 2, 4, 48, 128), BF16),
    fin=((2, 4, 48, 128), BF16),
    dkvown=((2, 4, 48, 128), BF16),
    att=((192, 128), F32),
    gin=((768, 128), BF16),
    gsh=((2, 8, 64, 128), BF16),
    zsh=((2, 8, 64, 128), BF16),
    po=((4, 32, 768), BF16),
    por=((4, 32, 768), BF16),
    upd=((4, 32, 768), BF16),
    gn=((4, 32, 768), BF16),
    gnr=((4, 32, 768), BF16),
    tok=((4, 32, 768), BF16),
    dws=((2, 8, 16, 384), BF16),
    dwr=((2, 8, 16, 384), BF16),
    dwall=((2, 4, 2, 8, 16, 384), BF16),
    pjz=((8, 16, 128), F32),
    pjr=((8, 16, 128), F32),
    pjc=((4, 16, 128), F32),
    pj1=((16, 128), F32),
    pj2=((16, 128), F32),
)
SEMS = dict(
    s_pair=8,
    s_in=4,
    s_send=260,
    s_qgx=1,
    s_qgc=2,
    s_kvp=1,
    s_xb=1,
    s_yo=4,
    s_yp=4,
    s_ncp=5,
    s_ncm=4,
    s_ncc=8,
    s_st=8,
    s_o=4,
    s_dq=4,
    s_xin=4,
    s_yin=4,
    s_fin=1,
    s_br=16,
    s_bg=16,
    s_out=16,
    s_po=4,
    s_upd=4,
    s_gn=4,
    s_tok=4,
    s_zi=16,
    s_dw=16,
    s_dz=16,
    s_ax=2,
    s_ay=8,
    s_by=8,
    s_bx=8,
    s_pz=8,
    s_pr=8,
    s_pc=4,
)
INPUTS = (
    "h_tokens", "h_cot", "h_win", "h_wout", "pair",
    "atom", "step", "bonds", "chirs", "table", "nrow", "gain", "pgain", "pw", "rw",
)
OUTPUTS = ("o_upd", "o_tok", "o_pg", "o_in", "o_out", "o_proj")


def wide_row(ref):
    return jnp.concatenate([ref[n : n + 1] for n in range(6)], axis=1)


def kernel(*refs):
    names = INPUTS + OUTPUTS + tuple(SCRATCH) + tuple(SEMS)
    r = dict(zip(names, refs, strict=True))

    class R:
        pass

    k = R()
    k.__dict__.update(r)
    z = lax.axis_index("samp")
    y = lax.axis_index("row_0")
    xl = lax.axis_index("row_1")
    xh = lax.axis_index("col_0")
    co = lax.axis_index("col_1")
    c = 2 * xh + co
    row = 2 * y + xl
    zof = [lax.rem(z + n, 8) for n in range(8)]
    zback = [lax.rem(z + 8 - n, 8) for n in range(8)]
    yof = [lax.rem(y + n, 4) for n in range(4)]
    x_other = {"row_1": 1 - xl}
    y_up = {"row_0": yof[1]}
    y_down = {"row_0": yof[3]}
    z_up = {"samp": zof[1]}
    z_down = {"samp": zof[7]}
    core_other = {"col_1": 1 - co}
    xh_other = {"col_0": 1 - xh}
    c_core = 2 * xh + (1 - co)
    c_xh = 2 * (1 - xh) + co
    cpeers = []
    for n in range(1, 4):
        ph, pc = lax.rem(xh + n // 2, 2), lax.rem(co + n % 2, 2)
        cpeers.append((n, {"col_0": ph, "col_1": pc}, 2 * ph + pc))
    rpeers = []
    for n in range(1, 8):
        py, px = lax.rem(y + n // 2, 4), lax.rem(xl + n % 2, 2)
        fy, fx = lax.rem(y + 4 - n // 2, 4), lax.rem(xl + n % 2, 2)
        rpeers.append((n, {"row_0": py, "row_1": px}, 2 * py + px, 2 * fy + fx))

    def when(cond, body):
        pl.when(cond)(body)

    loads = [
        pltpu.make_async_copy(k.h_tokens, k.tokens, k.s_in.at[0]),
        pltpu.make_async_copy(k.h_win, k.win, k.s_in.at[1]),
        pltpu.make_async_copy(k.h_cot, k.nc.at[z, 1], k.s_in.at[2]),
        pltpu.make_async_copy(k.h_wout, k.wout, k.s_in.at[3]),
    ]
    for copy in loads:
        copy.start()
    barrier = pltpu.get_barrier_semaphore()
    for n in range(1, 8):
        pl.semaphore_signal(barrier, inc=1, device_id={"samp": zof[n]}, device_id_type=MESH)
    for _, dev, _, _ in rpeers:
        pl.semaphore_signal(barrier, inc=1, device_id=dev, device_id_type=MESH)
    for _, dev, _ in cpeers:
        pl.semaphore_signal(barrier, inc=1, device_id=dev, device_id_type=MESH)
    swapped = {"row_0": c, "col_0": y // 2, "col_1": y % 2}
    swapped_x = {"row_0": c, "row_1": 1 - xl, "col_0": y // 2, "col_1": y % 2}

    @pl.when(c != y)
    def _():
        pl.semaphore_signal(barrier, inc=1, device_id=swapped, device_id_type=MESH)
        pl.semaphore_signal(barrier, inc=1, device_id=swapped_x, device_id_type=MESH)


    types = lax.broadcasted_iota(jnp.int32, (32, 128), 0) == k.atom[...]
    top_root = 160.0 ** (1.0 / 7.0)
    low_root = 0.0004 ** (1.0 / 7.0)
    root = top_root + k.step[...].astype(F32) / (STEPS - 1) * (low_root - top_root)
    level = 7.0 / 4.0 * jnp.log(root)
    add = tn(types.astype(F32).astype(BF16), k.table[...]) + level * wide_row(k.nrow)
    loads[0].wait()
    base = k.tokens[...].astype(F32) + add
    k.base[...] = base
    centered = base - jnp.mean(base, axis=1, keepdims=True)
    inv = lax.rsqrt(jnp.mean(centered * centered, axis=1, keepdims=True) + eps)
    unit = centered * inv
    k.inv[...] = inv
    k.unit[...] = unit
    normed = (unit * wide_row(k.gain)).astype(BF16)
    k.nc[z, 0] = normed
    loads[1].wait()
    loads[3].wait()
    loads[2].wait()
    pair_copies = []
    for n in range(8):
        part = pl.ds(16 * n, 16)
        copy = pltpu.make_async_copy(k.pair.at[part], k.xbuf.at[part], k.s_pair.at[n])
        copy.start()
        pair_copies.append(copy)
    proj_kv = nt(k.win[192:576], normed)
    for m in range(2):
        for hh in range(4):
            at = 192 * m + 48 * hh
            k.kvown[m, hh] = proj_kv[at : at + 48].astype(BF16)
    when(c == y, lambda: pl.semaphore_wait(barrier, 17))
    when(c != y, lambda: pl.semaphore_wait(barrier, 19))

    started = []
    count = [0]

    def make(src, dst, sem, dev):
        d = pltpu.make_async_remote_copy(
            src_ref=src,
            dst_ref=dst,
            send_sem=k.s_send.at[count[0]],
            recv_sem=sem,
            device_id=dev,
            device_id_type=MESH,
        )
        count[0] += 1
        return d

    def send(src, dst, sem, dev):
        d = make(src, dst, sem, dev)
        d.start()
        started.append((None, d))

    def arrived(dst, sem):
        pltpu.make_async_remote_copy(
            src_ref=dst,
            dst_ref=dst,
            send_sem=k.s_send.at[0],
            recv_sem=sem,
            device_id=z_up,
            device_id_type=MESH,
        ).wait_recv()

    give_kv = make(k.kvown, k.kv.at[xl, c], k.s_kvp.at[0], swapped)
    started.append((c != y, give_kv))
    send(k.kvown, k.kv.at[xl, c], k.s_xb.at[0], swapped_x)

    def keep_kv():
        k.kv[xl, y] = k.kvown[...]

    when(c != y, lambda: give_kv.start())
    when(c == y, keep_kv)
    y1, y2, y3 = yof[1], yof[2], yof[3]

    def kv_row(side, sem):
        block = k.kv.at[side, y]
        send(block, block, sem.at[0], y_up)
        send(block, block, sem.at[1], y_down)

    def kv_row_relay(side, sem):
        arrived(k.kv.at[side, y3], sem.at[0])
        send(k.kv.at[side, y3, 0], k.kv.at[side, y3, 0], sem.at[2], y_up)
        arrived(k.kv.at[side, y1], sem.at[1])
        send(k.kv.at[side, y1, 1], k.kv.at[side, y1, 1], sem.at[3], y_down)

    proj_q = nt(k.win[0:192], normed)
    gate = jax.nn.sigmoid(nt(k.win[576:768], normed))
    gmix = nt(k.wout[...], k.nc[z, 1])
    k.gate[...] = gate
    k.gmix[...] = gmix
    grad_attend = gmix * gate
    for hh in range(4):
        k.qg[c, 0, hh] = proj_q[48 * hh : 48 * hh + 48].astype(BF16)
        k.qg[c, 1, hh] = grad_attend[48 * hh : 48 * hh + 48].astype(BF16)
    send(k.qg.at[c], k.qg.at[c], k.s_qgx.at[0], xh_other)
    send(k.qg.at[c], k.qg.at[c], k.s_qgc.at[0], core_other)
    half = pl.ds(64 * co, 64)
    send(k.nc.at[z, :, half], k.nc.at[z, :, half], k.s_ncp.at[1], z_up)
    send(k.nc.at[z, :, half], k.nc.at[z, :, half], k.s_ncm.at[1], z_down)

    weights = k.pw[...] * k.pgain[...]
    w_hi = weights.astype(BF16)
    rest = weights - w_hi.astype(F32)
    w_mid = rest.astype(BF16)
    w_lo = (rest - w_mid.astype(F32)).astype(BF16)
    sub16 = lax.broadcasted_iota(jnp.int32, (16, 128), 0)
    lane16 = lax.broadcasted_iota(jnp.int32, (16, 128), 1)
    pick = (lane16 == 16 * z + sub16).astype(F32).astype(BF16)
    k.waug[0:16] = w_hi
    k.waug[16:32] = w_mid
    k.waug[32:48] = w_lo
    k.waug[48:64] = pick
    k.waug[64:80] = jnp.ones((16, 128), BF16)
    k.gh[...] = jnp.sum(weights, axis=1, keepdims=True)
    spread = weights - jnp.mean(weights, axis=1, keepdims=True)
    s_hi = spread.astype(BF16)
    s_lo = (spread - s_hi.astype(F32)).astype(BF16)
    sub256 = lax.broadcasted_iota(jnp.int32, (256, 256), 0)
    lane256 = lax.broadcasted_iota(jnp.int32, (256, 256), 1)
    same = (sub256 // 16) == (lane256 // 16)
    tall = (
        lax.broadcasted_iota(jnp.int32, (256, 16), 0) % 16 == lax.broadcasted_iota(jnp.int32, (256, 16), 1)
    ).astype(F32).astype(BF16)
    for n, part in enumerate((s_hi, s_lo)):
        small = nt(pick, part).astype(BF16)
        wide = nt(nn(tall, small).astype(BF16), tall)
        k.amat[n] = jnp.where(same, wide, 0.0).astype(BF16)
    k.emat[...] = jnp.where(same, 1.0 / 128.0, 0.0).astype(BF16)
    eye = lax.broadcasted_iota(jnp.int32, (16, 16), 0) == lax.broadcasted_iota(jnp.int32, (16, 16), 1)

    def block_counts(ref, total):
        first = (lax.broadcasted_iota(jnp.int32, (16, total), 0) + 4 * row) == ref[0:1]
        second = lax.broadcasted_iota(jnp.int32, (256, total), 0) // BLOCK + 8 * c == ref[1:2]
        return nt(first.astype(F32).astype(BF16), second.astype(F32).astype(BF16))

    bond = block_counts(k.bonds, 64)
    chir = block_counts(k.chirs, 32)
    w_bond = jnp.sum(jnp.where(eye, k.rw[0:1], 0.0), axis=1, keepdims=True)
    w_chir = jnp.sum(jnp.where(eye, k.rw[1:2], 0.0), axis=1, keepdims=True)
    for n in range(4):
        k.rst[n] = w_bond * bond[n : n + 1] + w_chir * chir[n : n + 1]

    ones = jnp.ones((8, 128), BF16)

    def pair_rows(n):
        pair_copies[n].wait()

        def body(i, carry):
            x = k.xbuf[i]
            res = nt(k.waug[...], x)
            xf = x.astype(F32)
            sq = xf * xf
            hi = sq.astype(BF16)
            lo = (sq - hi.astype(F32)).astype(BF16)
            ss = nt(ones, hi) + nt(ones, lo)
            mean = res[64:65] * (1.0 / 128.0)
            var = ss[0:1] * (1.0 / 128.0) - mean * mean
            inv = lax.rsqrt(jnp.maximum(var, 0.0) + eps)
            bias = res[0:16] + res[16:32] + res[32:48]
            bias = inv * (bias - mean * k.gh[...])
            rows = pl.ds(pl.multiple_of(i * 16, 16), 16)
            k.planes[0, rows, :] = bias[:, :128]
            k.planes[1, rows, :] = bias[:, 128:]
            k.hat[rows, :] = (res[48:64] - mean) * (inv * inv)
            k.invb[rows, :] = jnp.broadcast_to(inv, (16, 256))
            k.st[i, 0:1] = inv
            k.st[i, 1:2] = mean * inv
            return carry

        lax.fori_loop(16 * n, 16 * n + 16, body, 0, unroll=4)

    def nc_relay(n):
        src = k.nc.at[zback[n], :, half]
        arrived(src, k.s_ncp.at[n])
        if n < 4:
            send(src, src, k.s_ncp.at[n + 1], z_up)
        send(src, src, k.s_ncc.at[n], core_other)
        if n < 4:
            src = k.nc.at[zof[n], :, half]
            arrived(src, k.s_ncm.at[n])
            if n < 3:
                send(src, src, k.s_ncm.at[n + 1], z_down)
            send(src, src, k.s_ncc.at[8 - n], core_other)

    pair_rows(0)
    pair_rows(1)
    when(c != y, lambda: arrived(k.kv.at[xl, y], k.s_kvp.at[0]))
    kv_row(xl, k.s_yo)
    arrived(k.kv.at[1 - xl, y], k.s_xb.at[0])
    kv_row(1 - xl, k.s_yp)
    pair_rows(2)
    arrived(k.qg.at[c_xh], k.s_qgx.at[0])
    send(k.qg.at[c_xh], k.qg.at[c_xh], k.s_qgc.at[1], core_other)
    pair_rows(3)
    kv_row_relay(xl, k.s_yo)
    pair_rows(4)
    kv_row_relay(1 - xl, k.s_yp)
    pair_rows(5)
    nc_relay(1)
    pair_rows(6)
    pair_rows(7)
    for side, sem in ((xl, k.s_yo), (1 - xl, k.s_yp)):
        arrived(k.kv.at[side, y2, 0], sem.at[2])
        arrived(k.kv.at[side, y2, 1], sem.at[3])
    arrived(k.qg.at[c_core], k.s_qgc.at[0])
    arrived(k.qg.at[2 * (1 - xh) + 1 - co], k.s_qgc.at[1])

    lane = lax.broadcasted_iota(jnp.int32, (128, 128), 1)

    def head_kv(g, m, hh):
        return jnp.concatenate([k.kv[0, g, m, hh], k.kv[1, g, m, hh]], axis=1)

    order = (yof[1], yof[2], yof[3], y)

    def head_at(p):
        g, hh = lax.rem(y + 1 + p // 4, 4), p % 4
        return g, hh, 4 * g + hh

    def forward(p_at, packed):
        g, hh, h = head_at(p_at)
        keys = head_kv(g, 0, hh)
        vals = head_kv(g, 1, hh)
        by_head = pl.ds(h, 128, stride=16)
        bias = jnp.concatenate([k.planes[0, by_head, :], k.planes[1, by_head, :]], axis=1)
        extra = [jnp.broadcast_to(k.rst[n, pl.ds(h, 1), :], (32, 256)) for n in range(4)]
        s = tn(k.qg[g, 0, hh], keys) * SCALE + (bias + jnp.concatenate(extra, axis=0))
        top = jnp.max(s, axis=1, keepdims=True)
        p = jnp.exp(s - top)
        dp = tn(k.qg[g, 1, hh], vals)
        k.pr[p_at] = p
        k.dp[p_at] = dp
        k.ot[g, hh] = nt(vals, p.astype(BF16)).astype(BF16)
        total = jnp.sum(p, axis=1, keepdims=True)
        dots = jnp.sum(p * dp, axis=1, keepdims=True)
        packed = jnp.where(lane == p_at % 8, top, packed)
        packed = jnp.where(lane == 8 + p_at % 8, total, packed)
        return jnp.where(lane == 16 + p_at % 8, dots, packed)

    for b in range(2):
        packed = jnp.zeros((128, 128), F32)
        for p_at in range(8 * b, 8 * b + 8):
            packed = forward(p_at, packed)
        k.stats[b, c] = packed.T[0:24]
        for n, dev, _ in cpeers:
            send(k.stats.at[b, c], k.stats.at[b, c], k.s_st.at[4 * b + n], dev)
    for n, dev, who in cpeers:
        send(k.ot.at[who], k.oin.at[c], k.s_o.at[n], dev)
    k.oin[c] = k.ot[c]

    def combine(b):
        for n, _, who in cpeers:
            arrived(k.stats.at[b, who], k.s_st.at[4 * b + n])
        top = k.stats[b, 0, 0:8]
        for n in range(1, 4):
            top = jnp.maximum(top, k.stats[b, n, 0:8])
        total = jnp.zeros((8, 128), F32)
        dots = jnp.zeros((8, 128), F32)
        weights = []
        for n in range(4):
            w = jnp.exp(k.stats[b, n, 0:8] - top)
            weights.append(w)
            total += w * k.stats[b, n, 8:16]
            dots += w * k.stats[b, n, 16:24]
        inv_total = 1.0 / total
        for n in range(4):
            k.arow[n, 8 * b : 8 * b + 8] = weights[n] * inv_total
        own = k.arow[c, 8 * b : 8 * b + 8]
        k.arow_own[8 * b : 8 * b + 8] = own
        k.acol[b] = jnp.concatenate([own, dots * inv_total, jnp.zeros((112, 128), F32)], axis=0).T

    def backward(p_at, carry):
        g, hh, h = head_at(p_at)
        columns = k.acol[p_at // 8]
        alpha = columns[:, p_at % 8 : p_at % 8 + 1]
        delta = columns[:, 8 + p_at % 8 : 9 + p_at % 8]
        p = k.pr[p_at]
        ds = p * alpha * (k.dp[p_at] - delta)
        by_head = pl.ds(h, 128, stride=16)
        k.bgf[0, by_head, :] = ds[:, :128]
        k.bgf[1, by_head, :] = ds[:, 128:]
        low = ds.astype(BF16)
        k.dqt[g, hh] = (nt(head_kv(g, 0, hh), low) * SCALE).astype(BF16)
        dk = (nn(k.qg[g, 0, hh], low) * SCALE).astype(BF16)
        k.dkv[0, g, 0, hh] = dk[:, :128]
        k.dkv[1, g, 0, hh] = dk[:, 128:]
        ga = (k.qg[g, 1, hh].astype(F32) * k.arow_own[pl.ds(p_at, 1), :]).astype(BF16)
        dv = nn(ga, p.astype(BF16)).astype(BF16)
        k.dkv[0, g, 1, hh] = dv[:, :128]
        k.dkv[1, g, 1, hh] = dv[:, 128:]
        return carry

    def key_value_out(n):
        for p_at in range(4 * n, 4 * n + 4):
            backward(p_at, 0)
        g = order[n]
        send(k.dkv.at[1 - xl, g], k.xin.at[g], k.s_xin.at[n], x_other)
        d = make(
            k.dqt.at[g],
            k.dqin.at[c],
            k.s_dq.at[2 * lax.rem(xh + g // 2, 2) + lax.rem(co + g % 2, 2)],
            {"col_0": g // 2, "col_1": g % 2},
        )
        started.append((c != g, d))
        when(c != g, lambda: d.start())

    def ring_step(n):
        for way, owner, dev in ((0, zof[4 - n], z_up), (1, zback[4 - n], z_down)):
            for part in range(2):
                if n == 0 and part != way:
                    continue
                rows = pl.ds(pl.multiple_of(owner * 256 + 128 * part, 128), 128)
                value = k.bgf[:, rows, :]
                if n > 1 or (n == 1 and part == way):
                    arrived(k.brv.at[way, n - 1, part], k.s_br.at[8 * way + 2 * (n - 1) + part])
                    value = value + k.brv[way, n - 1, part].astype(F32)
                k.bst[way, n, part] = value.astype(BF16)
                send(k.bst.at[way, n, part], k.brv.at[way, n, part], k.s_br.at[8 * way + 2 * n + part], dev)

    def bg_finish():
        for part in range(2):
            rows = pl.ds(pl.multiple_of(z * 256 + 128 * part, 128), 128)
            value = k.bgf[:, rows, :]
            for way in range(2):
                arrived(k.brv.at[way, 3, part], k.s_br.at[8 * way + 6 + part])
                value = value + k.brv[way, 3, part].astype(F32)
            k.bgt[:, 128 * part : 128 * part + 128] = value
            k.bga[z, :, 128 * part : 128 * part + 128] = value.astype(BF16)
        for part in range(2):
            mine_bg = k.bga.at[z, :, pl.ds(128 * part, 128)]
            send(mine_bg, mine_bg, k.s_bg.at[part], z_up)
            send(mine_bg, mine_bg, k.s_bg.at[8 + part], z_down)

    def bg_relay(n):
        for part in range(2):
            half_rows = pl.ds(128 * part, 128)
            for way, owner, dev in ((0, zback[n], z_up), (1, zof[n], z_down)):
                if n == 4 and part != way:
                    continue
                block = k.bga.at[owner, :, half_rows]
                arrived(block, k.s_bg.at[8 * way + 2 * (n - 1) + part])
                if n < 3 or (n == 3 and part == way):
                    send(block, block, k.s_bg.at[8 * way + 2 * n + part], dev)

    combine(0)
    key_value_out(0)
    key_value_out(1)
    combine(1)
    key_value_out(2)
    key_value_out(3)
    k.dqin[c] = k.dqt[c]
    ring_step(0)
    nc_relay(2)

    for n, _, who in cpeers:
        arrived(k.oin.at[who], k.s_o.at[n])
    for hh in range(4):
        att = jnp.zeros((48, 128), F32)
        for n in range(4):
            w = k.arow[n, pl.ds(4 * lax.rem(c + 7 - y, 4) + hh, 1), :]
            att += k.oin[n, hh].astype(F32) * w
        k.att[48 * hh : 48 * hh + 48] = att
    gate = k.gate[...]
    att = k.att[...]
    mixed = (gate * att).astype(BF16)
    grad_gate = (k.gmix[...] * att * gate * (1.0 - gate)).astype(BF16)
    k.gin[576:768] = grad_gate
    for n in range(4):
        k.gsh[0, 4 + n, 0:48] = grad_gate[48 * n : 48 * n + 48]
    for n in range(8):
        for m in range(2):
            at = 32 * n + 16 * m
            k.gsh[m, n, 48:64] = mixed[at : at + 16] if n < 6 else jnp.zeros((16, 128), BF16)
    part_out = tn(mixed, k.wout[...]).astype(BF16)
    for n in range(4):
        k.po[n] = part_out[32 * n : 32 * n + 32]
    for n, dev, who in cpeers:
        send(k.po.at[who], k.por.at[c], k.s_po.at[n], dev)
    k.por[c] = k.po[c]

    def share(b):
        for n in range(1, 8):
            send(k.gsh.at[b, zof[n]], k.zsh.at[b, z], k.s_zi.at[8 * b + n], {"samp": zof[n]})
        k.zsh[b, z] = k.gsh[b, z]

    def weight_rows(b):
        for n in range(1, 8):
            arrived(k.zsh.at[b, zback[n]], k.s_zi.at[8 * b + n])
        acc = nn(k.zsh[b, 0, 0:48], k.nc[0, 0])
        acc_out = nn(k.zsh[b, 0, 48:64], k.nc[0, 1])
        for n in range(1, 8):
            acc += nn(k.zsh[b, n, 0:48], k.nc[n, 0])
            acc_out += nn(k.zsh[b, n, 48:64], k.nc[n, 1])
        for n in range(4):
            tall = (acc[16 * n : 16 * n + 16] if n < 3 else acc_out).astype(BF16)
            k.dws[b, 2 * n] = tall[:, :384]
            k.dws[b, 2 * n + 1] = tall[:, 384:]
        for n, dev, to, _ in rpeers:
            send(k.dws.at[b, to], k.dwr.at[b, row], k.s_dw.at[8 * b + n], dev)
        k.dwr[b, row] = k.dws[b, row]

    def weight_sum(b):
        for n, _, _, came in rpeers:
            arrived(k.dwr.at[b, came], k.s_dw.at[8 * b + n])
        total = k.dwr[b, 0].astype(F32)
        for n in range(1, 8):
            total += k.dwr[b, n].astype(F32)
        k.dwall[b, y, xl, z] = total.astype(BF16)
        for n in range(1, 8):
            here = k.dwall.at[b, y, xl, z]
            send(here, here, k.s_dz.at[8 * b + n], {"samp": zof[n]})

    low_z, high_z = pl.ds(0, 4), pl.ds(4, 4)

    def same_place(ref, sem, dev):
        send(ref, ref, sem, dev)

    def spread_1(b):
        w, ay, by, bx = k.dwall.at[b], 4 * b, 4 * b, 4 * b
        for n in range(1, 8):
            arrived(w.at[y, xl, zback[n]], k.s_dz.at[8 * b + n])
        same_place(w.at[y, xl, low_z], k.s_ax.at[b], x_other)
        same_place(w.at[y, xl, high_z], k.s_by.at[by], y_up)
        same_place(w.at[y, xl, high_z], k.s_by.at[by + 1], y_down)
        same_place(w.at[y, xl, high_z], k.s_bx.at[bx], x_other)

    def spread_2(b):
        w, ay, by, bx = k.dwall.at[b], 4 * b, 4 * b, 4 * b
        arrived(w.at[y, 1 - xl, low_z], k.s_ax.at[b])
        same_place(w.at[y, :, low_z], k.s_ay.at[ay], y_up)
        same_place(w.at[y, :, low_z], k.s_ay.at[ay + 1], y_down)
        arrived(w.at[y3, xl, high_z], k.s_by.at[by])
        same_place(w.at[y3, xl, pl.ds(4, 2)], k.s_by.at[by + 2], y_up)
        same_place(w.at[y3, xl, high_z], k.s_bx.at[bx + 1], x_other)
        arrived(w.at[y1, xl, high_z], k.s_by.at[by + 1])
        same_place(w.at[y1, xl, pl.ds(6, 2)], k.s_by.at[by + 3], y_down)
        same_place(w.at[y1, xl, high_z], k.s_bx.at[bx + 2], x_other)

    def spread_3(b):
        w, ay, by, bx = k.dwall.at[b], 4 * b, 4 * b, 4 * b
        arrived(w.at[y3, :, low_z], k.s_ay.at[ay])
        same_place(w.at[y3, 0, low_z], k.s_ay.at[ay + 2], y_up)
        arrived(w.at[y1, :, low_z], k.s_ay.at[ay + 1])
        same_place(w.at[y1, 1, low_z], k.s_ay.at[ay + 3], y_down)
        arrived(w.at[y2, xl, pl.ds(4, 2)], k.s_by.at[by + 2])
        arrived(w.at[y2, xl, pl.ds(6, 2)], k.s_by.at[by + 3])
        same_place(w.at[y2, xl, high_z], k.s_bx.at[bx + 3], x_other)

    def spread_4(b):
        w, ay, by, bx = k.dwall.at[b], 4 * b, 4 * b, 4 * b
        arrived(w.at[y, 1 - xl, high_z], k.s_bx.at[bx])
        arrived(w.at[y3, 1 - xl, high_z], k.s_bx.at[bx + 1])
        arrived(w.at[y1, 1 - xl, high_z], k.s_bx.at[bx + 2])
        arrived(w.at[y2, 1 - xl, high_z], k.s_bx.at[bx + 3])
        arrived(w.at[y2, 0, low_z], k.s_ay.at[ay + 2])
        arrived(w.at[y2, 1, low_z], k.s_ay.at[ay + 3])

    def plus(dst, piece, a, b):
        dst[piece] = (a.astype(F32) + b.astype(F32)).astype(BF16)

    def first_sum(n):
        g = order[n]
        arrived(k.xin.at[g], k.s_xin.at[n])
        plus(k.sx, g, k.dkv[xl, g], k.xin[g])
        if n < 3:
            send(k.sx.at[g], k.yin.at[y], k.s_yin.at[n + 1], {"row_0": g})

    give_back = make(k.fin, k.dkvown, k.s_fin.at[0], swapped)
    started.append((c != y, give_back))

    def last_sum():
        total = k.sx[y].astype(F32)
        for n in range(1, 4):
            arrived(k.yin.at[yof[4 - n]], k.s_yin.at[n])
            total += k.yin[yof[4 - n]].astype(F32)
        total = total.astype(BF16)
        k.fin[...] = total

        def keep():
            k.dkvown[...] = k.fin[...]

        when(c == y, keep)
        when(c != y, lambda: give_back.start())

    outs = []

    def give_out(src, dst):
        copy = pltpu.make_async_copy(src, dst, k.s_out.at[len(outs)])
        copy.start()
        outs.append(copy)

    def pair_back(owner):
        bg = jnp.concatenate([k.bga[owner, 0], k.bga[owner, 1]], axis=1)
        rows = pl.ds(pl.multiple_of(owner * 256, 256), 256)
        plane = jnp.concatenate([k.planes[0, rows, :], k.planes[1, rows, :]], axis=1)
        product = bg.astype(F32) * plane
        hi = product.astype(BF16)
        lo = (product - hi.astype(F32)).astype(BF16)
        both = nn(k.emat[...], hi) + nn(k.emat[...], lo)
        out = nn(k.amat[0], bg) + nn(k.amat[1], bg)
        k.pg[rows, :] = (k.invb[rows, :] * out - k.hat[rows, :] * both).astype(BF16)
        give_out(k.pg.at[rows], k.o_pg.at[rows])

    def project_pairs(n, carry):
        acc, low = carry
        part = pl.ds(pl.multiple_of(n * 16, 16), 16)
        bg = jnp.concatenate([k.bgt[0, part, :], k.bgt[1, part, :]], axis=1)
        i = 16 * z + n
        scaled = bg * k.st[i, 0:1]
        hi = scaled.astype(BF16)
        rest = (scaled - hi.astype(F32)).astype(BF16)
        acc = acc + nn(jnp.concatenate([hi, rest], axis=0), k.xbuf[i])
        low = low + jnp.sum(bg * k.st[i, 1:2], axis=1, keepdims=True)
        return (acc, low)

    first_sum(0)
    first_sum(1)
    for n, _, who in cpeers:
        arrived(k.dqin.at[who], k.s_dq.at[n])
    for hh in range(4):
        dq = k.dqin[0, hh].astype(F32)
        for n in range(1, 4):
            dq += k.dqin[n, hh].astype(F32)
        k.gin[48 * hh : 48 * hh + 48] = dq.astype(BF16)
        k.gsh[0, hh, 0:48] = dq.astype(BF16)
    share(0)
    ring_step(1)
    first_sum(2)
    first_sum(3)
    nc_relay(3)
    ring_step(2)
    last_sum()
    nc_relay(4)
    for n in range(1, 8):
        arrived(k.nc.at[zback[n], :, pl.ds(64 * (1 - co), 64)], k.s_ncc.at[n])
    weight_rows(0)
    when(c != y, lambda: arrived(k.dkvown, k.s_fin.at[0]))
    for hh in range(4):
        k.gin[192 + 48 * hh : 240 + 48 * hh] = k.dkvown[0, hh]
        k.gin[384 + 48 * hh : 432 + 48 * hh] = k.dkvown[1, hh]
        k.gsh[1, hh, 0:48] = k.dkvown[0, hh]
        k.gsh[1, 4 + hh, 0:48] = k.dkvown[1, hh]
    share(1)
    ring_step(3)
    weight_sum(0)
    part_normed = tn(k.gin[...], k.win[...]).astype(BF16)
    for n in range(4):
        k.gn[n] = part_normed[32 * n : 32 * n + 32]
    for n, dev, who in cpeers:
        send(k.gn.at[who], k.gnr.at[c], k.s_gn.at[n], dev)
    k.gnr[c] = k.gn[c]
    bg_finish()
    weight_rows(1)
    spread_1(0)
    acc, low = lax.fori_loop(
        0, 16, project_pairs, (jnp.zeros((32, 128), F32), jnp.zeros((16, 1), F32)), unroll=2
    )
    k.pj1[...] = k.pgain[...] * (acc[0:16] + acc[16:32] - low)
    for n in range(1, 8):
        send(k.pj1, k.pjz.at[z], k.s_pz.at[n], {"samp": zof[n]})
    k.pjz[z] = k.pj1[...]

    for n, _, who in cpeers:
        arrived(k.por.at[who], k.s_po.at[n])
    mine = pl.ds(pl.multiple_of(32 * c, 32), 32)
    total = k.base[mine]
    for n in range(4):
        total = total + k.por[n].astype(F32)
    k.upd[c] = total.astype(BF16)
    for n, dev, _ in cpeers:
        send(k.upd.at[c], k.upd.at[c], k.s_upd.at[n], dev)
    weight_sum(1)
    bg_relay(1)
    spread_2(0)
    for n, _, who in cpeers:
        arrived(k.gnr.at[who], k.s_gn.at[n])
    total = k.gnr[0].astype(F32)
    for n in range(1, 4):
        total += k.gnr[n].astype(F32)
    scaled = total * wide_row(k.gain)
    hat = k.unit[mine]
    back = k.inv[mine] * (
        scaled
        - jnp.mean(scaled, axis=1, keepdims=True)
        - hat * jnp.mean(scaled * hat, axis=1, keepdims=True)
    )
    k.tok[c] = (k.nc[z, 1, mine].astype(F32) + back).astype(BF16)
    for n, dev, _ in cpeers:
        send(k.tok.at[c], k.tok.at[c], k.s_tok.at[n], dev)

    pair_back(z)
    bg_relay(2)
    spread_1(1)
    for n in range(1, 8):
        arrived(k.pjz.at[zback[n]], k.s_pz.at[n])
    total = k.pjz[0]
    for n in range(1, 8):
        total += k.pjz[n]
    k.pj2[...] = total
    for n, dev, _, _ in rpeers:
        send(k.pj2, k.pjr.at[row], k.s_pr.at[n], dev)
    k.pjr[row] = total
    spread_3(0)
    pair_back(zof[1])
    pair_back(zback[1])
    spread_2(1)
    bg_relay(3)
    for n, _, _, came in rpeers:
        arrived(k.pjr.at[came], k.s_pr.at[n])
    total = k.pjr[0]
    for n in range(1, 8):
        total += k.pjr[n]
    k.pjc[c] = total
    for n, dev, _ in cpeers:
        send(k.pjc.at[c], k.pjc.at[c], k.s_pc.at[n], dev)
    pair_back(zof[2])
    spread_3(1)
    pair_back(zback[2])
    bg_relay(4)
    pair_back(zof[3])
    pair_back(zback[3])
    pair_back(zof[4])
    spread_4(0)
    for n, _, who in cpeers:
        arrived(k.upd.at[who], k.s_upd.at[n])
        arrived(k.tok.at[who], k.s_tok.at[n])
        arrived(k.pjc.at[who], k.s_pc.at[n])
    give_out(k.upd, k.o_upd)
    give_out(k.tok, k.o_tok)
    k.o_proj[...] = k.pjc[0] + k.pjc[1] + k.pjc[2] + k.pjc[3]

    def weight_out(b):
        for half_of in range(2):
            lanes = slice(384 * half_of, 384 * half_of + 384)
            for n in range(8):
                member = ((0, 3), (1, 2))[b][n // 4]
                for m in range(3):
                    at = 192 * member + 48 * (n % 4) + 16 * m
                    k.win_out[at : at + 16, lanes] = k.dwall[b, m, half_of, n]
                if n < 6:
                    at = 32 * n + 16 * b
                    k.wout_out[at : at + 16, lanes] = k.dwall[b, 3, half_of, n]

    weight_out(0)
    for at in (0, 576):
        give_out(k.win_out.at[pl.ds(at, 192)], k.o_in.at[pl.ds(at, 192)])
    spread_4(1)
    weight_out(1)
    give_out(k.win_out.at[pl.ds(192, 384)], k.o_in.at[pl.ds(192, 384)])
    give_out(k.wout_out, k.o_out)
    for copy in outs:
        copy.wait()
    for cond, d in started:
        if cond is None:
            d.wait_send()
        else:
            when(cond, lambda d=d: d.wait_send())


def copy_out(*refs):
    n = len(OUTPUTS)
    src, dst, buf, sems = refs[:n], refs[n : 2 * n], refs[2 * n : 3 * n], refs[3 * n]
    come = [pltpu.make_async_copy(src[m], buf[m], sems.at[m]) for m in range(n)]
    go = [pltpu.make_async_copy(buf[m], dst[m], sems.at[n + m]) for m in range(n)]
    for d in come:
        d.start()
    for d, e in zip(come, go):
        d.wait()
        e.start()
    for e in go:
        e.wait()


def on_device(
    tokens,
    atom_type,
    noise_step,
    pair_rep,
    bond_blocks,
    chiral_blocks,
    type_table,
    noise_row,
    norm_gain,
    pair_gain,
    in_weight,
    out_weight,
    pair_weight,
    restraint_weight,
    cotangent,
):
    args = dict(
        h_tokens=tokens[0],
        h_cot=cotangent[0],
        h_win=in_weight.reshape(768, 768),
        h_wout=out_weight,
        pair=pair_rep,
        atom=atom_type[None, :],
        step=noise_step[None, :],
        bonds=bond_blocks.T,
        chirs=chiral_blocks.T,
        table=type_table,
        nrow=noise_row.reshape(6, 128),
        gain=norm_gain.reshape(6, 128),
        pgain=pair_gain[None, :],
        pw=pair_weight.T,
        rw=restraint_weight,
    )
    vmem = pl.BlockSpec(memory_space=pltpu.VMEM)
    hbm = pl.BlockSpec(memory_space=pl.ANY)
    shapes = (
        jax.ShapeDtypeStruct((4, 32, 768), BF16),
        jax.ShapeDtypeStruct((4, 32, 768), BF16),
        jax.ShapeDtypeStruct((2048, 256), BF16),
        jax.ShapeDtypeStruct((768, 768), BF16),
        jax.ShapeDtypeStruct((192, 768), BF16),
        jax.ShapeDtypeStruct((16, 128), F32),
    )
    results = pl.pallas_call(
        kernel,
        out_shape=shapes,
        in_specs=[hbm if name.startswith("h_") or name == "pair" else vmem for name in INPUTS],
        out_specs=(hbm,) * 5 + (vmem,),
        scratch_shapes=[pltpu.VMEM(*s) for s in SCRATCH.values()]
        + [pltpu.SemaphoreType.DMA((n,)) for n in SEMS.values()],
        compiler_params=pltpu.CompilerParams(
            collective_id=0, has_side_effects=True, vmem_limit_bytes=60 * 1024 * 1024
        ),
    )(*(args[name] for name in INPUTS))
    upd, tok, pg, ing, outg, proj = pl.pallas_call(
        copy_out,
        out_shape=shapes,
        in_specs=[hbm] * 6,
        out_specs=(hbm,) * 6,
        scratch_shapes=[pltpu.VMEM(s.shape, s.dtype) for s in shapes]
        + [pltpu.SemaphoreType.DMA((12,))],
    )(*results)
    return (
        upd.reshape(1, 128, 768),
        tok.reshape(1, 128, 768),
        jnp.swapaxes(pg.reshape(128, 16, 256), 1, 2),
        ing.reshape(4, 192, 768),
        outg,
        proj.T,
    )


def solution(mesh):
    torus = Mesh(
        mesh.devices.reshape(mesh.shape["samp"], 4, 2, 2, 2),
        ("samp", "row_0", "row_1", "col_0", "col_1"),
    )
    placed = (
        P("samp", ROW, None),
        P(ROW),
        P("samp"),
        P(ROW, COL, None),
        P(),
        P(),
        P(),
        P(),
        P(),
        P(),
        P(None, COL, None),
        P(COL, None),
        P(),
        P(),
        P("samp", ROW, None),
    )
    return jax.shard_map(
        on_device,
        mesh=torus,
        in_specs=placed,
        out_specs=(
            P("samp", ROW, None),
            P("samp", ROW, None),
            P(ROW, COL, "samp"),
            P(None, COL, None),
            P(COL, None),
            P(),
        ),
        check_vma=False,
    )
```

```python
import math

import jax
import jax.numpy as jnp
from jax import lax
from jax.experimental import pallas as pl
from jax.experimental.pallas import tpu as pltpu
from jax.sharding import Mesh
from jax.sharding import PartitionSpec as P

HEAD_DIM = 48
BLOCK = 32
STEPS = 200
COL = ("col_0", "col_1")
ROW = ("row_0", "row_1")
MESH = pl.DeviceIdType.MESH
F32, BF16 = jnp.float32, jnp.bfloat16
SCALE = 1.0 / math.sqrt(HEAD_DIM)
eps = 1e-05


def nn(a, b):
    return lax.dot_general(a, b, (((1,), (0,)), ((), ())), preferred_element_type=F32)


def nt(a, b):
    return lax.dot_general(a, b, (((1,), (1,)), ((), ())), preferred_element_type=F32)


def tn(a, b):
    return lax.dot_general(a, b, (((0,), (0,)), ((), ())), preferred_element_type=F32)


SCRATCH = dict(
    xbuf=((128, 256, 128), BF16),
    tokens=((128, 768), BF16),
    win=((768, 768), BF16),
    wout=((192, 768), BF16),
    base=((128, 768), F32),
    unit=((128, 768), F32),
    inv=((128, 1), F32),
    gate=((192, 128), F32),
    gmix=((192, 128), F32),
    waug=((80, 128), BF16),
    gh=((16, 1), F32),
    rst=((4, 16, 256), F32),
    amat=((2, 256, 256), BF16),
    emat=((256, 256), BF16),
    planes=((2, 2048, 128), F32),
    hat=((2048, 256), F32),
    invb=((2048, 256), F32),
    st=((128, 8, 256), F32),
    qg=((4, 2, 4, 48, 128), BF16),
    kvown=((2, 4, 48, 128), BF16),
    kv=((2, 4, 2, 4, 48, 128), BF16),
    nc=((8, 2, 128, 768), BF16),
    pr=((16, 128, 256), F32),
    dp=((16, 128, 256), F32),
    ot=((4, 4, 48, 128), BF16),
    oin=((4, 4, 48, 128), BF16),
    stats=((2, 4, 24, 128), F32),
    acol=((2, 128, 128), F32),
    arow=((4, 16, 128), F32),
    arow_own=((16, 128), F32),
    bgf=((2, 2048, 128), F32),
    bst=((2, 4, 2, 2, 128, 128), BF16),
    brv=((2, 4, 2, 2, 128, 128), BF16),
    pg=((2048, 256), BF16),
    win_out=((768, 768), BF16),
    wout_out=((192, 768), BF16),
    bgt=((2, 256, 128), F32),
    bga=((8, 2, 256, 128), BF16),
    dqt=((4, 4, 48, 128), BF16),
    dqin=((4, 4, 48, 128), BF16),
    dkv=((2, 4, 2, 4, 48, 128), BF16),
    xin=((4, 2, 4, 48, 128), BF16),
    sx=((4, 2, 4, 48, 128), BF16),
    yin=((4, 2, 4, 48, 128), BF16),
    fin=((2, 4, 48, 128), BF16),
    dkvown=((2, 4, 48, 128), BF16),
    att=((192, 128), F32),
    gin=((768, 128), BF16),
    gsh=((2, 8, 64, 128), BF16),
    zsh=((2, 8, 64, 128), BF16),
    po=((4, 32, 768), BF16),
    por=((4, 32, 768), BF16),
    upd=((4, 32, 768), BF16),
    gn=((4, 32, 768), BF16),
    gnr=((4, 32, 768), BF16),
    tok=((4, 32, 768), BF16),
    dws=((2, 8, 16, 384), BF16),
    dwr=((2, 8, 16, 384), BF16),
    dwall=((2, 4, 2, 8, 16, 384), BF16),
    pjz=((8, 16, 128), F32),
    pjr=((8, 16, 128), F32),
    pjc=((4, 16, 128), F32),
    pj1=((16, 128), F32),
    pj2=((16, 128), F32),
)
SEMS = dict(
    s_pair=8,
    s_in=4,
    s_send=260,
    s_qgx=1,
    s_qgc=2,
    s_kvp=1,
    s_xb=1,
    s_yo=4,
    s_yp=4,
    s_ncp=5,
    s_ncm=4,
    s_ncc=8,
    s_st=8,
    s_o=4,
    s_dq=4,
    s_xin=4,
    s_yin=4,
    s_fin=1,
    s_br=16,
    s_bg=16,
    s_out=16,
    s_po=4,
    s_upd=4,
    s_gn=4,
    s_tok=4,
    s_zi=16,
    s_dw=16,
    s_dz=16,
    s_ax=2,
    s_ay=8,
    s_by=8,
    s_bx=8,
    s_pz=8,
    s_pr=8,
    s_pc=4,
)
INPUTS = (
    "h_tokens", "h_cot", "h_win", "h_wout", "pair",
    "atom", "step", "bonds", "chirs", "table", "nrow", "gain", "pgain", "pw", "rw",
)
OUTPUTS = ("o_upd", "o_tok", "o_pg", "o_in", "o_out", "o_proj")


def wide_row(ref):
    return jnp.concatenate([ref[n : n + 1] for n in range(6)], axis=1)


def kernel(*refs):
    names = INPUTS + OUTPUTS + tuple(SCRATCH) + tuple(SEMS)
    r = dict(zip(names, refs, strict=True))

    class R:
        pass

    k = R()
    k.__dict__.update(r)
    z = lax.axis_index("samp")
    y = lax.axis_index("row_0")
    xl = lax.axis_index("row_1")
    xh = lax.axis_index("col_0")
    co = lax.axis_index("col_1")
    c = 2 * xh + co
    row = 2 * y + xl
    zof = [lax.rem(z + n, 8) for n in range(8)]
    zback = [lax.rem(z + 8 - n, 8) for n in range(8)]
    yof = [lax.rem(y + n, 4) for n in range(4)]
    x_other = {"row_1": 1 - xl}
    y_up = {"row_0": yof[1]}
    y_down = {"row_0": yof[3]}
    z_up = {"samp": zof[1]}
    z_down = {"samp": zof[7]}
    core_other = {"col_1": 1 - co}
    xh_other = {"col_0": 1 - xh}
    c_core = 2 * xh + (1 - co)
    c_xh = 2 * (1 - xh) + co
    cpeers = []
    for n in range(1, 4):
        ph, pc = lax.rem(xh + n // 2, 2), lax.rem(co + n % 2, 2)
        cpeers.append((n, {"col_0": ph, "col_1": pc}, 2 * ph + pc))
    rpeers = []
    for n in range(1, 8):
        py, px = lax.rem(y + n // 2, 4), lax.rem(xl + n % 2, 2)
        fy, fx = lax.rem(y + 4 - n // 2, 4), lax.rem(xl + n % 2, 2)
        rpeers.append((n, {"row_0": py, "row_1": px}, 2 * py + px, 2 * fy + fx))

    def when(cond, body):
        pl.when(cond)(body)

    loads = [
        pltpu.make_async_copy(k.h_tokens, k.tokens, k.s_in.at[0]),
        pltpu.make_async_copy(k.h_win, k.win, k.s_in.at[1]),
        pltpu.make_async_copy(k.h_cot, k.nc.at[z, 1], k.s_in.at[2]),
        pltpu.make_async_copy(k.h_wout, k.wout, k.s_in.at[3]),
    ]
    for copy in loads:
        copy.start()
    barrier = pltpu.get_barrier_semaphore()
    for n in range(1, 8):
        pl.semaphore_signal(barrier, inc=1, device_id={"samp": zof[n]}, device_id_type=MESH)
    for _, dev, _, _ in rpeers:
        pl.semaphore_signal(barrier, inc=1, device_id=dev, device_id_type=MESH)
    for _, dev, _ in cpeers:
        pl.semaphore_signal(barrier, inc=1, device_id=dev, device_id_type=MESH)
    swapped = {"row_0": c, "col_0": y // 2, "col_1": y % 2}
    swapped_x = {"row_0": c, "row_1": 1 - xl, "col_0": y // 2, "col_1": y % 2}

    @pl.when(c != y)
    def _():
        pl.semaphore_signal(barrier, inc=1, device_id=swapped, device_id_type=MESH)
        pl.semaphore_signal(barrier, inc=1, device_id=swapped_x, device_id_type=MESH)


    types = lax.broadcasted_iota(jnp.int32, (32, 128), 0) == k.atom[...]
    top_root = 160.0 ** (1.0 / 7.0)
    low_root = 0.0004 ** (1.0 / 7.0)
    root = top_root + k.step[...].astype(F32) / (STEPS - 1) * (low_root - top_root)
    level = 7.0 / 4.0 * jnp.log(root)
    add = tn(types.astype(F32).astype(BF16), k.table[...]) + level * wide_row(k.nrow)
    loads[0].wait()
    base = k.tokens[...].astype(F32) + add
    k.base[...] = base
    centered = base - jnp.mean(base, axis=1, keepdims=True)
    inv = lax.rsqrt(jnp.mean(centered * centered, axis=1, keepdims=True) + eps)
    unit = centered * inv
    k.inv[...] = inv
    k.unit[...] = unit
    normed = (unit * wide_row(k.gain)).astype(BF16)
    k.nc[z, 0] = normed
    loads[1].wait()
    loads[3].wait()
    loads[2].wait()
    pair_copies = []
    for n in range(8):
        part = pl.ds(16 * n, 16)
        copy = pltpu.make_async_copy(k.pair.at[part], k.xbuf.at[part], k.s_pair.at[n])
        copy.start()
        pair_copies.append(copy)
    proj_kv = nt(k.win[192:576], normed)
    for m in range(2):
        for hh in range(4):
            at = 192 * m + 48 * hh
            k.kvown[m, hh] = proj_kv[at : at + 48].astype(BF16)
    when(c == y, lambda: pl.semaphore_wait(barrier, 17))
    when(c != y, lambda: pl.semaphore_wait(barrier, 19))

    started = []
    count = [0]

    def make(src, dst, sem, dev):
        d = pltpu.make_async_remote_copy(
            src_ref=src,
            dst_ref=dst,
            send_sem=k.s_send.at[count[0]],
            recv_sem=sem,
            device_id=dev,
            device_id_type=MESH,
        )
        count[0] += 1
        return d

    def send(src, dst, sem, dev):
        d = make(src, dst, sem, dev)
        d.start()
        started.append((None, d))

    def arrived(dst, sem):
        pltpu.make_async_remote_copy(
            src_ref=dst,
            dst_ref=dst,
            send_sem=k.s_send.at[0],
            recv_sem=sem,
            device_id=z_up,
            device_id_type=MESH,
        ).wait_recv()

    give_kv = make(k.kvown, k.kv.at[xl, c], k.s_kvp.at[0], swapped)
    started.append((c != y, give_kv))
    send(k.kvown, k.kv.at[xl, c], k.s_xb.at[0], swapped_x)

    def keep_kv():
        k.kv[xl, y] = k.kvown[...]

    when(c != y, lambda: give_kv.start())
    when(c == y, keep_kv)
    y1, y2, y3 = yof[1], yof[2], yof[3]

    def kv_row(side, sem):
        block = k.kv.at[side, y]
        send(block, block, sem.at[0], y_up)
        send(block, block, sem.at[1], y_down)

    def kv_row_relay(side, sem):
        arrived(k.kv.at[side, y3], sem.at[0])
        send(k.kv.at[side, y3, 0], k.kv.at[side, y3, 0], sem.at[2], y_up)
        arrived(k.kv.at[side, y1], sem.at[1])
        send(k.kv.at[side, y1, 1], k.kv.at[side, y1, 1], sem.at[3], y_down)

    proj_q = nt(k.win[0:192], normed)
    gate = jax.nn.sigmoid(nt(k.win[576:768], normed))
    gmix = nt(k.wout[...], k.nc[z, 1])
    k.gate[...] = gate
    k.gmix[...] = gmix
    grad_attend = gmix * gate
    for hh in range(4):
        k.qg[c, 0, hh] = proj_q[48 * hh : 48 * hh + 48].astype(BF16)
        k.qg[c, 1, hh] = grad_attend[48 * hh : 48 * hh + 48].astype(BF16)
    send(k.qg.at[c], k.qg.at[c], k.s_qgx.at[0], xh_other)
    send(k.qg.at[c], k.qg.at[c], k.s_qgc.at[0], core_other)
    half = pl.ds(64 * co, 64)
    send(k.nc.at[z, :, half], k.nc.at[z, :, half], k.s_ncp.at[1], z_up)
    send(k.nc.at[z, :, half], k.nc.at[z, :, half], k.s_ncm.at[1], z_down)

    weights = k.pw[...] * k.pgain[...]
    w_hi = weights.astype(BF16)
    rest = weights - w_hi.astype(F32)
    w_mid = rest.astype(BF16)
    w_lo = (rest - w_mid.astype(F32)).astype(BF16)
    sub16 = lax.broadcasted_iota(jnp.int32, (16, 128), 0)
    lane16 = lax.broadcasted_iota(jnp.int32, (16, 128), 1)
    pick = (lane16 == 16 * z + sub16).astype(F32).astype(BF16)
    k.waug[0:16] = w_hi
    k.waug[16:32] = w_mid
    k.waug[32:48] = w_lo
    k.waug[48:64] = pick
    k.waug[64:80] = jnp.ones((16, 128), BF16)
    k.gh[...] = jnp.sum(weights, axis=1, keepdims=True)
    spread = weights - jnp.mean(weights, axis=1, keepdims=True)
    s_hi = spread.astype(BF16)
    s_lo = (spread - s_hi.astype(F32)).astype(BF16)
    sub256 = lax.broadcasted_iota(jnp.int32, (256, 256), 0)
    lane256 = lax.broadcasted_iota(jnp.int32, (256, 256), 1)
    same = (sub256 // 16) == (lane256 // 16)
    tall = (
        lax.broadcasted_iota(jnp.int32, (256, 16), 0) % 16 == lax.broadcasted_iota(jnp.int32, (256, 16), 1)
    ).astype(F32).astype(BF16)
    for n, part in enumerate((s_hi, s_lo)):
        small = nt(pick, part).astype(BF16)
        wide = nt(nn(tall, small).astype(BF16), tall)
        k.amat[n] = jnp.where(same, wide, 0.0).astype(BF16)
    k.emat[...] = jnp.where(same, 1.0 / 128.0, 0.0).astype(BF16)
    eye = lax.broadcasted_iota(jnp.int32, (16, 16), 0) == lax.broadcasted_iota(jnp.int32, (16, 16), 1)

    def block_counts(ref, total):
        first = (lax.broadcasted_iota(jnp.int32, (16, total), 0) + 4 * row) == ref[0:1]
        second = lax.broadcasted_iota(jnp.int32, (256, total), 0) // BLOCK + 8 * c == ref[1:2]
        return nt(first.astype(F32).astype(BF16), second.astype(F32).astype(BF16))

    bond = block_counts(k.bonds, 64)
    chir = block_counts(k.chirs, 32)
    w_bond = jnp.sum(jnp.where(eye, k.rw[0:1], 0.0), axis=1, keepdims=True)
    w_chir = jnp.sum(jnp.where(eye, k.rw[1:2], 0.0), axis=1, keepdims=True)
    for n in range(4):
        k.rst[n] = w_bond * bond[n : n + 1] + w_chir * chir[n : n + 1]

    ones = jnp.ones((8, 128), BF16)

    def pair_rows(n):
        pair_copies[n].wait()

        def body(i, carry):
            x = k.xbuf[i]
            res = nt(k.waug[...], x)
            xf = x.astype(F32)
            sq = xf * xf
            hi = sq.astype(BF16)
            lo = (sq - hi.astype(F32)).astype(BF16)
            ss = nt(ones, hi) + nt(ones, lo)
            mean = res[64:65] * (1.0 / 128.0)
            var = ss[0:1] * (1.0 / 128.0) - mean * mean
            inv = lax.rsqrt(jnp.maximum(var, 0.0) + eps)
            bias = res[0:16] + res[16:32] + res[32:48]
            bias = inv * (bias - mean * k.gh[...])
            rows = pl.ds(pl.multiple_of(i * 16, 16), 16)
            k.planes[0, rows, :] = bias[:, :128]
            k.planes[1, rows, :] = bias[:, 128:]
            k.hat[rows, :] = (res[48:64] - mean) * (inv * inv)
            k.invb[rows, :] = jnp.broadcast_to(inv, (16, 256))
            k.st[i, 0:1] = inv
            k.st[i, 1:2] = mean * inv
            return carry

        lax.fori_loop(16 * n, 16 * n + 16, body, 0, unroll=8)

    def nc_relay(n):
        src = k.nc.at[zback[n], :, half]
        arrived(src, k.s_ncp.at[n])
        if n < 4:
            send(src, src, k.s_ncp.at[n + 1], z_up)
        send(src, src, k.s_ncc.at[n], core_other)
        if n < 4:
            src = k.nc.at[zof[n], :, half]
            arrived(src, k.s_ncm.at[n])
            if n < 3:
                send(src, src, k.s_ncm.at[n + 1], z_down)
            send(src, src, k.s_ncc.at[8 - n], core_other)

    pair_rows(0)
    pair_rows(1)
    when(c != y, lambda: arrived(k.kv.at[xl, y], k.s_kvp.at[0]))
    kv_row(xl, k.s_yo)
    arrived(k.kv.at[1 - xl, y], k.s_xb.at[0])
    kv_row(1 - xl, k.s_yp)
    pair_rows(2)
    arrived(k.qg.at[c_xh], k.s_qgx.at[0])
    send(k.qg.at[c_xh], k.qg.at[c_xh], k.s_qgc.at[1], core_other)
    pair_rows(3)
    kv_row_relay(xl, k.s_yo)
    pair_rows(4)
    kv_row_relay(1 - xl, k.s_yp)
    pair_rows(5)
    nc_relay(1)
    pair_rows(6)
    pair_rows(7)
    for side, sem in ((xl, k.s_yo), (1 - xl, k.s_yp)):
        arrived(k.kv.at[side, y2, 0], sem.at[2])
        arrived(k.kv.at[side, y2, 1], sem.at[3])
    arrived(k.qg.at[c_core], k.s_qgc.at[0])
    arrived(k.qg.at[2 * (1 - xh) + 1 - co], k.s_qgc.at[1])

    lane = lax.broadcasted_iota(jnp.int32, (128, 128), 1)

    def head_kv(g, m, hh):
        return jnp.concatenate([k.kv[0, g, m, hh], k.kv[1, g, m, hh]], axis=1)

    order = (yof[1], yof[2], yof[3], y)

    def head_at(p):
        g, hh = lax.rem(y + 1 + p // 4, 4), p % 4
        return g, hh, 4 * g + hh

    def forward(p_at, packed):
        g, hh, h = head_at(p_at)
        keys = head_kv(g, 0, hh)
        vals = head_kv(g, 1, hh)
        by_head = pl.ds(h, 128, stride=16)
        bias = jnp.concatenate([k.planes[0, by_head, :], k.planes[1, by_head, :]], axis=1)
        extra = [jnp.broadcast_to(k.rst[n, pl.ds(h, 1), :], (32, 256)) for n in range(4)]
        s = tn(k.qg[g, 0, hh], keys) * SCALE + (bias + jnp.concatenate(extra, axis=0))
        top = jnp.max(s, axis=1, keepdims=True)
        p = jnp.exp(s - top)
        dp = tn(k.qg[g, 1, hh], vals)
        k.pr[p_at] = p
        k.dp[p_at] = dp
        k.ot[g, hh] = nt(vals, p.astype(BF16)).astype(BF16)
        total = jnp.sum(p, axis=1, keepdims=True)
        dots = jnp.sum(p * dp, axis=1, keepdims=True)
        packed = jnp.where(lane == p_at % 8, top, packed)
        packed = jnp.where(lane == 8 + p_at % 8, total, packed)
        return jnp.where(lane == 16 + p_at % 8, dots, packed)

    for b in range(2):
        packed = jnp.zeros((128, 128), F32)
        for p_at in range(8 * b, 8 * b + 8):
            packed = forward(p_at, packed)
        k.stats[b, c] = packed.T[0:24]
        for n, dev, _ in cpeers:
            send(k.stats.at[b, c], k.stats.at[b, c], k.s_st.at[4 * b + n], dev)
    for n, dev, who in cpeers:
        send(k.ot.at[who], k.oin.at[c], k.s_o.at[n], dev)
    k.oin[c] = k.ot[c]

    def combine(b):
        for n, _, who in cpeers:
            arrived(k.stats.at[b, who], k.s_st.at[4 * b + n])
        top = k.stats[b, 0, 0:8]
        for n in range(1, 4):
            top = jnp.maximum(top, k.stats[b, n, 0:8])
        total = jnp.zeros((8, 128), F32)
        dots = jnp.zeros((8, 128), F32)
        weights = []
        for n in range(4):
            w = jnp.exp(k.stats[b, n, 0:8] - top)
            weights.append(w)
            total += w * k.stats[b, n, 8:16]
            dots += w * k.stats[b, n, 16:24]
        inv_total = 1.0 / total
        for n in range(4):
            k.arow[n, 8 * b : 8 * b + 8] = weights[n] * inv_total
        own = k.arow[c, 8 * b : 8 * b + 8]
        k.arow_own[8 * b : 8 * b + 8] = own
        k.acol[b] = jnp.concatenate([own, dots * inv_total, jnp.zeros((112, 128), F32)], axis=0).T

    def backward(p_at, carry):
        g, hh, h = head_at(p_at)
        columns = k.acol[p_at // 8]
        alpha = columns[:, p_at % 8 : p_at % 8 + 1]
        delta = columns[:, 8 + p_at % 8 : 9 + p_at % 8]
        p = k.pr[p_at]
        ds = p * alpha * (k.dp[p_at] - delta)
        by_head = pl.ds(h, 128, stride=16)
        k.bgf[0, by_head, :] = ds[:, :128]
        k.bgf[1, by_head, :] = ds[:, 128:]
        low = ds.astype(BF16)
        k.dqt[g, hh] = (nt(head_kv(g, 0, hh), low) * SCALE).astype(BF16)
        dk = (nn(k.qg[g, 0, hh], low) * SCALE).astype(BF16)
        k.dkv[0, g, 0, hh] = dk[:, :128]
        k.dkv[1, g, 0, hh] = dk[:, 128:]
        ga = (k.qg[g, 1, hh].astype(F32) * k.arow_own[pl.ds(p_at, 1), :]).astype(BF16)
        dv = nn(ga, p.astype(BF16)).astype(BF16)
        k.dkv[0, g, 1, hh] = dv[:, :128]
        k.dkv[1, g, 1, hh] = dv[:, 128:]
        return carry

    def key_value_out(n):
        for p_at in range(4 * n, 4 * n + 4):
            backward(p_at, 0)
        g = order[n]
        send(k.dkv.at[1 - xl, g], k.xin.at[g], k.s_xin.at[n], x_other)
        d = make(
            k.dqt.at[g],
            k.dqin.at[c],
            k.s_dq.at[2 * lax.rem(xh + g // 2, 2) + lax.rem(co + g % 2, 2)],
            {"col_0": g // 2, "col_1": g % 2},
        )
        started.append((c != g, d))
        when(c != g, lambda: d.start())

    def ring_step(n):
        for way, owner, dev in ((0, zof[4 - n], z_up), (1, zback[4 - n], z_down)):
            for part in range(2):
                if n == 0 and part != way:
                    continue
                rows = pl.ds(pl.multiple_of(owner * 256 + 128 * part, 128), 128)
                value = k.bgf[:, rows, :]
                if n > 1 or (n == 1 and part == way):
                    arrived(k.brv.at[way, n - 1, part], k.s_br.at[8 * way + 2 * (n - 1) + part])
                    value = value + k.brv[way, n - 1, part].astype(F32)
                k.bst[way, n, part] = value.astype(BF16)
                send(k.bst.at[way, n, part], k.brv.at[way, n, part], k.s_br.at[8 * way + 2 * n + part], dev)

    def bg_finish():
        for part in range(2):
            rows = pl.ds(pl.multiple_of(z * 256 + 128 * part, 128), 128)
            value = k.bgf[:, rows, :]
            for way in range(2):
                arrived(k.brv.at[way, 3, part], k.s_br.at[8 * way + 6 + part])
                value = value + k.brv[way, 3, part].astype(F32)
            k.bgt[:, 128 * part : 128 * part + 128] = value
            k.bga[z, :, 128 * part : 128 * part + 128] = value.astype(BF16)
        for part in range(2):
            mine_bg = k.bga.at[z, :, pl.ds(128 * part, 128)]
            send(mine_bg, mine_bg, k.s_bg.at[part], z_up)
            send(mine_bg, mine_bg, k.s_bg.at[8 + part], z_down)

    def bg_relay(n):
        for part in range(2):
            half_rows = pl.ds(128 * part, 128)
            for way, owner, dev in ((0, zback[n], z_up), (1, zof[n], z_down)):
                if n == 4 and part != way:
                    continue
                block = k.bga.at[owner, :, half_rows]
                arrived(block, k.s_bg.at[8 * way + 2 * (n - 1) + part])
                if n < 3 or (n == 3 and part == way):
                    send(block, block, k.s_bg.at[8 * way + 2 * n + part], dev)

    combine(0)
    key_value_out(0)
    key_value_out(1)
    combine(1)
    key_value_out(2)
    key_value_out(3)
    k.dqin[c] = k.dqt[c]
    ring_step(0)
    nc_relay(2)

    for n, _, who in cpeers:
        arrived(k.oin.at[who], k.s_o.at[n])
    for hh in range(4):
        att = jnp.zeros((48, 128), F32)
        for n in range(4):
            w = k.arow[n, pl.ds(4 * lax.rem(c + 7 - y, 4) + hh, 1), :]
            att += k.oin[n, hh].astype(F32) * w
        k.att[48 * hh : 48 * hh + 48] = att
    gate = k.gate[...]
    att = k.att[...]
    mixed = (gate * att).astype(BF16)
    grad_gate = (k.gmix[...] * att * gate * (1.0 - gate)).astype(BF16)
    k.gin[576:768] = grad_gate
    for n in range(4):
        k.gsh[0, 4 + n, 0:48] = grad_gate[48 * n : 48 * n + 48]
    for n in range(8):
        for m in range(2):
            at = 32 * n + 16 * m
            k.gsh[m, n, 48:64] = mixed[at : at + 16] if n < 6 else jnp.zeros((16, 128), BF16)
    part_out = tn(mixed, k.wout[...]).astype(BF16)
    for n in range(4):
        k.po[n] = part_out[32 * n : 32 * n + 32]
    for n, dev, who in cpeers:
        send(k.po.at[who], k.por.at[c], k.s_po.at[n], dev)
    k.por[c] = k.po[c]

    def share(b):
        for n in range(1, 8):
            send(k.gsh.at[b, zof[n]], k.zsh.at[b, z], k.s_zi.at[8 * b + n], {"samp": zof[n]})
        k.zsh[b, z] = k.gsh[b, z]

    def weight_rows(b):
        for n in range(1, 8):
            arrived(k.zsh.at[b, zback[n]], k.s_zi.at[8 * b + n])
        acc = nn(k.zsh[b, 0, 0:48], k.nc[0, 0])
        acc_out = nn(k.zsh[b, 0, 48:64], k.nc[0, 1])
        for n in range(1, 8):
            acc += nn(k.zsh[b, n, 0:48], k.nc[n, 0])
            acc_out += nn(k.zsh[b, n, 48:64], k.nc[n, 1])
        for n in range(4):
            tall = (acc[16 * n : 16 * n + 16] if n < 3 else acc_out).astype(BF16)
            k.dws[b, 2 * n] = tall[:, :384]
            k.dws[b, 2 * n + 1] = tall[:, 384:]
        for n, dev, to, _ in rpeers:
            send(k.dws.at[b, to], k.dwr.at[b, row], k.s_dw.at[8 * b + n], dev)
        k.dwr[b, row] = k.dws[b, row]

    def weight_sum(b):
        for n, _, _, came in rpeers:
            arrived(k.dwr.at[b, came], k.s_dw.at[8 * b + n])
        total = k.dwr[b, 0].astype(F32)
        for n in range(1, 8):
            total += k.dwr[b, n].astype(F32)
        k.dwall[b, y, xl, z] = total.astype(BF16)
        for n in range(1, 8):
            here = k.dwall.at[b, y, xl, z]
            send(here, here, k.s_dz.at[8 * b + n], {"samp": zof[n]})

    low_z, high_z = pl.ds(0, 4), pl.ds(4, 4)

    def same_place(ref, sem, dev):
        send(ref, ref, sem, dev)

    def spread_1(b):
        w, ay, by, bx = k.dwall.at[b], 4 * b, 4 * b, 4 * b
        for n in range(1, 8):
            arrived(w.at[y, xl, zback[n]], k.s_dz.at[8 * b + n])
        same_place(w.at[y, xl, low_z], k.s_ax.at[b], x_other)
        same_place(w.at[y, xl, high_z], k.s_by.at[by], y_up)
        same_place(w.at[y, xl, high_z], k.s_by.at[by + 1], y_down)
        same_place(w.at[y, xl, high_z], k.s_bx.at[bx], x_other)

    def spread_2(b):
        w, ay, by, bx = k.dwall.at[b], 4 * b, 4 * b, 4 * b
        arrived(w.at[y, 1 - xl, low_z], k.s_ax.at[b])
        same_place(w.at[y, :, low_z], k.s_ay.at[ay], y_up)
        same_place(w.at[y, :, low_z], k.s_ay.at[ay + 1], y_down)
        arrived(w.at[y3, xl, high_z], k.s_by.at[by])
        same_place(w.at[y3, xl, pl.ds(4, 2)], k.s_by.at[by + 2], y_up)
        same_place(w.at[y3, xl, high_z], k.s_bx.at[bx + 1], x_other)
        arrived(w.at[y1, xl, high_z], k.s_by.at[by + 1])
        same_place(w.at[y1, xl, pl.ds(6, 2)], k.s_by.at[by + 3], y_down)
        same_place(w.at[y1, xl, high_z], k.s_bx.at[bx + 2], x_other)

    def spread_3(b):
        w, ay, by, bx = k.dwall.at[b], 4 * b, 4 * b, 4 * b
        arrived(w.at[y3, :, low_z], k.s_ay.at[ay])
        same_place(w.at[y3, 0, low_z], k.s_ay.at[ay + 2], y_up)
        arrived(w.at[y1, :, low_z], k.s_ay.at[ay + 1])
        same_place(w.at[y1, 1, low_z], k.s_ay.at[ay + 3], y_down)
        arrived(w.at[y2, xl, pl.ds(4, 2)], k.s_by.at[by + 2])
        arrived(w.at[y2, xl, pl.ds(6, 2)], k.s_by.at[by + 3])
        same_place(w.at[y2, xl, high_z], k.s_bx.at[bx + 3], x_other)

    def spread_4(b):
        w, ay, by, bx = k.dwall.at[b], 4 * b, 4 * b, 4 * b
        arrived(w.at[y, 1 - xl, high_z], k.s_bx.at[bx])
        arrived(w.at[y3, 1 - xl, high_z], k.s_bx.at[bx + 1])
        arrived(w.at[y1, 1 - xl, high_z], k.s_bx.at[bx + 2])
        arrived(w.at[y2, 1 - xl, high_z], k.s_bx.at[bx + 3])
        arrived(w.at[y2, 0, low_z], k.s_ay.at[ay + 2])
        arrived(w.at[y2, 1, low_z], k.s_ay.at[ay + 3])

    def plus(dst, piece, a, b):
        dst[piece] = (a.astype(F32) + b.astype(F32)).astype(BF16)

    def first_sum(n):
        g = order[n]
        arrived(k.xin.at[g], k.s_xin.at[n])
        plus(k.sx, g, k.dkv[xl, g], k.xin[g])
        if n < 3:
            send(k.sx.at[g], k.yin.at[y], k.s_yin.at[n + 1], {"row_0": g})

    give_back = make(k.fin, k.dkvown, k.s_fin.at[0], swapped)
    started.append((c != y, give_back))

    def last_sum():
        total = k.sx[y].astype(F32)
        for n in range(1, 4):
            arrived(k.yin.at[yof[4 - n]], k.s_yin.at[n])
            total += k.yin[yof[4 - n]].astype(F32)
        total = total.astype(BF16)
        k.fin[...] = total

        def keep():
            k.dkvown[...] = k.fin[...]

        when(c == y, keep)
        when(c != y, lambda: give_back.start())

    outs = []

    def give_out(src, dst):
        copy = pltpu.make_async_copy(src, dst, k.s_out.at[len(outs)])
        copy.start()
        outs.append(copy)

    def pair_back(owner):
        bg = jnp.concatenate([k.bga[owner, 0], k.bga[owner, 1]], axis=1)
        rows = pl.ds(pl.multiple_of(owner * 256, 256), 256)
        plane = jnp.concatenate([k.planes[0, rows, :], k.planes[1, rows, :]], axis=1)
        product = bg.astype(F32) * plane
        hi = product.astype(BF16)
        lo = (product - hi.astype(F32)).astype(BF16)
        both = nn(k.emat[...], hi) + nn(k.emat[...], lo)
        out = nn(k.amat[0], bg) + nn(k.amat[1], bg)
        k.pg[rows, :] = (k.invb[rows, :] * out - k.hat[rows, :] * both).astype(BF16)
        give_out(k.pg.at[rows], k.o_pg.at[rows])

    def project_pairs(n, carry):
        acc, low = carry
        part = pl.ds(pl.multiple_of(n * 16, 16), 16)
        bg = jnp.concatenate([k.bgt[0, part, :], k.bgt[1, part, :]], axis=1)
        i = 16 * z + n
        scaled = bg * k.st[i, 0:1]
        hi = scaled.astype(BF16)
        rest = (scaled - hi.astype(F32)).astype(BF16)
        acc = acc + nn(jnp.concatenate([hi, rest], axis=0), k.xbuf[i])
        low = low + jnp.sum(bg * k.st[i, 1:2], axis=1, keepdims=True)
        return (acc, low)

    first_sum(0)
    first_sum(1)
    for n, _, who in cpeers:
        arrived(k.dqin.at[who], k.s_dq.at[n])
    for hh in range(4):
        dq = k.dqin[0, hh].astype(F32)
        for n in range(1, 4):
            dq += k.dqin[n, hh].astype(F32)
        k.gin[48 * hh : 48 * hh + 48] = dq.astype(BF16)
        k.gsh[0, hh, 0:48] = dq.astype(BF16)
    share(0)
    ring_step(1)
    first_sum(2)
    first_sum(3)
    nc_relay(3)
    ring_step(2)
    last_sum()
    nc_relay(4)
    for n in range(1, 8):
        arrived(k.nc.at[zback[n], :, pl.ds(64 * (1 - co), 64)], k.s_ncc.at[n])
    weight_rows(0)
    when(c != y, lambda: arrived(k.dkvown, k.s_fin.at[0]))
    for hh in range(4):
        k.gin[192 + 48 * hh : 240 + 48 * hh] = k.dkvown[0, hh]
        k.gin[384 + 48 * hh : 432 + 48 * hh] = k.dkvown[1, hh]
        k.gsh[1, hh, 0:48] = k.dkvown[0, hh]
        k.gsh[1, 4 + hh, 0:48] = k.dkvown[1, hh]
    share(1)
    ring_step(3)
    weight_sum(0)
    part_normed = tn(k.gin[...], k.win[...]).astype(BF16)
    for n in range(4):
        k.gn[n] = part_normed[32 * n : 32 * n + 32]
    for n, dev, who in cpeers:
        send(k.gn.at[who], k.gnr.at[c], k.s_gn.at[n], dev)
    k.gnr[c] = k.gn[c]
    bg_finish()
    weight_rows(1)
    spread_1(0)
    acc, low = lax.fori_loop(
        0, 16, project_pairs, (jnp.zeros((32, 128), F32), jnp.zeros((16, 1), F32)), unroll=2
    )
    k.pj1[...] = k.pgain[...] * (acc[0:16] + acc[16:32] - low)
    for n in range(1, 8):
        send(k.pj1, k.pjz.at[z], k.s_pz.at[n], {"samp": zof[n]})
    k.pjz[z] = k.pj1[...]

    for n, _, who in cpeers:
        arrived(k.por.at[who], k.s_po.at[n])
    mine = pl.ds(pl.multiple_of(32 * c, 32), 32)
    total = k.base[mine]
    for n in range(4):
        total = total + k.por[n].astype(F32)
    k.upd[c] = total.astype(BF16)
    for n, dev, _ in cpeers:
        send(k.upd.at[c], k.upd.at[c], k.s_upd.at[n], dev)
    weight_sum(1)
    bg_relay(1)
    spread_2(0)
    for n, _, who in cpeers:
        arrived(k.gnr.at[who], k.s_gn.at[n])
    total = k.gnr[0].astype(F32)
    for n in range(1, 4):
        total += k.gnr[n].astype(F32)
    scaled = total * wide_row(k.gain)
    hat = k.unit[mine]
    back = k.inv[mine] * (
        scaled
        - jnp.mean(scaled, axis=1, keepdims=True)
        - hat * jnp.mean(scaled * hat, axis=1, keepdims=True)
    )
    k.tok[c] = (k.nc[z, 1, mine].astype(F32) + back).astype(BF16)
    for n, dev, _ in cpeers:
        send(k.tok.at[c], k.tok.at[c], k.s_tok.at[n], dev)

    pair_back(z)
    bg_relay(2)
    spread_1(1)
    for n in range(1, 8):
        arrived(k.pjz.at[zback[n]], k.s_pz.at[n])
    total = k.pjz[0]
    for n in range(1, 8):
        total += k.pjz[n]
    k.pj2[...] = total
    for n, dev, _, _ in rpeers:
        send(k.pj2, k.pjr.at[row], k.s_pr.at[n], dev)
    k.pjr[row] = total
    spread_3(0)
    pair_back(zof[1])
    pair_back(zback[1])
    spread_2(1)
    bg_relay(3)
    for n, _, _, came in rpeers:
        arrived(k.pjr.at[came], k.s_pr.at[n])
    total = k.pjr[0]
    for n in range(1, 8):
        total += k.pjr[n]
    k.pjc[c] = total
    for n, dev, _ in cpeers:
        send(k.pjc.at[c], k.pjc.at[c], k.s_pc.at[n], dev)
    pair_back(zof[2])
    spread_3(1)
    pair_back(zback[2])
    bg_relay(4)
    pair_back(zof[3])
    pair_back(zback[3])
    pair_back(zof[4])
    spread_4(0)
    for n, _, who in cpeers:
        arrived(k.upd.at[who], k.s_upd.at[n])
        arrived(k.tok.at[who], k.s_tok.at[n])
        arrived(k.pjc.at[who], k.s_pc.at[n])
    give_out(k.upd, k.o_upd)
    give_out(k.tok, k.o_tok)
    k.o_proj[...] = k.pjc[0] + k.pjc[1] + k.pjc[2] + k.pjc[3]

    def weight_out(b):
        for half_of in range(2):
            lanes = slice(384 * half_of, 384 * half_of + 384)
            for n in range(8):
                member = ((0, 3), (1, 2))[b][n // 4]
                for m in range(3):
                    at = 192 * member + 48 * (n % 4) + 16 * m
                    k.win_out[at : at + 16, lanes] = k.dwall[b, m, half_of, n]
                if n < 6:
                    at = 32 * n + 16 * b
                    k.wout_out[at : at + 16, lanes] = k.dwall[b, 3, half_of, n]

    weight_out(0)
    for at in (0, 576):
        give_out(k.win_out.at[pl.ds(at, 192)], k.o_in.at[pl.ds(at, 192)])
    spread_4(1)
    weight_out(1)
    give_out(k.win_out.at[pl.ds(192, 384)], k.o_in.at[pl.ds(192, 384)])
    give_out(k.wout_out, k.o_out)
    for copy in outs:
        copy.wait()
    for cond, d in started:
        if cond is None:
            d.wait_send()
        else:
            when(cond, lambda d=d: d.wait_send())


def copy_out(*refs):
    n = len(OUTPUTS)
    src, dst, buf, sems = refs[:n], refs[n : 2 * n], refs[2 * n : 3 * n], refs[3 * n]
    parts = [(m, pl.ds(512 * i, 512)) for m in (2,) for i in range(4)]
    parts += [(3, pl.ds(192 * i, 192)) for i in range(4)] + [(m, pl.ds(0, 4)) for m in (0, 1)]
    parts += [(4, pl.ds(0, 192)), (5, pl.ds(0, 16))]
    total = len(parts)
    come = [
        pltpu.make_async_copy(src[m].at[at], buf[m].at[at], sems.at[i]) for i, (m, at) in enumerate(parts)
    ]
    go = [
        pltpu.make_async_copy(buf[m].at[at], dst[m].at[at], sems.at[total + i])
        for i, (m, at) in enumerate(parts)
    ]
    for d in come:
        d.start()
    for d, e in zip(come, go):
        d.wait()
        e.start()
    for e in go:
        e.wait()


def on_device(
    tokens,
    atom_type,
    noise_step,
    pair_rep,
    bond_blocks,
    chiral_blocks,
    type_table,
    noise_row,
    norm_gain,
    pair_gain,
    in_weight,
    out_weight,
    pair_weight,
    restraint_weight,
    cotangent,
):
    args = dict(
        h_tokens=tokens[0],
        h_cot=cotangent[0],
        h_win=in_weight.reshape(768, 768),
        h_wout=out_weight,
        pair=pair_rep,
        atom=atom_type[None, :],
        step=noise_step[None, :],
        bonds=bond_blocks.T,
        chirs=chiral_blocks.T,
        table=type_table,
        nrow=noise_row.reshape(6, 128),
        gain=norm_gain.reshape(6, 128),
        pgain=pair_gain[None, :],
        pw=pair_weight.T,
        rw=restraint_weight,
    )
    vmem = pl.BlockSpec(memory_space=pltpu.VMEM)
    hbm = pl.BlockSpec(memory_space=pl.ANY)
    shapes = (
        jax.ShapeDtypeStruct((4, 32, 768), BF16),
        jax.ShapeDtypeStruct((4, 32, 768), BF16),
        jax.ShapeDtypeStruct((2048, 256), BF16),
        jax.ShapeDtypeStruct((768, 768), BF16),
        jax.ShapeDtypeStruct((192, 768), BF16),
        jax.ShapeDtypeStruct((16, 128), F32),
    )
    results = pl.pallas_call(
        kernel,
        out_shape=shapes,
        in_specs=[hbm if name.startswith("h_") or name == "pair" else vmem for name in INPUTS],
        out_specs=(hbm,) * 5 + (vmem,),
        scratch_shapes=[pltpu.VMEM(*s) for s in SCRATCH.values()]
        + [pltpu.SemaphoreType.DMA((n,)) for n in SEMS.values()],
        compiler_params=pltpu.CompilerParams(
            collective_id=0, has_side_effects=True, vmem_limit_bytes=60 * 1024 * 1024
        ),
    )(*(args[name] for name in INPUTS))
    upd, tok, pg, ing, outg, proj = pl.pallas_call(
        copy_out,
        out_shape=shapes,
        in_specs=[hbm] * 6,
        out_specs=(hbm,) * 6,
        scratch_shapes=[pltpu.VMEM(s.shape, s.dtype) for s in shapes]
        + [pltpu.SemaphoreType.DMA((24,))],
    )(*results)
    return (
        upd.reshape(1, 128, 768),
        tok.reshape(1, 128, 768),
        jnp.swapaxes(pg.reshape(128, 16, 256), 1, 2),
        ing.reshape(4, 192, 768),
        outg,
        proj.T,
    )


def solution(mesh):
    torus = Mesh(
        mesh.devices.reshape(mesh.shape["samp"], 4, 2, 2, 2),
        ("samp", "row_0", "row_1", "col_0", "col_1"),
    )
    placed = (
        P("samp", ROW, None),
        P(ROW),
        P("samp"),
        P(ROW, COL, None),
        P(),
        P(),
        P(),
        P(),
        P(),
        P(),
        P(None, COL, None),
        P(COL, None),
        P(),
        P(),
        P("samp", ROW, None),
    )
    return jax.shard_map(
        on_device,
        mesh=torus,
        in_specs=placed,
        out_specs=(
            P("samp", ROW, None),
            P("samp", ROW, None),
            P(ROW, COL, "samp"),
            P(None, COL, None),
            P(COL, None),
            P(),
        ),
        check_vma=False,
    )
```
